32 devices in a mesh: dp: 16 (over z, y, x), role: 2 (over core).
Axes of the slice: x: 2, y: 2, z: 4, core: 2. Of those that a mesh axis runs over, the one named last changes fastest.
Arguments:
- frames: bfloat16 [16, 768, 1024], P('dp', 'role'), may hold values from -6 to 6
- frames_cotangent: bfloat16 [16, 768, 1024], P('dp', 'role'), may hold values from -6 to 6
- phoneme_len: int32 [16], P('dp'), may hold values from 1 to 96, as said below
- prompt_len: int32 [16], P('dp'), may hold values from 96 to 288, as said below
- target_segment: int32 [16, 384], P('dp'), may hold values from 0 to 3, never falling along the last dimension, each value on 1 to 192 neighbouring positions
- first_gain: bfloat16 [1024], P(('dp', 'role')), may hold values from 0.5 to 1.5
- first_shift: bfloat16 [1024], P(('dp', 'role')), may hold values from -1.5 to 1.5
- inward_weight: bfloat16 [1024, 3072], P(('dp', 'role')), may hold values from -0.1875 to 0.1875
- query_bias: bfloat16 [1024], P(('dp', 'role')), may hold values from -2.5 to 2.5
- value_bias: bfloat16 [1024], P(('dp', 'role')), may hold values from -0.25 to 0.25
- outward_weight: bfloat16 [1024, 1024], P(('dp', 'role')), may hold values from -2 to 2
- outward_bias: bfloat16 [1024], P(('dp', 'role')), may hold values from -2.5 to 2.5
- second_gain: bfloat16 [1024], P(('dp', 'role')), may hold values from 0.5 to 1.5
- second_shift: bfloat16 [1024], P(('dp', 'role')), may hold values from -1.5 to 1.5
- expand_weight: bfloat16 [1024, 4096], P(('dp', 'role')), may hold values from -0.1875 to 0.1875
- expand_bias: bfloat16 [4096], P(('dp', 'role')), may hold values from -2.5 to 2.5
- reduce_weight: bfloat16 [4096, 1024], P(('dp', 'role')), may hold values from -0.09375 to 0.09375
- reduce_bias: bfloat16 [1024], P(('dp', 'role')), may hold values from -2.5 to 2.5
Outputs:
- result: bfloat16 [16, 768, 1024], P('dp', 'role')
- frames_gradient: bfloat16 [16, 768, 1024], P('dp', 'role')
- first_gain_gradient: float32 [1024], P(('dp', 'role'))
- first_shift_gradient: float32 [1024], P(('dp', 'role'))
- inward_weight_gradient: float32 [1024, 3072], P(('dp', 'role'))
- query_bias_gradient: float32 [1024], P(('dp', 'role'))
- value_bias_gradient: float32 [1024], P(('dp', 'role'))
- outward_weight_gradient: float32 [1024, 1024], P(('dp', 'role'))
- outward_bias_gradient: float32 [1024], P(('dp', 'role'))
- second_gain_gradient: float32 [1024], P(('dp', 'role'))
- second_shift_gradient: float32 [1024], P(('dp', 'role'))
- expand_weight_gradient: float32 [1024, 4096], P(('dp', 'role'))
- expand_bias_gradient: float32 [4096], P(('dp', 'role'))
- reduce_weight_gradient: float32 [4096, 1024], P(('dp', 'role'))
- reduce_bias_gradient: float32 [1024], P(('dp', 'role'))
The draws below stay inside these ranges and needn't reach their ends.
Inputs may be any that keep to these rules, and one draw needn't show every extreme that they name: In some group phoneme_len + prompt_len equals 384; in some group phoneme_len is 1. phoneme_len + prompt_len never exceeds 384. `target_segment`: each group's target rows hold 4 utterances in order, each of at most 192 rows.
All inputs are finite; a program needn't handle non-finite values.
Results may differ from the reference program's by a relative error of at most 0.014.
Values may be sent and summed in bfloat16 or wider, within the bound.
A program may use at most 256 MiB of HBM per device.

```python
import math
import jax
import jax.numpy as jnp
import numpy as np
from jax import lax

D = 1024
H = 16
HD = 64
FF = 4096
ROWS = 384
UTT = 4
GROUPS = 16


def lengths_pair(key):
    base = jax.random.fold_in(key, 11)
    first_key, second_key, third_key = jax.random.split(base, 3)
    phonemes = jax.random.randint(first_key, (GROUPS,), 1, ROWS // 4 + 1)
    prompts = jax.random.randint(second_key, (GROUPS,), ROWS // 4, 3 * ROWS // 4 + 1)
    order = jax.random.permutation(third_key, GROUPS)
    phonemes = phonemes.at[order[0]].set(ROWS // 4).at[order[1]].set(1)
    prompts = prompts.at[order[0]].set(3 * ROWS // 4).at[order[1]].set(ROWS // 4)
    return (phonemes.astype(jnp.int32), prompts.astype(jnp.int32))


def draw_phoneme_len(key, part):
    return lengths_pair(key)[0]


def draw_prompt_len(key, part):
    return lengths_pair(key)[1]


def shard_levels(rng, dims, pieces, smallest, top_value):
    def one(position, blocks):
        heights = jax.random.uniform(jax.random.fold_in(jax.random.fold_in(rng, 6), position), (blocks,), jnp.float32, smallest / len(pieces), top_value / len(pieces))
        return jnp.repeat(jnp.exp(heights), dims[position] // blocks).reshape((-1,) + (1,) * (len(dims) - position - 1))

    level = one(*pieces[0])
    for cut in pieces[1:]:
        level = level * one(*cut)
    return level


def profile(count, total, reach, lean):
    portions = [(1 << 20) // math.isqrt(rank ** lean) + 1 for rank in range(2, count + 1)]
    surplus, holding = total - reach - (count - 1), [1] * (count - 1)
    while surplus > 0:
        movable = [i for i in range(count - 1) if holding[i] < reach]
        whole, remaining = sum([portions[i] for i in movable]), surplus
        for i in movable:
            more = min(reach - holding[i], max(1, remaining * portions[i] // whole), surplus)
            holding[i] = holding[i] + more
            surplus = surplus - more
    return np.array([reach] + holding)


def ragged(stream_key, number_of, total, reach, skew):
    if number_of == 2:
        one = jax.random.randint(stream_key, (), max(1, total - reach), min(reach, total - 1) + 1)
        return jnp.stack([one, total - one])
    sizes = jnp.asarray(profile(number_of, total, reach, skew), jnp.int32)
    pairs = (number_of - 1) // 2
    source_of, taker = sizes[1:1 + 2 * pairs:2], sizes[2:2 + 2 * pairs:2]
    margin = jnp.minimum(source_of - 1, reach - taker)
    moved = jax.random.randint(jax.random.fold_in(stream_key, 1), (pairs,), 0, 1 << 20) % (margin + 1)
    sizes = sizes.at[1:1 + 2 * pairs:2].set(source_of - moved).at[2:2 + 2 * pairs:2].set(taker + moved)
    return sizes[jax.random.permutation(jax.random.fold_in(stream_key, 2), number_of)]


def normal_values(own_key, shape, width, bound, cuts=(), dtype=jnp.bfloat16):
    loudness = shard_levels(own_key, shape, cuts, -0.22, 0.18) if cuts else 1.0
    array = jax.random.normal(own_key, shape, jnp.float32) * width * loudness
    return jnp.minimum(jnp.maximum(array, -bound), bound).astype(dtype)


def setup_inputs(seed: int = 0) -> dict:
    seeds = jax.random.split(jax.random.key(seed), 19)
    frames = normal_values(seeds[0], (GROUPS, 2 * ROWS, D), 1.0, 6.0, ((0, 16), (1, 2)))
    frames_cotangent = normal_values(seeds[1], (GROUPS, 2 * ROWS, D), 1.0, 6.0, ((0, 16), (1, 2)))
    phoneme_len = draw_phoneme_len(jax.random.fold_in(seeds[18], 71), 0)
    prompt_len = draw_prompt_len(jax.random.fold_in(seeds[18], 71), 0)
    target_segment = jax.vmap(lambda own: jnp.searchsorted(jnp.cumsum(ragged(own, UTT, ROWS, ROWS // 2, 2)), jnp.arange(ROWS), side="right"))(jax.random.split(seeds[4], GROUPS)).reshape((GROUPS, ROWS)).astype(jnp.int32)
    first_gain = jnp.clip(0.5 + 1.0 * jax.random.uniform(seeds[5], (D,), jnp.float32) ** shard_levels(seeds[5], (D,), ((0, 32),), -0.2, 0.2), 0.5, 1.5).astype(jnp.bfloat16)
    first_shift = normal_values(seeds[6], (D,), 0.3, 1.5, ((0, 32),))
    inward_weight = normal_values(seeds[7], (D, 3 * D), D ** -0.5, 0.1875, ((0, 32),))
    query_bias = normal_values(seeds[8], (D,), 0.5, 2.5, ((0, 32),))
    value_bias = normal_values(seeds[9], (D,), 0.05, 0.25, ((0, 32),))
    outward_weight = normal_values(seeds[10], (D, D), 8 ** -0.5, 2.0, ((0, 32),))
    outward_bias = normal_values(seeds[11], (D,), 0.5, 2.5, ((0, 32),))
    second_gain = jnp.clip(0.5 + 1.0 * jax.random.uniform(seeds[12], (D,), jnp.float32) ** shard_levels(seeds[12], (D,), ((0, 32),), -0.2, 0.2), 0.5, 1.5).astype(jnp.bfloat16)
    second_shift = normal_values(seeds[13], (D,), 0.3, 1.5, ((0, 32),))
    expand_weight = normal_values(seeds[14], (D, FF), D ** -0.5, 0.1875, ((0, 32),))
    expand_bias = normal_values(seeds[15], (FF,), 0.5, 2.5, ((0, 32),))
    reduce_weight = normal_values(seeds[16], (FF, D), FF ** -0.5, 0.09375, ((0, 32),))
    reduce_bias = normal_values(seeds[17], (D,), 0.5, 2.5, ((0, 32),))
    return {"frames": frames, "frames_cotangent": frames_cotangent, "phoneme_len": phoneme_len, "prompt_len": prompt_len, "target_segment": target_segment, "first_gain": first_gain, "first_shift": first_shift, "inward_weight": inward_weight, "query_bias": query_bias, "value_bias": value_bias, "outward_weight": outward_weight, "outward_bias": outward_bias, "second_gain": second_gain, "second_shift": second_shift, "expand_weight": expand_weight, "expand_bias": expand_bias, "reduce_weight": reduce_weight, "reduce_bias": reduce_bias}


@jax.custom_vjp
def low(v):
    return lax.optimization_barrier(v.astype(jnp.bfloat16)).astype(jnp.float32)

@jax.custom_vjp
def low_back(v):
    return v

def low_keep(v):
    return (low(v), None)

def low_pass(kept, grad):
    return (grad,)

def back_keep(v):
    return (v, None)

def back_low(kept, grad):
    return (low(grad),)
low.defvjp(low_keep, low_pass)
low_back.defvjp(back_keep, back_low)
EPS = 1e-05
MASKED = -1e+30
HIGH = lax.Precision.HIGHEST

def normalize(values, gain, shift):
    mean_value = lax.optimization_barrier(jnp.mean(values, axis=-1, keepdims=True))
    centered = values - mean_value
    spread = lax.optimization_barrier(jnp.mean(centered * centered, axis=-1, keepdims=True))
    return centered * lax.rsqrt(spread + EPS) * gain + shift

def allowed_mask(prefix_length, segment):
    positions = jnp.arange(2 * ROWS)
    row_index = positions[:, None]
    col_index = positions[None, :]
    key_segment = jnp.concatenate([jnp.full((ROWS,), -1, jnp.int32), segment.astype(jnp.int32)])
    prefix_cols = col_index < prefix_length
    prompt_rows = (row_index < ROWS) & (col_index <= row_index) & prefix_cols
    same_utterance = (col_index >= ROWS) & (col_index <= row_index) & (key_segment[None, :] == key_segment[:, None])
    target_rows = (row_index >= ROWS) & (prefix_cols | same_utterance)
    return prompt_rows | target_rows

def block(params, frames, allowed):
    first_gain, first_shift, inward_weight, query_bias, value_bias, outward_weight, outward_bias, second_gain, second_shift, expand_weight, expand_bias, reduce_weight, reduce_bias = params
    length = frames.shape[0]
    normed = low(normalize(frames, first_gain, first_shift))
    mixed = jnp.dot(normed, inward_weight, precision=HIGH)
    queries = low_back(low(mixed[:, :D] + query_bias))
    keys = low_back(low(mixed[:, D:2 * D]))
    values = low_back(low(mixed[:, 2 * D:] + value_bias))
    head_queries = queries.reshape(length, H, HD).transpose(1, 0, 2)
    head_keys = keys.reshape(length, H, HD).transpose(1, 0, 2)
    head_values = values.reshape(length, H, HD).transpose(1, 0, 2)
    scores = low_back(jnp.einsum('hqd,hkd->hqk', head_queries, head_keys, precision=HIGH) * HD ** (-0.5))
    masked = jnp.where(allowed[None], scores, MASKED)
    peak = lax.optimization_barrier(jnp.max(masked, axis=-1, keepdims=True))
    expo = jnp.exp(masked - peak)
    probs = low(expo / lax.optimization_barrier(jnp.sum(expo, axis=-1, keepdims=True)))
    heads = jnp.einsum('hqk,hkd->hqd', probs, head_values, precision=HIGH)
    attended = low_back(low(heads.transpose(1, 0, 2).reshape(length, D)))
    branch = low_back(jnp.dot(attended, outward_weight, precision=HIGH) + outward_bias)
    middle = frames + branch
    normed_second = low(normalize(middle, second_gain, second_shift))
    inner = low_back(jnp.dot(normed_second, expand_weight, precision=HIGH) + expand_bias)
    active = low(jax.nn.gelu(inner, approximate=False))
    return middle + jnp.dot(active, reduce_weight, precision=HIGH) + reduce_bias

def reference(frames, frames_cotangent, phoneme_len, prompt_len, target_segment, first_gain, first_shift, inward_weight, query_bias, value_bias, outward_weight, outward_bias, second_gain, second_shift, expand_weight, expand_bias, reduce_weight, reduce_bias):
    params = tuple((item.astype(jnp.float32) for item in (first_gain, first_shift, inward_weight, query_bias, value_bias, outward_weight, outward_bias, second_gain, second_shift, expand_weight, expand_bias, reduce_weight, reduce_bias)))

    def one_group(totals, inputs):
        group_frames, group_cotangent, prefix_length, segment = inputs
        allowed = allowed_mask(prefix_length, segment)

        def run(weights, values):
            return block(weights, values, allowed)
        output, pull = jax.vjp(run, params, group_frames.astype(jnp.float32))
        weight_grads, frame_grad = pull(group_cotangent.astype(jnp.float32))
        totals = jax.tree.map(lambda left, right: left + right, totals, weight_grads)
        return (totals, (output.astype(jnp.bfloat16), frame_grad.astype(jnp.bfloat16)))
    zeros = jax.tree.map(jnp.zeros_like, params)
    prefix_lengths = (phoneme_len + prompt_len).astype(jnp.int32)
    totals, (outputs, frame_grads) = lax.scan(one_group, zeros, (frames, frames_cotangent, prefix_lengths, target_segment))
    return (outputs, frame_grads, totals[0], totals[1], totals[2], totals[3], totals[4], totals[5], totals[6], totals[7], totals[8], totals[9], totals[10], totals[11], totals[12])
```

```python
import functools

import jax
import jax.numpy as jnp
from jax import lax
from jax.experimental import pallas as pl
from jax.experimental.pallas import tpu as pltpu
from jax.sharding import PartitionSpec as P

D = 1024
H = 16
HD = 64
EPS = 1e-05
MASKED = -1e30
LOG2E = 1.4426950408889634
BF = jnp.bfloat16
F32 = jnp.float32
MESH = pl.DeviceIdType.MESH


def dot(left, right):
    return lax.dot_general(left, right, (((1,), (0,)), ((), ())), preferred_element_type=F32)


def dot_nt(left, right):
    return lax.dot_general(left, right, (((1,), (1,)), ((), ())), preferred_element_type=F32)


def flip(value):
    return value.astype(F32).T.astype(value.dtype)


def centre(values):
    mean_value = jnp.mean(values, axis=-1, keepdims=True)
    centered = values - mean_value
    spread = jnp.mean(centered * centered, axis=-1, keepdims=True)
    return centered * lax.rsqrt(spread + EPS), lax.rsqrt(spread + EPS)


def norm_back(unit, rate, gain, upstream):
    pulled = upstream * gain
    first = jnp.mean(pulled, axis=-1, keepdims=True)
    second = jnp.mean(pulled * unit, axis=-1, keepdims=True)
    return rate * (pulled - first - unit * second)


SLOTS = 3


def scratch_list():
    dma = pltpu.SemaphoreType.DMA
    v = pltpu.VMEM
    return dict(
        small=v((4, 2, 2, 2, 16, 128), BF),
        vec=v((8, 1024), F32),
        ebias=v((4, 8, 512), F32),
        frames_all=v((2, 384, 1024), BF),
        c_all=v((2, 384, 1024), BF),
        n_all=v((2, 384, 1024), BF),
        n1t=v((1024, 768), BF),
        n2t=v((1024, 768), BF),
        win=v((3, 4, 2, 2, 64, 512), BF),
        wout=v((4, 2, 2, 2, 32, 1024), BF),
        wexp=v((4, 4, 2, 2, 64, 512), BF),
        wred=v((4, 2, 2, 128, 1024), BF),
        stage=v((2, 32, 2048), BF),
        qkv=v((3, 4, 768, 128), BF),
        mask=v((768, 768), BF),
        lse=v((4, 6, 8, 256), F32),
        half=v((2, 384, 512), BF),
        half_t=v((2, 512, 384), BF),
        wide=v((384, 1024), BF),
        att_t=v((1024, 384), BF),
        middle=v((384, 1024), F32),
        out_acc=v((2, 384, 1024), F32),
        bn_acc=v((2, 384, 1024), F32),
        cross=v((2, 384, 1024), F32),
        ffb=v((3, 768, 512), BF),
        act_t=v((512, 768), BF),
        ba_all=v((2, 384, 512), BF),
        dkv=v((2, 768, 128), F32),
        gvec=v((8, 1024), F32),
        gexp=v((4, 8, 512), F32),
        outx=v((4, 2, 2, 32, 1024), BF),
        rb=v((SLOTS, 2, 4, 64, 512), BF),
        ra=v((SLOTS, 4, 64, 512), BF),
        rz=v((7, 3, 64, 512), BF),
        rb_red=v((SLOTS, 2, 128, 1024), BF),
        ra_red=v((SLOTS, 128, 1024), BF),
        rz_red=v((3, 128, 1024), BF),
        rb_out=v((2, 4, 32, 1024), BF),
        ra_out=v((4, 32, 1024), BF),
        rz_out=v((3, 32, 1024), BF),
        sg=v((4, 2, 2, 16, 128), F32),
        rb_sg=v((2, 4, 16, 128), F32),
        ra_sg=v((4, 16, 128), F32),
        rz_sg=v((3, 16, 128), F32),
        fin=v((7, 64, 512), F32),
        fin_in=v((7, 32, 512), F32),
        sfin=v((16, 128), F32),
        sfin_in=v((16, 128), F32),
        own_s=dma((2,)),
        pre_s=dma((10,)),
        pre_r=dma((10,)),
        agz_s=dma((13, 3)),
        agz_r=dma((13, 3)),
        aga_s=dma((13,)),
        aga_r=dma((13,)),
        agb_s=dma((13, 2)),
        agb_r=dma((13, 2)),
        core_s=dma((9,)),
        core_r=dma((9,)),
        rsb_s=dma((13, 2)),
        rsb_r=dma((13, 2)),
        rsa_s=dma((13,)),
        rsa_r=dma((13,)),
        rsz_s=dma((13, 3)),
        rsz_r=dma((13, 3)),
        fin_s=dma((8,)),
        fin_r=dma((8,)),
    )


class Bag:
    def __init__(self, **kw):
        self.__dict__.update(kw)


N_IN = 10
N_OUT = 7


def layer_kernel(names, *refs):
    (phon_ref, prom_ref, seg_ref, frames_ref, cot_ref, small_in, win_in, wout_in, wexp_in, wred_in) = refs[:N_IN]
    (result_ref, fgrad_ref, dwin_ref, dwout_ref, dwexp_ref, dwred_ref, dsmall_ref) = refs[N_IN : N_IN + N_OUT]
    s = Bag(**dict(zip(names, refs[N_IN + N_OUT :])))

    dp = lax.axis_index("dp")
    r = lax.axis_index("role")
    o = 1 - r
    z, y, x = dp // 4, (dp // 2) % 2, dp % 2
    ya, xa = y + r * (1 - 2 * y), x + (1 - r) * (1 - 2 * x)
    yb, xb = y + (1 - r) * (1 - 2 * y), x + r * (1 - 2 * x)
    yc, xc = 1 - y, 1 - x
    core_dev = (dp, o)
    a_dev = (z * 4 + ya * 2 + xa, r)
    b_dev = (z * 4 + yb * 2 + xb, r)
    z_dev = [(((z + k) % 4) * 4 + y * 2 + x, r) for k in (1, 2, 3)]
    z_at = [(z + k) % 4 for k in (1, 2, 3)]
    z_from = [(z + 4 - k) % 4 for k in (1, 2, 3)]

    def copy(src, dst, ss, rs, dev):
        return pltpu.make_async_remote_copy(
            src_ref=src, dst_ref=dst, send_sem=ss, recv_sem=rs, device_id=dev, device_id_type=MESH
        )

    barrier = pltpu.get_barrier_semaphore()
    for dev in z_dev + [a_dev, b_dev, core_dev]:
        pl.semaphore_signal(barrier, inc=1, device_id=dev, device_id_type=MESH)
    pl.semaphore_wait(barrier, 6)

    my_rows = pl.ds(pl.multiple_of(r * 32, 32), 32)
    o_rows = pl.ds(pl.multiple_of(o * 32, 32), 32)

    def half_cols(section, who):
        return pl.ds(pl.multiple_of(section * 1024 + who * 512, 512), 512)

    for block in range(16):
        for who in range(2):
            s.stage[who, :, block * 128 : (block + 1) * 128] = wexp_in[
                :, (2 * block + who) * 128 : (2 * block + who + 1) * 128
            ]
    pre = []
    pre.append(copy(small_in, s.small.at[z, y, x, r], s.pre_s.at[0], s.pre_r.at[0], core_dev))
    for i in range(3):
        pre.append(
            copy(
                win_in.at[:, half_cols(i, o)],
                s.win.at[i, z, y, x, my_rows],
                s.pre_s.at[1 + i],
                s.pre_r.at[1 + i],
                core_dev,
            )
        )
    pre.append(copy(frames_ref, s.frames_all.at[r], s.pre_s.at[4], s.pre_r.at[4], core_dev))
    for j in range(4):
        pre.append(
            copy(
                s.stage.at[o, :, pl.ds(j * 512, 512)],
                s.wexp.at[j, z, y, x, my_rows],
                s.pre_s.at[5 + j],
                s.pre_r.at[5 + j],
                core_dev,
            )
        )
    pre.append(copy(cot_ref, s.c_all.at[r], s.pre_s.at[9], s.pre_r.at[9], core_dev))
    for item in pre:
        item.start()
    own_frames = pltpu.make_async_copy(frames_ref, s.frames_all.at[r], s.own_s.at[0])
    own_cot = pltpu.make_async_copy(cot_ref, s.c_all.at[r], s.own_s.at[1])
    own_frames.start()
    own_cot.start()
    s.small[z, y, x, r] = small_in[...]
    for i in range(3):
        s.win[i, z, y, x, my_rows] = win_in[:, half_cols(i, r)]
    s.wout[z, y, x, r] = wout_in[...]
    s.wred[z, y, x] = wred_in[...]
    for j in range(4):
        s.wexp[j, z, y, x, my_rows] = s.stage[r, :, j * 512 : (j + 1) * 512]

    def ag_small():
        return Bag(t=0, piece=lambda a, b, c: s.small.at[a, b, c], col=lambda b, c: s.small.at[:, b, c], plane=None)

    def ag_in(i):
        return Bag(
            t=1 + i, piece=lambda a, b, c: s.win.at[i, a, b, c], col=lambda b, c: s.win.at[i, :, b, c], plane=None
        )

    def ag_out():
        return Bag(
            t=4, piece=lambda a, b, c: s.wout.at[a, b, c, r], col=lambda b, c: s.wout.at[:, b, c, r], plane=None
        )

    def ag_exp(j):
        return Bag(
            t=5 + 2 * j,
            piece=lambda a, b, c: s.wexp.at[j, a, b, c],
            col=lambda b, c: s.wexp.at[j, :, b, c],
            plane=None,
        )

    def ag_red(j):
        return Bag(
            t=6 + 2 * j, piece=lambda a, b, c: s.wred.at[j, b, c], col=lambda b, c: s.wred.at[j, b, c], plane=j
        )

    def z_copies(it):
        return [
            copy(it.piece(z, y, x), it.piece(z, y, x), s.agz_s.at[it.t, k], s.agz_r.at[it.t, k], z_dev[k])
            for k in range(3)
        ]

    def a_copy(it, yy, xx):
        return copy(it.col(yy, xx), it.col(yy, xx), s.aga_s.at[it.t], s.aga_r.at[it.t], a_dev)

    def b_copy(it, which, yy, xx):
        return copy(it.col(yy, xx), it.col(yy, xx), s.agb_s.at[it.t, which], s.agb_r.at[it.t, which], b_dev)

    def e0(it):
        def go():
            for c in z_copies(it):
                c.start()

        if it.plane is None:
            go()
        else:
            pl.when(z == it.plane)(go)

    def e1(it):
        if it.plane is None:
            for k in range(3):
                p = it.piece(z_from[k], y, x)
                copy(p, p, s.agz_s.at[it.t, k], s.agz_r.at[it.t, k], z_dev[k]).wait_recv()
        else:

            @pl.when(z != it.plane)
            def _():
                k = (z + 4 - it.plane) % 4 - 1
                p = it.piece(z, y, x)
                copy(p, p, s.agz_s.at[it.t, k], s.agz_r.at[it.t, k], z_dev[0]).wait_recv()

        a_copy(it, y, x).start()
        b_copy(it, 0, y, x).start()

    def e2(it):
        a_copy(it, ya, xa).wait_recv()
        b_copy(it, 1, ya, xa).start()

    def e3(it):
        b_copy(it, 0, yb, xb).wait_recv()
        b_copy(it, 1, yc, xc).wait_recv()

    def sent(it):
        def go():
            for c in z_copies(it):
                c.wait_send()

        if it.plane is None:
            go()
        else:
            pl.when(z == it.plane)(go)
        a_copy(it, y, x).wait_send()
        b_copy(it, 0, y, x).wait_send()
        b_copy(it, 1, ya, xa).wait_send()

    i_small, i_q, i_k, i_v, i_out = ag_small(), ag_in(0), ag_in(1), ag_in(2), ag_out()

    def pre_in(index, dst):
        copy(dst, dst, s.pre_s.at[index], s.pre_r.at[index], core_dev).wait_recv()

    pre_in(0, s.small.at[z, y, x, o])
    e0(i_small)
    pre_in(1, s.win.at[0, z, y, x, o_rows])
    e0(i_q)
    e1(i_small)
    pre_in(2, s.win.at[1, z, y, x, o_rows])
    e0(i_k)

    own_frames.wait()
    own_cot.wait()
    prefix = phon_ref[0] + prom_ref[0]
    seg_row = seg_ref[...].astype(F32)
    seg_wide = jnp.broadcast_to(seg_row, (384, 384))
    seg_tall = seg_wide.T
    key_at = lax.broadcasted_iota(jnp.int32, (384, 384), 0)
    row_at = lax.broadcasted_iota(jnp.int32, (384, 384), 1)
    causal = key_at <= row_at
    seen = key_at < prefix

    def as_bias(allowed):
        return jnp.where(allowed, 0.0, MASKED).astype(BF)

    s.mask[0:384, 0:384] = as_bias(causal & seen)
    s.mask[0:384, 384:768] = as_bias(seen)
    s.mask[384:768, 384:768] = as_bias(causal & (seg_wide == seg_tall))

    e1(i_q)
    e2(i_small)
    pre_in(3, s.win.at[2, z, y, x, o_rows])
    e0(i_v)
    e1(i_k)
    e2(i_q)
    e3(i_small)

    def tile_sum(q):
        total = jnp.zeros((16, 128), F32)
        for xx in range(2):
            for who in range(2):
                total = total + s.small[q // 2, q % 2, xx, who].astype(F32)
        return total

    for q in range(8):
        s.vec[:, q * 128 : (q + 1) * 128] = tile_sum(q)[0:8]
    for j in range(4):
        for yy in range(2):
            for xx in range(2):
                at = (yy * 2 + xx) * 128
                s.ebias[j, 0:1, at : at + 128] = s.small[j, yy, xx, r].astype(F32)[8:9]

    def vec_row(i):
        return s.vec[i : i + 1, :]

    pre_in(4, s.frames_all.at[o])

    def norm_tile(i, carry):
        who, rows = i // 3, pl.ds(pl.multiple_of((i % 3) * 128, 128), 128)
        unit, _ = centre(s.frames_all[who, rows].astype(F32))
        normed = unit * vec_row(0) + vec_row(1)
        s.n_all[who, rows] = normed.astype(BF)
        s.n1t[:, pl.ds(pl.multiple_of(i * 128, 128), 128)] = normed.T.astype(BF)
        return carry

    lax.fori_loop(0, 6, norm_tile, 0)

    def project(i):
        def body(n, carry):
            cols = pl.ds(pl.multiple_of(n * 256, 256), 256)
            weight = s.win[i, :, :, :, :, cols].reshape(1024, 256)
            left = s.n_all[...].reshape(768, 1024)
            mixed = dot(left, weight)
            if i != 1:
                bias_at = pl.ds(pl.multiple_of(r * 512 + n * 256, 256), 256)
                bias_row = 2 if i == 0 else 3
                mixed = mixed + s.vec[bias_row : bias_row + 1, bias_at]
            mixed = mixed.astype(BF)
            s.qkv[i, 2 * n] = mixed[:, 0:128]
            s.qkv[i, 2 * n + 1] = mixed[:, 128:256]
            return carry

        lax.fori_loop(0, 2, body, 0)

    e0(i_out)
    e1(i_v)
    e2(i_k)
    e3(i_q)
    project(0)
    for j in range(4):
        pre_in(5 + j, s.wexp.at[j, z, y, x, o_rows])
    e0(ag_exp(0))
    e1(i_out)
    e2(i_v)
    e3(i_k)
    project(1)
    e0(ag_red(0))
    e1(ag_exp(0))
    e2(i_out)
    e3(i_v)
    project(2)

    factor = HD**-0.5 * LOG2E
    low_lane = lax.broadcasted_iota(jnp.int32, (128, 128), 1) < 64

    def pair_rows(block):
        zero = jnp.zeros_like(block)
        return jnp.concatenate([jnp.where(low_lane, block, zero), jnp.where(low_lane, zero, block)], axis=0)

    def pair_mask(keys, rb):
        bias = s.mask[0:keys, rb * 128 : (rb + 1) * 128].astype(F32)
        return jnp.concatenate([bias, bias], axis=1)

    def key_count(rb):
        return (rb + 1) * 128 if rb < 3 else 384 + (rb - 2) * 128

    def attend(hp, carry):
        v_t = flip(s.qkv[2, hp])
        dims = pl.ds(pl.multiple_of(hp * 128, 128), 128)
        for rb in range(6):
            keys = key_count(rb)
            both = pair_rows(s.qkv[0, hp, rb * 128 : (rb + 1) * 128])
            scores = dot_nt(s.qkv[1, hp, 0:keys], both) * factor + pair_mask(keys, rb)
            peak = jnp.max(scores, axis=0, keepdims=True)
            expo = jnp.exp2(scores - peak)
            total = jnp.sum(expo, axis=0, keepdims=True)
            heads = dot(v_t[:, 0:keys], expo.astype(BF)) / total
            s.lse[hp, rb] = jnp.broadcast_to(peak + jnp.log2(total), (8, 256))
            out = jnp.concatenate([heads[0:64, 0:128], heads[64:128, 128:256]], axis=0)
            at = (rb % 3) * 128
            s.half_t[rb // 3, dims, at : at + 128] = out.astype(BF)
            s.half[rb // 3, at : at + 128, dims] = out.T.astype(BF)
        return carry

    lax.fori_loop(0, 4, attend, 0)

    my_half = pl.ds(pl.multiple_of(r * 512, 512), 512)
    o_half = pl.ds(pl.multiple_of(o * 512, 512), 512)

    def core_copy(index, src, dst):
        return copy(src, dst, s.core_s.at[index], s.core_r.at[index], core_dev)

    core_copy(0, s.half.at[o], s.wide.at[:, my_half]).start()
    core_copy(1, s.half_t.at[o], s.att_t.at[my_half]).start()
    s.wide[:, my_half] = s.half[r]
    s.att_t[my_half] = s.half_t[r]
    e0(ag_exp(1))
    e1(ag_red(0))
    e2(ag_exp(0))
    e3(i_out)
    out_swap = core_copy(2, s.wout.at[:, :, :, r], s.wout.at[:, :, :, r])
    out_swap.start()
    core_copy(0, s.wide.at[:, o_half], s.wide.at[:, o_half]).wait_recv()
    core_copy(1, s.att_t.at[o_half], s.att_t.at[o_half]).wait_recv()
    core_copy(2, s.wout.at[:, :, :, o], s.wout.at[:, :, :, o]).wait_recv()

    def out_tile(n, carry):
        cols = pl.ds(pl.multiple_of(n * 256, 256), 256)
        branch = dot(s.wide[...], s.wout[:, :, :, :, :, cols].reshape(1024, 256))
        s.middle[:, cols] = s.frames_all[r, :, cols].astype(F32) + branch + s.vec[4:5, cols]
        return carry

    lax.fori_loop(0, 4, out_tile, 0)

    def norm_two(i, carry):
        rows = pl.ds(pl.multiple_of(i * 128, 128), 128)
        unit, _ = centre(s.middle[rows])
        s.n_all[r, rows] = (unit * vec_row(5) + vec_row(6)).astype(BF)
        return carry

    lax.fori_loop(0, 3, norm_two, 0)
    core_copy(3, s.n_all.at[r], s.n_all.at[r]).start()
    pre_in(9, s.c_all.at[o])
    s.out_acc[...] = jnp.zeros_like(s.out_acc)
    s.bn_acc[...] = jnp.zeros_like(s.bn_acc)
    core_copy(3, s.n_all.at[o], s.n_all.at[o]).wait_recv()

    def flip_two(i, carry):
        who, rows = i // 3, pl.ds(pl.multiple_of((i % 3) * 128, 128), 128)
        s.n2t[:, pl.ds(pl.multiple_of(i * 128, 128), 128)] = flip(s.n_all[who, rows])
        return carry

    lax.fori_loop(0, 6, flip_two, 0)

    def feed(j, carry):
        more = j < 3

        @pl.when(more)
        def _():
            e0(ag_red(j + 1))
            e1(ag_exp(j + 1))

        e2(ag_red(j))
        e3(ag_exp(j))

        @pl.when(j < 2)
        def _():
            e0(ag_exp(j + 2))

        @pl.when(more)
        def _():
            e1(ag_red(j + 1))
            e2(ag_exp(j + 1))

        e3(ag_red(j))
        sent(ag_exp(j))
        sent(ag_red(j))

        def hidden(n, inside):
            cols = pl.ds(pl.multiple_of(n * 256, 256), 256)
            left = s.n_all[...].reshape(768, 1024)
            inner = dot(left, s.wexp[j, :, :, :, :, cols].reshape(1024, 256)) + s.ebias[j, 0:1, cols]
            phi = 0.5 + 0.5 * lax.erf(inner * (2.0**-0.5))
            active = inner * phi
            s.ffb[0, :, cols] = active.astype(BF)
            s.act_t[cols] = active.T.astype(BF)
            slope = phi + inner * (jnp.exp(-0.5 * inner * inner) * 0.3989422804014327)
            up = s.c_all[...].reshape(768, 1024)
            back = (dot_nt(up, s.wred[j, n].reshape(256, 1024)) * slope).astype(BF)
            s.ffb[1, :, cols] = back
            s.gexp[j, 0:1, cols] = jnp.sum(back.astype(F32), axis=0, keepdims=True)
            return inside

        lax.fori_loop(0, 2, hidden, 0)

        def wide_tile(n, inside):
            cols = pl.ds(pl.multiple_of(n * 256, 256), 256)
            part = dot(s.ffb[0], s.wred[j, :, :, :, cols].reshape(512, 256))
            s.out_acc[:, :, cols] += part.reshape(2, 384, 256)
            back = dot_nt(s.ffb[1], s.wexp[j, n].reshape(256, 512))
            s.bn_acc[:, :, cols] += back.reshape(2, 384, 256)
            return inside

        lax.fori_loop(0, 4, wide_tile, 0)

        def grad_red(n, inside):
            cols = pl.ds(pl.multiple_of(n * 256, 256), 256)
            up = s.c_all[:, :, cols].reshape(768, 256)
            s.wred[j, :, :, :, cols] = dot(s.act_t[...], up).astype(BF).reshape(2, 2, 128, 256)
            return inside

        lax.fori_loop(0, 4, grad_red, 0)

        def grad_exp(n, inside):
            cols = pl.ds(pl.multiple_of(n * 256, 256), 256)
            grad = dot(s.n2t[...], s.ffb[1, :, cols]).astype(BF)
            s.wexp[j, :, :, :, :, cols] = grad.reshape(4, 2, 2, 64, 256)
            return inside

        lax.fori_loop(0, 2, grad_exp, 0)
        return carry

    lax.fori_loop(0, 4, feed, 0)

    def rs_exp(j):
        return Bag(
            t=j, fin=j, parts=4, plane=None, piece=lambda a, b, c: s.wexp.at[j, a, b, c],
            col=lambda b, c: s.wexp.at[j, :, b, c], rb=lambda w: s.rb.at[j % SLOTS, w], ra=s.ra.at[j % SLOTS],
            rz=lambda k: s.rz.at[j, k],
        )

    def rs_in(i):
        return Bag(
            t=9 + i, fin=4 + i, parts=4, plane=None, piece=lambda a, b, c: s.win.at[i, a, b, c],
            col=lambda b, c: s.win.at[i, :, b, c], rb=lambda w: s.rb.at[(4 + i) % SLOTS, w],
            ra=s.ra.at[(4 + i) % SLOTS], rz=lambda k: s.rz.at[4 + i, k],
        )

    def rs_red(j):
        return Bag(
            t=4 + j, fin=None, parts=1, plane=j, piece=lambda a, b, c: s.wred.at[j, b, c],
            col=lambda b, c: s.wred.at[j, b, c], rb=lambda w: s.rb_red.at[j % SLOTS, w],
            ra=s.ra_red.at[j % SLOTS], rz=lambda k: s.rz_red.at[k],
        )

    def rs_out():
        return Bag(
            t=8, fin=None, parts=4, plane=None, piece=lambda a, b, c: s.wout.at[a, b, c, r],
            col=lambda b, c: s.wout.at[:, b, c, r], rb=lambda w: s.rb_out.at[w], ra=s.ra_out,
            rz=lambda k: s.rz_out.at[k],
        )

    def rs_small():
        return Bag(
            t=12, fin=None, parts=4, plane=None, piece=lambda a, b, c: s.sg.at[a, b, c],
            col=lambda b, c: s.sg.at[:, b, c], rb=lambda w: s.rb_sg.at[w], ra=s.ra_sg,
            rz=lambda k: s.rz_sg.at[k],
        )

    def rb_copy(it, which, yy, xx):
        return copy(it.col(yy, xx), it.rb(which), s.rsb_s.at[it.t, which], s.rsb_r.at[it.t, which], b_dev)

    def ra_copy(it):
        return copy(it.col(ya, xa), it.ra, s.rsa_s.at[it.t], s.rsa_r.at[it.t], a_dev)

    def rz_copy(it, k, at):
        return copy(it.piece(at, y, x), it.rz(k), s.rsz_s.at[it.t, k], s.rsz_r.at[it.t, k], z_dev[k])

    def add_into(it, yy, xx, sources):
        target = it.col(yy, xx)
        kind = F32 if it.t == 12 else BF

        def one(at):
            total = target[at].astype(F32)
            for src in sources:
                total = total + src[at].astype(F32)
            target[at] = total.astype(kind)

        if it.parts == 4:

            def body(i, carry):
                one(i)
                return carry
        else:

            def body(i, carry):
                one(pl.ds(pl.multiple_of(i * 32, 32), 32))
                return carry

        lax.fori_loop(0, 4, body, 0)

    def f0(it):
        rb_copy(it, 0, yc, xc).start()
        rb_copy(it, 1, yb, xb).start()

    def f1(it):
        rb_copy(it, 0, yc, xc).wait_recv()
        add_into(it, ya, xa, [it.rb(0)])
        ra_copy(it).start()

    def f2(it):
        rb_copy(it, 1, yb, xb).wait_recv()
        ra_copy(it).wait_recv()
        add_into(it, y, x, [it.rb(1), it.ra])

        if it.plane is None:
            for k in range(3):
                rz_copy(it, k, z_at[k]).start()
        else:

            @pl.when(z != it.plane)
            def _():
                k = (it.plane + 4 - z) % 4 - 1
                copy(
                    it.piece(z, y, x), it.rz(k), s.rsz_s.at[it.t, k], s.rsz_r.at[it.t, k],
                    (it.plane * 4 + y * 2 + x, r),
                ).start()

    def z_total(it):
        for k in range(3):
            rz_copy(it, k, z_at[k]).wait_recv()
        total = it.piece(z, y, x)[...].astype(F32)
        for k in range(3):
            total = total + it.rz(k)[...].astype(F32)
        return total

    def fin_copy(index):
        return copy(s.fin.at[index, o_rows], s.fin_in.at[index], s.fin_s.at[index], s.fin_r.at[index], core_dev)

    def small_fin():
        return copy(s.sfin, s.sfin_in, s.fin_s.at[7], s.fin_r.at[7], core_dev)

    def put(index, value, who):
        if index < 4:
            for i in range(4):
                at = pl.ds(pl.multiple_of((2 * (4 * index + i) + who) * 128, 128), 128)
                dwexp_ref[:, at] = value[:, i * 128 : (i + 1) * 128]
        else:
            dwin_ref[:, half_cols(index - 4, who)] = value

    def f4(it):
        if it.plane is not None:

            @pl.when(z == it.plane)
            def _():
                dwred_ref[...] = z_total(it)
        elif it.t == 8:
            dwout_ref[...] = z_total(it)
        elif it.t == 12:
            s.sfin[...] = z_total(it)
            small_fin().start()
        else:
            s.fin[it.fin] = z_total(it)
            fin_copy(it.fin).start()
            put(it.fin, s.fin[it.fin, my_rows], r)

    def f5(it):
        if it.fin is not None:
            fin_copy(it.fin).wait_recv()
            put(it.fin, s.fin_in[it.fin], o)
        elif it.t == 12:
            small_fin().wait_recv()
            row = lax.broadcasted_iota(jnp.int32, (16, 128), 0)
            own = s.sfin[...]
            dsmall_ref[...] = jnp.where(row < 8, own + s.sfin_in[...], own)

    def all_sent(it):
        rb_copy(it, 0, yc, xc).wait_send()
        rb_copy(it, 1, yb, xb).wait_send()
        ra_copy(it).wait_send()
        if it.plane is None:
            for k in range(3):
                rz_copy(it, k, z_at[k]).wait_send()
        else:

            @pl.when(z != it.plane)
            def _():
                k = (it.plane + 4 - z) % 4 - 1
                copy(
                    it.piece(z, y, x), it.rz(k), s.rsz_s.at[it.t, k], s.rsz_r.at[it.t, k],
                    (it.plane * 4 + y * 2 + x, r),
                ).wait_send()
        if it.fin is not None:
            fin_copy(it.fin).wait_send()
        elif it.t == 12:
            small_fin().wait_send()

    order = []
    for j in range(4):
        order += [rs_exp(j), rs_red(j)]
    order += [rs_out(), rs_in(0), rs_in(1), rs_in(2), rs_small()]

    def step(i):
        for event, lag in ((f0, 0), (f1, 1), (f2, 2), (f4, 3), (f5, 4)):
            if 0 <= i - lag < len(order):
                event(order[i - lag])

    core_copy(4, s.bn_acc.at[o], s.cross.at[0]).start()
    core_copy(5, s.out_acc.at[o], s.cross.at[1]).start()
    step(0)
    core_copy(4, s.bn_acc.at[o], s.cross.at[0]).wait_recv()

    def middle_back(i, carry):
        rows = pl.ds(pl.multiple_of(i * 128, 128), 128)
        unit, rate = centre(s.middle[rows])
        upstream = s.bn_acc[r, rows] + s.cross[0, rows]
        cot = s.c_all[r, rows].astype(F32)
        back = cot + norm_back(unit, rate, vec_row(5), upstream)
        s.bn_acc[r, rows] = back
        branch = back.astype(BF)
        s.wide[rows] = branch
        gain_t, shift_t, out_t, red_t = carry
        return (
            gain_t + jnp.sum(upstream * unit, axis=0, keepdims=True),
            shift_t + jnp.sum(upstream, axis=0, keepdims=True),
            out_t + jnp.sum(branch.astype(F32), axis=0, keepdims=True),
            red_t + jnp.sum(cot, axis=0, keepdims=True),
        )

    zero_row = jnp.zeros((1, 1024), F32)
    gain_t, shift_t, out_t, red_t = lax.fori_loop(0, 3, middle_back, (zero_row,) * 4)
    s.gvec[5:6] = gain_t
    s.gvec[6:7] = shift_t
    s.gvec[4:5] = out_t
    s.gvec[7:8] = red_t

    core_copy(0, s.half.at[o], s.half.at[o]).wait_send()
    core_copy(2, s.wout.at[:, :, :, r], s.wout.at[:, :, :, r]).wait_send()

    def back_att(n, carry):
        weight = s.wout[n].reshape(256, 1024)
        cols = pl.ds(pl.multiple_of((n % 2) * 256, 256), 256)
        s.half[n // 2, :, cols] = dot_nt(s.wide[...], weight).astype(BF)
        return carry

    lax.fori_loop(0, 4, back_att, 0)
    core_copy(6, s.half.at[o], s.ba_all.at[r]).start()
    s.ba_all[r] = s.half[r]
    step(1)
    sent(i_out)

    def grad_out(n, carry):
        cols = pl.ds(pl.multiple_of(n * 256, 256), 256)
        grad = dot(s.att_t[...], s.wide[:, cols]).astype(BF)
        s.wout[:, :, :, :, :, cols] = grad.reshape(4, 2, 2, 2, 32, 256)
        return carry

    lax.fori_loop(0, 4, grad_out, 0)
    core_copy(7, s.wout.at[:, :, :, o], s.outx).start()
    step(2)
    core_copy(5, s.out_acc.at[o], s.cross.at[1]).wait_recv()

    def result_tile(i, carry):
        rows = pl.ds(pl.multiple_of(i * 128, 128), 128)
        total = s.middle[rows] + s.out_acc[r, rows] + s.cross[1, rows] + vec_row(7)
        result_ref[rows] = total.astype(BF)
        return carry

    lax.fori_loop(0, 3, result_tile, 0)
    core_copy(6, s.ba_all.at[o], s.ba_all.at[o]).wait_recv()
    step(3)

    def attend_back(hp, carry):
        k_t = flip(s.qkv[1, hp])
        dims = pl.ds(pl.multiple_of(hp * 128, 128), 128)
        s.dkv[...] = jnp.zeros_like(s.dkv)
        for rb in range(6):
            keys = key_count(rb)
            rows = slice(rb * 128, (rb + 1) * 128)
            both = pair_rows(s.qkv[0, hp, rows])
            at = (rb % 3) * 128
            up = pair_rows(s.ba_all[rb // 3, at : at + 128, dims])
            scores = dot_nt(s.qkv[1, hp, 0:keys], both) * factor + pair_mask(keys, rb)
            probs = jnp.exp2(scores - s.lse[hp, rb, 0:1])
            back_probs = dot_nt(s.qkv[2, hp, 0:keys], up)
            weighted = probs * back_probs
            centre_row = jnp.sum(weighted, axis=0, keepdims=True)
            back_scores = (weighted - probs * centre_row).astype(BF)
            s.dkv[1, 0:keys] += dot(probs.astype(BF), up)
            s.dkv[0, 0:keys] += dot(back_scores, both)
            query = dot(k_t[:, 0:keys], back_scores)
            query = jnp.concatenate([query[0:64, 0:128], query[64:128, 128:256]], axis=0)
            s.ffb[0, rows, dims] = (query.T * HD**-0.5).astype(BF)
        s.ffb[1, :, dims] = (s.dkv[0] * HD**-0.5).astype(BF)
        s.ffb[2, :, dims] = s.dkv[1].astype(BF)
        return carry

    for hp in range(4):
        lax.fori_loop(hp, hp + 1, attend_back, 0)
        step(4 + hp)

    core_copy(5, s.out_acc.at[o], s.cross.at[1]).wait_send()

    def back_in(n, carry):
        cols = pl.ds(pl.multiple_of(n * 256, 256), 256)
        total = dot_nt(s.ffb[0], s.win[0, n].reshape(256, 512))
        total = total + dot_nt(s.ffb[1], s.win[1, n].reshape(256, 512))
        total = total + dot_nt(s.ffb[2], s.win[2, n].reshape(256, 512))
        s.out_acc[:, :, cols] = total.reshape(2, 384, 256)
        return carry

    lax.fori_loop(0, 4, back_in, 0)
    core_copy(8, s.out_acc.at[o], s.cross.at[0]).start()
    for i in range(3):
        sent(ag_in(i))

        def grad_in(n, carry, i=i):
            cols = pl.ds(pl.multiple_of(n * 256, 256), 256)
            grad = dot(s.n1t[...], s.ffb[i, :, cols]).astype(BF)
            s.win[i, :, :, :, :, cols] = grad.reshape(4, 2, 2, 64, 256)
            return carry

        lax.fori_loop(0, 2, grad_in, 0)

    core_copy(7, s.outx, s.outx).wait_recv()

    def add_out(i, carry):
        for yy in range(2):
            for xx in range(2):
                total = s.wout[i, yy, xx, r].astype(F32) + s.outx[i, yy, xx].astype(F32)
                s.wout[i, yy, xx, r] = total.astype(BF)
        return carry

    lax.fori_loop(0, 4, add_out, 0)
    step(8)
    step(9)
    step(10)

    core_copy(8, s.out_acc.at[o], s.cross.at[0]).wait_recv()

    def frame_back(i, carry):
        rows = pl.ds(pl.multiple_of(i * 128, 128), 128)
        unit, rate = centre(s.frames_all[r, rows].astype(F32))
        upstream = s.out_acc[r, rows] + s.cross[0, rows]
        back = s.bn_acc[r, rows] + norm_back(unit, rate, vec_row(0), upstream)
        fgrad_ref[rows] = back.astype(BF)
        gain_t, shift_t = carry
        return (
            gain_t + jnp.sum(upstream * unit, axis=0, keepdims=True),
            shift_t + jnp.sum(upstream, axis=0, keepdims=True),
        )

    gain_t, shift_t = lax.fori_loop(0, 3, frame_back, (zero_row,) * 2)
    s.gvec[0:1] = gain_t
    s.gvec[1:2] = shift_t
    s.gvec[2:4] = jnp.zeros((2, 1024), F32)
    s.gvec[2:3, my_half] = jnp.sum(s.ffb[0].astype(F32), axis=0, keepdims=True)
    s.gvec[3:4, my_half] = jnp.sum(s.ffb[2].astype(F32), axis=0, keepdims=True)
    s.sg[...] = jnp.zeros_like(s.sg)
    for zz in range(4):
        for yy in range(2):
            for xx in range(2):
                at = (zz * 2 + yy) * 128
                s.sg[zz, yy, xx, 0:8] = s.gvec[:, at : at + 128]
                at = (yy * 2 + xx) * 128
                s.sg[zz, yy, xx, 8:9] = s.gexp[zz, 0:1, at : at + 128]

    for i in range(11, len(order) + 4):
        step(i)

    for item in pre:
        item.wait_send()
    sent(i_small)
    core_copy(1, s.half_t.at[o], s.half_t.at[o]).wait_send()
    core_copy(3, s.n_all.at[r], s.n_all.at[r]).wait_send()
    core_copy(4, s.bn_acc.at[o], s.cross.at[0]).wait_send()
    core_copy(6, s.half.at[o], s.ba_all.at[r]).wait_send()
    core_copy(7, s.wout.at[:, :, :, o], s.outx).wait_send()
    core_copy(8, s.out_acc.at[o], s.cross.at[0]).wait_send()
    for it in order:
        all_sent(it)


def fused_shards(
    frames, frames_cotangent, phoneme_len, prompt_len, target_segment, first_gain, first_shift, inward_weight,
    query_bias, value_bias, outward_weight, outward_bias, second_gain, second_shift, expand_weight, expand_bias,
    reduce_weight, reduce_bias,
):
    number = lax.axis_index("dp") * 2 + lax.axis_index("role")
    quarter = number % 4
    rows = jnp.stack(
        [first_gain, first_shift, query_bias, value_bias, outward_bias, second_gain, second_shift, reduce_bias]
    )
    lane = jnp.arange(128) // 32
    rows = jnp.where(lane[None] == quarter, jnp.tile(rows, (1, 4)), jnp.zeros((), BF))
    small = jnp.concatenate([rows, expand_bias[None], jnp.zeros((7, 128), BF)], axis=0)

    scratch = scratch_list()
    vmem = pl.BlockSpec(memory_space=pltpu.VMEM)
    smem = pl.BlockSpec(memory_space=pltpu.SMEM)
    hbm = pl.BlockSpec(memory_space=pl.ANY)
    outs = pl.pallas_call(
        functools.partial(layer_kernel, tuple(scratch)),
        out_shape=[
            jax.ShapeDtypeStruct((384, 1024), BF),
            jax.ShapeDtypeStruct((384, 1024), BF),
            jax.ShapeDtypeStruct((32, 3072), F32),
            jax.ShapeDtypeStruct((32, 1024), F32),
            jax.ShapeDtypeStruct((32, 4096), F32),
            jax.ShapeDtypeStruct((128, 1024), F32),
            jax.ShapeDtypeStruct((16, 128), F32),
        ],
        in_specs=[smem, smem, vmem, hbm, hbm] + [vmem] * 5,
        out_specs=[vmem] * 7,
        scratch_shapes=list(scratch.values()),
        compiler_params=pltpu.CompilerParams(
            collective_id=0, has_side_effects=True, vmem_limit_bytes=62 * 1024 * 1024
        ),
    )(
        phoneme_len, prompt_len, target_segment, frames[0], frames_cotangent[0], small, inward_weight,
        outward_weight, expand_weight, reduce_weight,
    )
    result, frames_gradient, d_in, d_out, d_exp, d_red, d_small = outs
    mine = lax.dynamic_slice(d_small, (0, quarter * 32), (8, 32))
    return (
        result[None], frames_gradient[None], mine[0], mine[1], d_in, mine[2], mine[3], d_out, mine[4], mine[5],
        mine[6], d_exp, d_small[8], d_red, mine[7],
    )


def passed_along(block, axis, distance):
    devices = range(lax.axis_size(axis))
    route = [(i - distance, i) for i in devices if i - distance in devices]
    return lax.ppermute(block, axis, route)


def normalize(values, gain, shift):
    mean_value = jnp.mean(values, axis=-1, keepdims=True)
    centered = values - mean_value
    spread = jnp.mean(centered * centered, axis=-1, keepdims=True)
    return centered * lax.rsqrt(spread + EPS) * gain + shift


def smooth_gate(values):
    return jax.nn.gelu(values, approximate=False)


def inner_rows(left, right):
    return lax.dot_general(
        left, right, (((0,), (0,)), ((), ())), preferred_element_type=jnp.float32
    )


def outer_cols(left, right):
    return lax.dot_general(
        left, right, (((1,), (1,)), ((), ())), preferred_element_type=jnp.float32
    )


def plain_shards(
    frames,
    frames_cotangent,
    phoneme_len,
    prompt_len,
    target_segment,
    first_gain,
    first_shift,
    inward_weight,
    query_bias,
    value_bias,
    outward_weight,
    outward_bias,
    second_gain,
    second_shift,
    expand_weight,
    expand_bias,
    reduce_weight,
    reduce_bias,
):
    attention_part = (
        lax.all_gather(first_gain, ("dp", "role"), axis=0, tiled=True),
        lax.all_gather(first_shift, ("dp", "role"), axis=0, tiled=True),
        lax.all_gather(inward_weight, ("dp", "role"), axis=0, tiled=True),
        lax.all_gather(query_bias, ("dp", "role"), axis=0, tiled=True),
        lax.all_gather(value_bias, ("dp", "role"), axis=0, tiled=True),
        lax.all_gather(outward_weight, ("dp", "role"), axis=0, tiled=True),
        lax.all_gather(outward_bias, ("dp", "role"), axis=0, tiled=True),
    )
    (
        full_gain,
        full_shift,
        full_inward,
        full_query_bias,
        full_value_bias,
        full_outward,
        full_outward_bias,
    ) = attention_part
    side = lax.axis_index("role")
    local_rows = frames.shape[1]
    scale = HD ** (-0.5)
    current = frames[0].astype(jnp.float32)
    normed = normalize(
        current, full_gain.astype(jnp.float32), full_shift.astype(jnp.float32)
    ).astype(jnp.bfloat16)
    mixed = jnp.dot(normed, full_inward, preferred_element_type=jnp.float32)
    queries = (mixed[:, :D] + full_query_bias.astype(jnp.float32)).astype(jnp.bfloat16)
    keys_own = mixed[:, D : 2 * D].astype(jnp.bfloat16)
    values_own = (mixed[:, 2 * D :] + full_value_bias.astype(jnp.float32)).astype(jnp.bfloat16)
    remote_keys, remote_values = passed_along((keys_own, values_own), "role", 1)
    keys_all = jnp.concatenate([remote_keys, keys_own], axis=0)
    values_all = jnp.concatenate([remote_values, values_own], axis=0)
    row_index = jnp.arange(local_rows)[:, None]
    col_index = jnp.arange(2 * local_rows)[None, :]
    own_col = col_index - local_rows
    prefix_length = phoneme_len[0] + prompt_len[0]
    segment = target_segment[0]
    key_segment = jnp.concatenate([jnp.full((local_rows,), -1, jnp.int32), segment])
    prompt_rows = (own_col >= 0) & (own_col <= row_index) & (own_col < prefix_length)
    target_rows = (col_index < prefix_length) | (own_col >= 0) & (own_col <= row_index) & (
        key_segment[None, :] == segment[:, None]
    )
    allowed = jnp.where(side == 0, prompt_rows, target_rows)

    def attend(index):
        start = index * HD
        head_query = lax.dynamic_slice_in_dim(queries, start, HD, 1)
        head_key = lax.dynamic_slice_in_dim(keys_all, start, HD, 1)
        head_value = lax.dynamic_slice_in_dim(values_all, start, HD, 1)
        scores = outer_cols(head_query, head_key) * scale
        masked = jnp.where(allowed, scores, MASKED)
        peak = jnp.max(masked, axis=1, keepdims=True)
        expo = jnp.exp(masked - peak)
        total = jnp.sum(expo, axis=1, keepdims=True)
        probs = (expo / total).astype(jnp.bfloat16)
        return (
            jnp.dot(probs, head_value, preferred_element_type=jnp.float32),
            (peak + jnp.log(total))[:, 0],
        )

    head_outs, log_totals = lax.map(attend, jnp.arange(H))
    attended = head_outs.transpose(1, 0, 2).reshape(local_rows, D).astype(jnp.bfloat16)
    middle = (
        current
        + jnp.dot(attended, full_outward, preferred_element_type=jnp.float32)
        + full_outward_bias.astype(jnp.float32)
    )
    feed_part = (
        lax.all_gather(second_gain, ("dp", "role"), axis=0, tiled=True),
        lax.all_gather(second_shift, ("dp", "role"), axis=0, tiled=True),
        lax.all_gather(expand_weight, ("dp", "role"), axis=0, tiled=True),
        lax.all_gather(expand_bias, ("dp", "role"), axis=0, tiled=True),
        lax.all_gather(reduce_weight, ("dp", "role"), axis=0, tiled=True),
        lax.all_gather(reduce_bias, ("dp", "role"), axis=0, tiled=True),
    )
    full_gain_two, full_shift_two, full_expand, full_expand_bias, full_reduce, full_reduce_bias = (
        feed_part
    )
    gain_two = full_gain_two.astype(jnp.float32)
    shift_two = full_shift_two.astype(jnp.float32)
    normed_two = normalize(middle, gain_two, shift_two).astype(jnp.bfloat16)
    inner = jnp.dot(
        normed_two, full_expand, preferred_element_type=jnp.float32
    ) + full_expand_bias.astype(jnp.float32)
    active = smooth_gate(inner).astype(jnp.bfloat16)
    output = (
        middle
        + jnp.dot(active, full_reduce, preferred_element_type=jnp.float32)
        + full_reduce_bias.astype(jnp.float32)
    )
    result = output.astype(jnp.bfloat16)[None]
    again_expand = feed_part[2]
    again_reduce = feed_part[4]
    again_gain = attention_part[0].astype(jnp.float32)
    again_shift = attention_part[1].astype(jnp.float32)
    again_inward = attention_part[2]
    again_outward = attention_part[5]
    upstream = frames_cotangent[0]
    upstream_float = upstream.astype(jnp.float32)
    reduce_bias_term = jnp.sum(upstream_float, axis=0)
    reduce_weight_term = inner_rows(active, upstream)
    back_active = outer_cols(upstream, again_reduce)
    gate_pull = jax.vjp(smooth_gate, inner)[1]
    back_inner = gate_pull(back_active)[0].astype(jnp.bfloat16)
    expand_bias_term = jnp.sum(back_inner.astype(jnp.float32), axis=0)
    expand_weight_term = inner_rows(normed_two, back_inner)
    back_normed_two = outer_cols(back_inner, again_expand)
    second_pull = jax.vjp(normalize, middle, gain_two, shift_two)[1]
    middle_part, second_gain_term, second_shift_term = second_pull(back_normed_two)
    back_middle = upstream_float + middle_part
    back_branch = back_middle.astype(jnp.bfloat16)
    outward_bias_term = jnp.sum(back_branch.astype(jnp.float32), axis=0)
    outward_weight_term = inner_rows(attended, back_branch)
    back_attended = outer_cols(back_branch, again_outward).astype(jnp.bfloat16)

    def attend_back(inputs):
        index, log_total = inputs
        start = index * HD
        head_query = lax.dynamic_slice_in_dim(queries, start, HD, 1)
        head_key = lax.dynamic_slice_in_dim(keys_all, start, HD, 1)
        head_value = lax.dynamic_slice_in_dim(values_all, start, HD, 1)
        head_upstream = lax.dynamic_slice_in_dim(back_attended, start, HD, 1)
        scores = outer_cols(head_query, head_key) * scale
        probs = jnp.where(allowed, jnp.exp(scores - log_total[:, None]), 0.0)
        back_probs = outer_cols(head_upstream, head_value)
        centre = jnp.sum(probs * back_probs, axis=1, keepdims=True)
        back_scores = (probs * (back_probs - centre)).astype(jnp.bfloat16)
        back_query = jnp.dot(back_scores, head_key, preferred_element_type=jnp.float32) * scale
        back_key = inner_rows(back_scores, head_query) * scale
        back_value = inner_rows(probs.astype(jnp.bfloat16), head_upstream)
        return (back_query, back_key, back_value)

    head_query_grads, head_key_grads, head_value_grads = lax.map(
        attend_back, (jnp.arange(H), log_totals)
    )
    back_queries = head_query_grads.transpose(1, 0, 2).reshape(local_rows, D)
    back_keys_all = head_key_grads.transpose(1, 0, 2).reshape(2 * local_rows, D)
    back_values_all = head_value_grads.transpose(1, 0, 2).reshape(2 * local_rows, D)
    returned_keys, returned_values = (
        passed_along(back_keys_all[:local_rows].astype(jnp.bfloat16), "role", -1).astype(
            jnp.float32
        ),
        passed_along(back_values_all[:local_rows].astype(jnp.bfloat16), "role", -1).astype(
            jnp.float32
        ),
    )
    query_low = back_queries.astype(jnp.bfloat16)
    key_low = (back_keys_all[local_rows:] + returned_keys).astype(jnp.bfloat16)
    value_low = (back_values_all[local_rows:] + returned_values).astype(jnp.bfloat16)
    back_mixed = jnp.concatenate([query_low, key_low, value_low], axis=1)
    query_bias_term = jnp.sum(query_low.astype(jnp.float32), axis=0)
    value_bias_term = jnp.sum(value_low.astype(jnp.float32), axis=0)
    inward_weight_term = inner_rows(normed, back_mixed)
    back_normed = outer_cols(back_mixed, again_inward)
    first_pull = jax.vjp(normalize, current, again_gain, again_shift)[1]
    frame_part, first_gain_term, first_shift_term = first_pull(back_normed)
    frames_gradient = (back_middle + frame_part).astype(jnp.bfloat16)[None]
    totals = (
        lax.psum_scatter(first_gain_term, ("dp", "role"), scatter_dimension=0, tiled=True),
        lax.psum_scatter(first_shift_term, ("dp", "role"), scatter_dimension=0, tiled=True),
        lax.psum_scatter(inward_weight_term, ("dp", "role"), scatter_dimension=0, tiled=True),
        lax.psum_scatter(query_bias_term, ("dp", "role"), scatter_dimension=0, tiled=True),
        lax.psum_scatter(value_bias_term, ("dp", "role"), scatter_dimension=0, tiled=True),
        lax.psum_scatter(outward_weight_term, ("dp", "role"), scatter_dimension=0, tiled=True),
        lax.psum_scatter(outward_bias_term, ("dp", "role"), scatter_dimension=0, tiled=True),
        lax.psum_scatter(second_gain_term, ("dp", "role"), scatter_dimension=0, tiled=True),
        lax.psum_scatter(second_shift_term, ("dp", "role"), scatter_dimension=0, tiled=True),
        lax.psum_scatter(expand_weight_term, ("dp", "role"), scatter_dimension=0, tiled=True),
        lax.psum_scatter(expand_bias_term, ("dp", "role"), scatter_dimension=0, tiled=True),
        lax.psum_scatter(reduce_weight_term, ("dp", "role"), scatter_dimension=0, tiled=True),
        lax.psum_scatter(reduce_bias_term, ("dp", "role"), scatter_dimension=0, tiled=True),
    )
    return (
        result,
        frames_gradient,
        totals[0],
        totals[1],
        totals[2],
        totals[3],
        totals[4],
        totals[5],
        totals[6],
        totals[7],
        totals[8],
        totals[9],
        totals[10],
        totals[11],
        totals[12],
    )


def solution(mesh):
    placed = (
        P("dp", "role", None),
        P("dp", "role", None),
        P("dp"),
        P("dp"),
        P("dp", None),
        P(("dp", "role")),
        P(("dp", "role")),
        P(("dp", "role"), None),
        P(("dp", "role")),
        P(("dp", "role")),
        P(("dp", "role"), None),
        P(("dp", "role")),
        P(("dp", "role")),
        P(("dp", "role")),
        P(("dp", "role"), None),
        P(("dp", "role")),
        P(("dp", "role"), None),
        P(("dp", "role")),
    )
    fused = mesh.shape["dp"] == 16 and mesh.shape["role"] == 2
    return jax.shard_map(
        fused_shards if fused else plain_shards,
        mesh=mesh,
        in_specs=placed,
        out_specs=(
            P("dp", "role", None),
            P("dp", "role", None),
            P(("dp", "role")),
            P(("dp", "role")),
            P(("dp", "role"), None),
            P(("dp", "role")),
            P(("dp", "role")),
            P(("dp", "role"), None),
            P(("dp", "role")),
            P(("dp", "role")),
            P(("dp", "role")),
            P(("dp", "role"), None),
            P(("dp", "role")),
            P(("dp", "role"), None),
            P(("dp", "role")),
        ),
        check_vma=False,
    )
```

```python
import functools

import jax
import jax.numpy as jnp
from jax import lax
from jax.experimental import pallas as pl
from jax.experimental.pallas import tpu as pltpu
from jax.sharding import PartitionSpec as P

D = 1024
H = 16
HD = 64
EPS = 1e-05
MASKED = -1e30
LOG2E = 1.4426950408889634
BF = jnp.bfloat16
F32 = jnp.float32
MESH = pl.DeviceIdType.MESH


def dot(left, right):
    return lax.dot_general(left, right, (((1,), (0,)), ((), ())), preferred_element_type=F32)


def dot_nt(left, right):
    return lax.dot_general(left, right, (((1,), (1,)), ((), ())), preferred_element_type=F32)


def flip(value):
    return value.astype(F32).T.astype(value.dtype)


def centre(values):
    mean_value = jnp.mean(values, axis=-1, keepdims=True)
    centered = values - mean_value
    spread = jnp.mean(centered * centered, axis=-1, keepdims=True)
    return centered * lax.rsqrt(spread + EPS), lax.rsqrt(spread + EPS)


def norm_back(unit, rate, gain, upstream):
    pulled = upstream * gain
    first = jnp.mean(pulled, axis=-1, keepdims=True)
    second = jnp.mean(pulled * unit, axis=-1, keepdims=True)
    return rate * (pulled - first - unit * second)


SLOTS = 4
LEAD = 1


def scratch_list():
    dma = pltpu.SemaphoreType.DMA
    v = pltpu.VMEM
    return dict(
        small=v((4, 2, 2, 2, 16, 128), BF),
        vec=v((8, 1024), F32),
        ebias=v((4, 8, 512), F32),
        frames_all=v((2, 384, 1024), BF),
        c_all=v((2, 384, 1024), BF),
        n_all=v((2, 384, 1024), BF),
        n1t=v((1024, 768), BF),
        n2t=v((1024, 768), BF),
        win=v((6, 4, 2, 2, 64, 256), BF),
        wout=v((4, 2, 2, 2, 32, 1024), BF),
        wexp=v((4, 4, 2, 2, 64, 512), BF),
        wred=v((4, 2, 2, 128, 1024), BF),
        stage=v((2, 32, 2048), BF),
        qkv=v((3, 4, 768, 128), BF),
        mask=v((768, 768), BF),
        lse=v((4, 6, 8, 256), F32),
        half=v((2, 384, 512), BF),
        half_t=v((2, 512, 384), BF),
        wide=v((384, 1024), BF),
        att_t=v((1024, 384), BF),
        middle=v((384, 1024), F32),
        out_acc=v((2, 384, 1024), F32),
        bn_acc=v((2, 384, 1024), F32),
        cross=v((2, 384, 1024), F32),
        ffb=v((3, 768, 512), BF),
        act_t=v((512, 768), BF),
        ba_all=v((2, 384, 512), BF),
        dkv=v((2, 768, 128), F32),
        gvec=v((8, 1024), F32),
        gexp=v((4, 8, 512), F32),
        outx=v((4, 2, 2, 32, 1024), BF),
        rb=v((SLOTS, 2, 4, 64, 512), BF),
        ra=v((3, 4, 64, 512), BF),
        rz=v((4, 3, 64, 512), BF),
        rz_in=v((6, 3, 64, 256), BF),
        rb_red=v((SLOTS, 2, 128, 1024), BF),
        ra_red=v((3, 128, 1024), BF),
        rz_red=v((3, 128, 1024), BF),
        rb_out=v((2, 4, 32, 1024), BF),
        ra_out=v((4, 32, 1024), BF),
        rz_out=v((3, 32, 1024), BF),
        sg=v((4, 2, 2, 16, 128), F32),
        rb_sg=v((2, 4, 16, 128), F32),
        ra_sg=v((4, 16, 128), F32),
        rz_sg=v((3, 16, 128), F32),
        fin=v((4, 64, 512), F32),
        fin_in=v((4, 32, 512), F32),
        fin_w=v((6, 64, 256), F32),
        fin_w_in=v((6, 32, 256), F32),
        sfin=v((16, 128), F32),
        sfin_in=v((16, 128), F32),
        own_s=dma((2,)),
        pre_s=dma((13,)),
        pre_r=dma((13,)),
        agz_s=dma((16, 3)),
        agz_r=dma((16, 3)),
        aga_s=dma((16,)),
        aga_r=dma((16,)),
        agb_s=dma((16, 2)),
        agb_r=dma((16, 2)),
        core_s=dma((9,)),
        core_r=dma((9,)),
        rsb_s=dma((16, 2)),
        rsb_r=dma((16, 2)),
        rsa_s=dma((16,)),
        rsa_r=dma((16,)),
        rsz_s=dma((16, 3)),
        rsz_r=dma((16, 3)),
        fin_s=dma((11,)),
        fin_r=dma((11,)),
    )


class Bag:
    def __init__(self, **kw):
        self.__dict__.update(kw)


N_IN = 10
N_OUT = 7


def layer_kernel(names, *refs):
    (phon_ref, prom_ref, seg_ref, frames_ref, cot_ref, small_in, win_in, wout_in, wexp_in, wred_in) = refs[:N_IN]
    (result_ref, fgrad_ref, dwin_ref, dwout_ref, dwexp_ref, dwred_ref, dsmall_ref) = refs[N_IN : N_IN + N_OUT]
    s = Bag(**dict(zip(names, refs[N_IN + N_OUT :])))

    dp = lax.axis_index("dp")
    r = lax.axis_index("role")
    o = 1 - r
    z, y, x = dp // 4, (dp // 2) % 2, dp % 2
    ya, xa = y + r * (1 - 2 * y), x + (1 - r) * (1 - 2 * x)
    yb, xb = y + (1 - r) * (1 - 2 * y), x + r * (1 - 2 * x)
    yc, xc = 1 - y, 1 - x
    core_dev = (dp, o)
    a_dev = (z * 4 + ya * 2 + xa, r)
    b_dev = (z * 4 + yb * 2 + xb, r)
    z_dev = [(((z + k) % 4) * 4 + y * 2 + x, r) for k in (1, 2, 3)]
    z_at = [(z + k) % 4 for k in (1, 2, 3)]
    z_from = [(z + 4 - k) % 4 for k in (1, 2, 3)]

    def copy(src, dst, ss, rs, dev):
        return pltpu.make_async_remote_copy(
            src_ref=src, dst_ref=dst, send_sem=ss, recv_sem=rs, device_id=dev, device_id_type=MESH
        )

    barrier = pltpu.get_barrier_semaphore()
    for dev in z_dev + [a_dev, b_dev, core_dev]:
        pl.semaphore_signal(barrier, inc=1, device_id=dev, device_id_type=MESH)
    pl.semaphore_wait(barrier, 6)

    my_rows = pl.ds(pl.multiple_of(r * 32, 32), 32)
    o_rows = pl.ds(pl.multiple_of(o * 32, 32), 32)

    def part_cols(part, who):
        return pl.ds(pl.multiple_of((part // 2) * 1024 + who * 512 + (part % 2) * 256, 256), 256)

    for block in range(16):
        for who in range(2):
            s.stage[who, :, block * 128 : (block + 1) * 128] = wexp_in[
                :, (2 * block + who) * 128 : (2 * block + who + 1) * 128
            ]
    pre = []
    pre.append(copy(small_in, s.small.at[z, y, x, r], s.pre_s.at[0], s.pre_r.at[0], core_dev))
    for i in range(6):
        pre.append(
            copy(
                win_in.at[:, part_cols(i, o)],
                s.win.at[i, z, y, x, my_rows],
                s.pre_s.at[1 + i],
                s.pre_r.at[1 + i],
                core_dev,
            )
        )
    pre.append(copy(frames_ref, s.frames_all.at[r], s.pre_s.at[7], s.pre_r.at[7], core_dev))
    for j in range(4):
        pre.append(
            copy(
                s.stage.at[o, :, pl.ds(j * 512, 512)],
                s.wexp.at[j, z, y, x, my_rows],
                s.pre_s.at[8 + j],
                s.pre_r.at[8 + j],
                core_dev,
            )
        )
    pre.append(copy(cot_ref, s.c_all.at[r], s.pre_s.at[12], s.pre_r.at[12], core_dev))
    for item in pre:
        item.start()
    own_frames = pltpu.make_async_copy(frames_ref, s.frames_all.at[r], s.own_s.at[0])
    own_cot = pltpu.make_async_copy(cot_ref, s.c_all.at[r], s.own_s.at[1])
    own_frames.start()
    own_cot.start()
    s.small[z, y, x, r] = small_in[...]
    for i in range(6):
        s.win[i, z, y, x, my_rows] = win_in[:, part_cols(i, r)]
    s.wout[z, y, x, r] = wout_in[...]
    s.wred[z, y, x] = wred_in[...]
    for j in range(4):
        s.wexp[j, z, y, x, my_rows] = s.stage[r, :, j * 512 : (j + 1) * 512]

    def ag_small():
        return Bag(t=0, piece=lambda a, b, c: s.small.at[a, b, c], col=lambda b, c: s.small.at[:, b, c], plane=None)

    def ag_in(i):
        return Bag(
            t=1 + i, piece=lambda a, b, c: s.win.at[i, a, b, c], col=lambda b, c: s.win.at[i, :, b, c], plane=None
        )

    def ag_out():
        return Bag(
            t=7, piece=lambda a, b, c: s.wout.at[a, b, c, r], col=lambda b, c: s.wout.at[:, b, c, r], plane=None
        )

    def ag_exp(j):
        return Bag(
            t=8 + 2 * j,
            piece=lambda a, b, c: s.wexp.at[j, a, b, c],
            col=lambda b, c: s.wexp.at[j, :, b, c],
            plane=None,
        )

    def ag_red(j):
        return Bag(
            t=9 + 2 * j, piece=lambda a, b, c: s.wred.at[j, b, c], col=lambda b, c: s.wred.at[j, b, c], plane=j
        )

    def z_copies(it):
        return [
            copy(it.piece(z, y, x), it.piece(z, y, x), s.agz_s.at[it.t, k], s.agz_r.at[it.t, k], z_dev[k])
            for k in range(3)
        ]

    def a_copy(it, yy, xx):
        return copy(it.col(yy, xx), it.col(yy, xx), s.aga_s.at[it.t], s.aga_r.at[it.t], a_dev)

    def b_copy(it, which, yy, xx):
        return copy(it.col(yy, xx), it.col(yy, xx), s.agb_s.at[it.t, which], s.agb_r.at[it.t, which], b_dev)

    def e0(it):
        def go():
            for c in z_copies(it):
                c.start()

        if it.plane is None:
            go()
        else:
            pl.when(z == it.plane)(go)

    def e1(it):
        if it.plane is None:
            for k in range(3):
                p = it.piece(z_from[k], y, x)
                copy(p, p, s.agz_s.at[it.t, k], s.agz_r.at[it.t, k], z_dev[k]).wait_recv()
        else:

            @pl.when(z != it.plane)
            def _():
                k = (z + 4 - it.plane) % 4 - 1
                p = it.piece(z, y, x)
                copy(p, p, s.agz_s.at[it.t, k], s.agz_r.at[it.t, k], z_dev[0]).wait_recv()

        a_copy(it, y, x).start()
        b_copy(it, 0, y, x).start()

    def e2(it):
        a_copy(it, ya, xa).wait_recv()
        b_copy(it, 1, ya, xa).start()

    def e3(it):
        b_copy(it, 0, yb, xb).wait_recv()
        b_copy(it, 1, yc, xc).wait_recv()

    def sent(it):
        def go():
            for c in z_copies(it):
                c.wait_send()

        if it.plane is None:
            go()
        else:
            pl.when(z == it.plane)(go)
        a_copy(it, y, x).wait_send()
        b_copy(it, 0, y, x).wait_send()
        b_copy(it, 1, ya, xa).wait_send()

    i_small, i_out = ag_small(), ag_out()
    i_w = [ag_in(i) for i in range(6)]

    def pre_in(index, dst):
        copy(dst, dst, s.pre_s.at[index], s.pre_r.at[index], core_dev).wait_recv()

    def begin(i):
        pre_in(1 + i, s.win.at[i, z, y, x, o_rows])
        e0(i_w[i])

    pre_in(0, s.small.at[z, y, x, o])
    e0(i_small)
    begin(0)
    begin(1)
    e1(i_small)
    e1(i_w[0])
    begin(2)

    own_frames.wait()
    own_cot.wait()
    prefix = phon_ref[0] + prom_ref[0]
    seg_row = seg_ref[...].astype(F32)
    seg_wide = jnp.broadcast_to(seg_row, (384, 384))
    seg_tall = seg_wide.T
    key_at = lax.broadcasted_iota(jnp.int32, (384, 384), 0)
    row_at = lax.broadcasted_iota(jnp.int32, (384, 384), 1)
    causal = key_at <= row_at
    seen = key_at < prefix

    def as_bias(allowed):
        return jnp.where(allowed, 0.0, MASKED).astype(BF)

    s.mask[0:384, 0:384] = as_bias(causal & seen)
    s.mask[0:384, 384:768] = as_bias(seen)
    s.mask[384:768, 384:768] = as_bias(causal & (seg_wide == seg_tall))

    e2(i_small)
    e1(i_w[1])
    e2(i_w[0])
    begin(3)
    e3(i_small)

    def tile_sum(q):
        total = jnp.zeros((16, 128), F32)
        for xx in range(2):
            for who in range(2):
                total = total + s.small[q // 2, q % 2, xx, who].astype(F32)
        return total

    for q in range(8):
        s.vec[:, q * 128 : (q + 1) * 128] = tile_sum(q)[0:8]
    for j in range(4):
        for yy in range(2):
            for xx in range(2):
                at = (yy * 2 + xx) * 128
                s.ebias[j, 0:1, at : at + 128] = s.small[j, yy, xx, r].astype(F32)[8:9]

    def vec_row(i):
        return s.vec[i : i + 1, :]

    pre_in(7, s.frames_all.at[o])

    def norm_tile(i, carry):
        who, rows = i // 3, pl.ds(pl.multiple_of((i % 3) * 128, 128), 128)
        unit, _ = centre(s.frames_all[who, rows].astype(F32))
        normed = unit * vec_row(0) + vec_row(1)
        s.n_all[who, rows] = normed.astype(BF)
        s.n1t[:, pl.ds(pl.multiple_of(i * 128, 128), 128)] = normed.T.astype(BF)
        return carry

    lax.fori_loop(0, 6, norm_tile, 0)

    def project(part):
        section, n = part // 2, part % 2
        mixed = dot(s.n_all[...].reshape(768, 1024), s.win[part].reshape(1024, 256))
        if section != 1:
            bias_at = pl.ds(pl.multiple_of(r * 512 + n * 256, 256), 256)
            bias_row = 2 if section == 0 else 3
            mixed = mixed + s.vec[bias_row : bias_row + 1, bias_at]
        mixed = mixed.astype(BF)
        s.qkv[section, 2 * n] = mixed[:, 0:128]
        s.qkv[section, 2 * n + 1] = mixed[:, 128:256]

    e1(i_w[2])
    e2(i_w[1])
    begin(4)
    e3(i_w[0])
    project(0)
    e1(i_w[3])
    e2(i_w[2])
    begin(5)
    e3(i_w[1])
    project(1)
    e1(i_w[4])
    e2(i_w[3])
    e0(i_out)
    e3(i_w[2])
    project(2)
    for j in range(4):
        pre_in(8 + j, s.wexp.at[j, z, y, x, o_rows])
    e1(i_w[5])
    e2(i_w[4])
    e0(ag_exp(0))
    e3(i_w[3])
    project(3)
    e1(i_out)
    e2(i_w[5])
    e0(ag_red(0))
    e3(i_w[4])
    project(4)
    e1(ag_exp(0))
    e2(i_out)
    e3(i_w[5])
    project(5)
    e0(ag_exp(1))
    e1(ag_red(0))

    factor = HD**-0.5 * LOG2E
    low_lane = lax.broadcasted_iota(jnp.int32, (128, 128), 1) < 64

    def pair_rows(block):
        zero = jnp.zeros_like(block)
        return jnp.concatenate([jnp.where(low_lane, block, zero), jnp.where(low_lane, zero, block)], axis=0)

    def pair_mask(keys, rb):
        bias = s.mask[0:keys, rb * 128 : (rb + 1) * 128].astype(F32)
        return jnp.concatenate([bias, bias], axis=1)

    def key_count(rb):
        return (rb + 1) * 128 if rb < 3 else 384 + (rb - 2) * 128

    def attend(hp, carry):
        v_t = flip(s.qkv[2, hp])
        dims = pl.ds(pl.multiple_of(hp * 128, 128), 128)
        for rb in range(6):
            keys = key_count(rb)
            both = pair_rows(s.qkv[0, hp, rb * 128 : (rb + 1) * 128])
            scores = dot_nt(s.qkv[1, hp, 0:keys], both) * factor + pair_mask(keys, rb)
            peak = jnp.max(scores, axis=0, keepdims=True)
            expo = jnp.exp2(scores - peak)
            total = jnp.sum(expo, axis=0, keepdims=True)
            heads = dot(v_t[:, 0:keys], expo.astype(BF)) / total
            s.lse[hp, rb] = jnp.broadcast_to(peak + jnp.log2(total), (8, 256))
            out = jnp.concatenate([heads[0:64, 0:128], heads[64:128, 128:256]], axis=0)
            at = (rb % 3) * 128
            s.half_t[rb // 3, dims, at : at + 128] = out.astype(BF)
            s.half[rb // 3, at : at + 128, dims] = out.T.astype(BF)
        return carry

    lax.fori_loop(0, 4, attend, 0)

    my_half = pl.ds(pl.multiple_of(r * 512, 512), 512)
    o_half = pl.ds(pl.multiple_of(o * 512, 512), 512)

    def core_copy(index, src, dst):
        return copy(src, dst, s.core_s.at[index], s.core_r.at[index], core_dev)

    core_copy(0, s.half.at[o], s.wide.at[:, my_half]).start()
    core_copy(1, s.half_t.at[o], s.att_t.at[my_half]).start()
    s.wide[:, my_half] = s.half[r]
    s.att_t[my_half] = s.half_t[r]
    e2(ag_exp(0))
    e3(i_out)
    out_swap = core_copy(2, s.wout.at[:, :, :, r], s.wout.at[:, :, :, r])
    out_swap.start()
    core_copy(0, s.wide.at[:, o_half], s.wide.at[:, o_half]).wait_recv()
    core_copy(1, s.att_t.at[o_half], s.att_t.at[o_half]).wait_recv()
    core_copy(2, s.wout.at[:, :, :, o], s.wout.at[:, :, :, o]).wait_recv()
    e0(ag_red(1))
    e1(ag_exp(1))
    e2(ag_red(0))

    def out_tile(n, carry):
        cols = pl.ds(pl.multiple_of(n * 256, 256), 256)
        branch = dot(s.wide[...], s.wout[:, :, :, :, :, cols].reshape(1024, 256))
        s.middle[:, cols] = s.frames_all[r, :, cols].astype(F32) + branch + s.vec[4:5, cols]
        return carry

    lax.fori_loop(0, 4, out_tile, 0)

    def norm_two(i, carry):
        rows = pl.ds(pl.multiple_of(i * 128, 128), 128)
        unit, _ = centre(s.middle[rows])
        s.n_all[r, rows] = (unit * vec_row(5) + vec_row(6)).astype(BF)
        return carry

    lax.fori_loop(0, 3, norm_two, 0)
    core_copy(3, s.n_all.at[r], s.n_all.at[r]).start()
    pre_in(12, s.c_all.at[o])
    s.out_acc[...] = jnp.zeros_like(s.out_acc)
    s.bn_acc[...] = jnp.zeros_like(s.bn_acc)
    core_copy(3, s.n_all.at[o], s.n_all.at[o]).wait_recv()

    def flip_two(i, carry):
        who, rows = i // 3, pl.ds(pl.multiple_of((i % 3) * 128, 128), 128)
        s.n2t[:, pl.ds(pl.multiple_of(i * 128, 128), 128)] = flip(s.n_all[who, rows])
        return carry

    lax.fori_loop(0, 6, flip_two, 0)

    def rs_exp(j):
        return Bag(
            t=j, fin=j, parts=4, plane=None, piece=lambda a, b, c: s.wexp.at[j, a, b, c],
            col=lambda b, c: s.wexp.at[j, :, b, c], rb=lambda w: s.rb.at[j % SLOTS, w], ra=s.ra.at[j % 3],
            rz=lambda k: s.rz.at[j, k],
        )

    def rs_in(i):
        slot, part = ((0, 0), (1, 0), (0, 1), (1, 1), (2, 0), (2, 1))[i]
        half = slice(256 * part, 256 * part + 256)
        again = slice(256 * (i % 2), 256 * (i % 2) + 256)
        return Bag(
            t=9 + i, fin=4 + i, parts=4, plane=None, piece=lambda a, b, c: s.win.at[i, a, b, c],
            col=lambda b, c: s.win.at[i, :, b, c], rb=lambda w: s.rb.at[slot, w, :, :, half],
            ra=s.ra.at[(1, 2, 0)[i // 2], :, :, again], rz=lambda k: s.rz_in.at[i, k],
        )

    def rs_red(j):
        return Bag(
            t=4 + j, fin=None, parts=1, plane=j, piece=lambda a, b, c: s.wred.at[j, b, c],
            col=lambda b, c: s.wred.at[j, b, c], rb=lambda w: s.rb_red.at[j % SLOTS, w],
            ra=s.ra_red.at[j % 3], rz=lambda k: s.rz_red.at[k],
        )

    def rs_out():
        return Bag(
            t=8, fin=None, parts=4, plane=None, piece=lambda a, b, c: s.wout.at[a, b, c, r],
            col=lambda b, c: s.wout.at[:, b, c, r], rb=lambda w: s.rb_out.at[w], ra=s.ra_out,
            rz=lambda k: s.rz_out.at[k],
        )

    def rs_small():
        return Bag(
            t=15, fin=None, parts=4, plane=None, piece=lambda a, b, c: s.sg.at[a, b, c],
            col=lambda b, c: s.sg.at[:, b, c], rb=lambda w: s.rb_sg.at[w], ra=s.ra_sg,
            rz=lambda k: s.rz_sg.at[k],
        )

    def rb_copy(it, which, yy, xx):
        return copy(it.col(yy, xx), it.rb(which), s.rsb_s.at[it.t, which], s.rsb_r.at[it.t, which], b_dev)

    def ra_copy(it):
        return copy(it.col(ya, xa), it.ra, s.rsa_s.at[it.t], s.rsa_r.at[it.t], a_dev)

    def rz_copy(it, k, at):
        return copy(it.piece(at, y, x), it.rz(k), s.rsz_s.at[it.t, k], s.rsz_r.at[it.t, k], z_dev[k])

    def add_into(it, yy, xx, sources):
        target = it.col(yy, xx)
        kind = F32 if it.t == 15 else BF

        def one(at):
            total = target[at].astype(F32)
            for src in sources:
                total = total + src[at].astype(F32)
            target[at] = total.astype(kind)

        if it.parts == 4:

            def body(i, carry):
                one(i)
                return carry
        else:

            def body(i, carry):
                one(pl.ds(pl.multiple_of(i * 32, 32), 32))
                return carry

        lax.fori_loop(0, 4, body, 0)

    def f0(it):
        rb_copy(it, 0, yc, xc).start()
        rb_copy(it, 1, yb, xb).start()

    def f1(it):
        rb_copy(it, 0, yc, xc).wait_recv()
        add_into(it, ya, xa, [it.rb(0)])
        ra_copy(it).start()

    def f2(it):
        rb_copy(it, 1, yb, xb).wait_recv()
        ra_copy(it).wait_recv()
        add_into(it, y, x, [it.rb(1), it.ra])

        if it.plane is None:
            for k in range(3):
                rz_copy(it, k, z_at[k]).start()
        else:

            @pl.when(z != it.plane)
            def _():
                k = (it.plane + 4 - z) % 4 - 1
                copy(
                    it.piece(z, y, x), it.rz(k), s.rsz_s.at[it.t, k], s.rsz_r.at[it.t, k],
                    (it.plane * 4 + y * 2 + x, r),
                ).start()

    def z_total(it):
        for k in range(3):
            rz_copy(it, k, z_at[k]).wait_recv()
        total = it.piece(z, y, x)[...].astype(F32)
        for k in range(3):
            total = total + it.rz(k)[...].astype(F32)
        return total

    def fin_refs(index):
        if index < 4:
            return s.fin.at[index], s.fin_in.at[index]
        return s.fin_w.at[index - 4], s.fin_w_in.at[index - 4]

    def fin_copy(index):
        out, back = fin_refs(index)
        return copy(out.at[o_rows], back, s.fin_s.at[index], s.fin_r.at[index], core_dev)

    def small_fin():
        return copy(s.sfin, s.sfin_in, s.fin_s.at[10], s.fin_r.at[10], core_dev)

    def put(index, value, who):
        if index < 4:
            for i in range(4):
                at = pl.ds(pl.multiple_of((2 * (4 * index + i) + who) * 128, 128), 128)
                dwexp_ref[:, at] = value[:, i * 128 : (i + 1) * 128]
        else:
            dwin_ref[:, part_cols(index - 4, who)] = value

    def f4(it):
        if it.plane is not None:

            @pl.when(z == it.plane)
            def _():
                dwred_ref[...] = z_total(it)
        elif it.t == 8:
            dwout_ref[...] = z_total(it)
        elif it.t == 15:
            s.sfin[...] = z_total(it)
            small_fin().start()
        else:
            out, _ = fin_refs(it.fin)
            out[...] = z_total(it)
            fin_copy(it.fin).start()
            put(it.fin, out[my_rows], r)

    def f5(it):
        if it.fin is not None:
            fin_copy(it.fin).wait_recv()
            put(it.fin, fin_refs(it.fin)[1][...], o)
        elif it.t == 15:
            small_fin().wait_recv()
            row = lax.broadcasted_iota(jnp.int32, (16, 128), 0)
            own = s.sfin[...]
            dsmall_ref[...] = jnp.where(row < 8, own + s.sfin_in[...], own)

    def all_sent(it):
        rb_copy(it, 0, yc, xc).wait_send()
        rb_copy(it, 1, yb, xb).wait_send()
        ra_copy(it).wait_send()
        if it.plane is None:
            for k in range(3):
                rz_copy(it, k, z_at[k]).wait_send()
        else:

            @pl.when(z != it.plane)
            def _():
                k = (it.plane + 4 - z) % 4 - 1
                copy(
                    it.piece(z, y, x), it.rz(k), s.rsz_s.at[it.t, k], s.rsz_r.at[it.t, k],
                    (it.plane * 4 + y * 2 + x, r),
                ).wait_send()
        if it.fin is not None:
            fin_copy(it.fin).wait_send()
        elif it.t == 15:
            small_fin().wait_send()

    order = []
    for j in range(4):
        order += [rs_red(j), rs_exp(j)]
    order += [rs_out()] + [rs_in(i) for i in range(6)] + [rs_small()]

    def step(i):
        for event, lag in ((f0, -LEAD), (f1, 1), (f2, 2), (f4, 3), (f5, 4)):
            if 0 <= i - lag < len(order):
                event(order[i - lag])

    def when(cond, go):
        if isinstance(cond, bool):
            if cond:
                go()
        else:
            pl.when(cond)(go)

    def feed(j, between):
        def ahead_one():
            e1(ag_red(j + 1))
            e2(ag_exp(j + 1))

        def ahead_two():
            e0(ag_red(j + 2))
            e1(ag_exp(j + 2))

        when(j < 2, lambda: e0(ag_exp(j + 2)))
        when(j < 3, ahead_one)
        e3(ag_exp(j))
        when(j < 2, ahead_two)
        when(j < 3, lambda: e2(ag_red(j + 1)))
        e3(ag_red(j))
        sent(ag_exp(j))
        sent(ag_red(j))
        between(0)

        def hidden(n, inside):
            cols = pl.ds(pl.multiple_of(n * 256, 256), 256)
            left = s.n_all[...].reshape(768, 1024)
            inner = dot(left, s.wexp[j, :, :, :, :, cols].reshape(1024, 256)) + s.ebias[j, 0:1, cols]
            phi = 0.5 + 0.5 * lax.erf(inner * (2.0**-0.5))
            active = inner * phi
            s.ffb[0, :, cols] = active.astype(BF)
            s.act_t[cols] = active.T.astype(BF)
            slope = phi + inner * (jnp.exp(-0.5 * inner * inner) * 0.3989422804014327)
            up = s.c_all[...].reshape(768, 1024)
            back = (dot_nt(up, s.wred[j, n].reshape(256, 1024)) * slope).astype(BF)
            s.ffb[1, :, cols] = back
            s.gexp[j, 0:1, cols] = jnp.sum(back.astype(F32), axis=0, keepdims=True)
            return inside

        lax.fori_loop(0, 2, hidden, 0)

        def wide_tile(n, inside):
            cols = pl.ds(pl.multiple_of(n * 256, 256), 256)
            part = dot(s.ffb[0], s.wred[j, :, :, :, cols].reshape(512, 256))
            s.out_acc[:, :, cols] += part.reshape(2, 384, 256)
            back = dot_nt(s.ffb[1], s.wexp[j, n].reshape(256, 512))
            s.bn_acc[:, :, cols] += back.reshape(2, 384, 256)
            return inside

        lax.fori_loop(0, 4, wide_tile, 0)
        between(1)

        def grad_red(n, inside):
            cols = pl.ds(pl.multiple_of(n * 256, 256), 256)
            up = s.c_all[:, :, cols].reshape(768, 256)
            s.wred[j, :, :, :, cols] = dot(s.act_t[...], up).astype(BF).reshape(2, 2, 128, 256)
            return inside

        lax.fori_loop(0, 4, grad_red, 0)

        def grad_exp(n, inside):
            cols = pl.ds(pl.multiple_of(n * 256, 256), 256)
            grad = dot(s.n2t[...], s.ffb[1, :, cols]).astype(BF)
            s.wexp[j, :, :, :, :, cols] = grad.reshape(4, 2, 2, 64, 256)
            return inside

        lax.fori_loop(0, 2, grad_exp, 0)
        between(2)

    def early_feed(j, carry):
        feed(j, lambda place: None)
        return carry

    lax.fori_loop(0, 3, early_feed, 0)

    def start_reduction(place):
        if place == 0:
            for it in order[:LEAD]:
                f0(it)
            step(0)
        elif place == 1:
            core_copy(4, s.bn_acc.at[o], s.cross.at[0]).start()
            core_copy(5, s.out_acc.at[o], s.cross.at[1]).start()
            step(1)
        else:
            step(2)

    feed(3, start_reduction)

    core_copy(4, s.bn_acc.at[o], s.cross.at[0]).wait_recv()

    def middle_back(i, carry):
        rows = pl.ds(pl.multiple_of(i * 128, 128), 128)
        unit, rate = centre(s.middle[rows])
        upstream = s.bn_acc[r, rows] + s.cross[0, rows]
        cot = s.c_all[r, rows].astype(F32)
        back = cot + norm_back(unit, rate, vec_row(5), upstream)
        s.bn_acc[r, rows] = back
        branch = back.astype(BF)
        s.wide[rows] = branch
        gain_t, shift_t, out_t, red_t = carry
        return (
            gain_t + jnp.sum(upstream * unit, axis=0, keepdims=True),
            shift_t + jnp.sum(upstream, axis=0, keepdims=True),
            out_t + jnp.sum(branch.astype(F32), axis=0, keepdims=True),
            red_t + jnp.sum(cot, axis=0, keepdims=True),
        )

    zero_row = jnp.zeros((1, 1024), F32)
    gain_t, shift_t, out_t, red_t = lax.fori_loop(0, 3, middle_back, (zero_row,) * 4)
    s.gvec[5:6] = gain_t
    s.gvec[6:7] = shift_t
    s.gvec[4:5] = out_t
    s.gvec[7:8] = red_t

    core_copy(0, s.half.at[o], s.half.at[o]).wait_send()
    core_copy(2, s.wout.at[:, :, :, r], s.wout.at[:, :, :, r]).wait_send()

    def back_att(n, carry):
        weight = s.wout[n].reshape(256, 1024)
        cols = pl.ds(pl.multiple_of((n % 2) * 256, 256), 256)
        s.half[n // 2, :, cols] = dot_nt(s.wide[...], weight).astype(BF)
        return carry

    lax.fori_loop(0, 4, back_att, 0)
    core_copy(6, s.half.at[o], s.ba_all.at[r]).start()
    s.ba_all[r] = s.half[r]
    step(3)
    sent(i_out)

    def grad_out(n, carry):
        cols = pl.ds(pl.multiple_of(n * 256, 256), 256)
        grad = dot(s.att_t[...], s.wide[:, cols]).astype(BF)
        s.wout[:, :, :, :, :, cols] = grad.reshape(4, 2, 2, 2, 32, 256)
        return carry

    lax.fori_loop(0, 4, grad_out, 0)
    core_copy(7, s.wout.at[:, :, :, o], s.outx).start()
    core_copy(5, s.out_acc.at[o], s.cross.at[1]).wait_recv()

    def result_tile(i, carry):
        rows = pl.ds(pl.multiple_of(i * 128, 128), 128)
        total = s.middle[rows] + s.out_acc[r, rows] + s.cross[1, rows] + vec_row(7)
        result_ref[rows] = total.astype(BF)
        return carry

    lax.fori_loop(0, 3, result_tile, 0)
    core_copy(6, s.ba_all.at[o], s.ba_all.at[o]).wait_recv()

    def attend_back(hp, carry):
        k_t = flip(s.qkv[1, hp])
        dims = pl.ds(pl.multiple_of(hp * 128, 128), 128)
        s.dkv[...] = jnp.zeros_like(s.dkv)
        for rb in range(6):
            keys = key_count(rb)
            rows = slice(rb * 128, (rb + 1) * 128)
            both = pair_rows(s.qkv[0, hp, rows])
            at = (rb % 3) * 128
            up = pair_rows(s.ba_all[rb // 3, at : at + 128, dims])
            scores = dot_nt(s.qkv[1, hp, 0:keys], both) * factor + pair_mask(keys, rb)
            probs = jnp.exp2(scores - s.lse[hp, rb, 0:1])
            back_probs = dot_nt(s.qkv[2, hp, 0:keys], up)
            weighted = probs * back_probs
            centre_row = jnp.sum(weighted, axis=0, keepdims=True)
            back_scores = (weighted - probs * centre_row).astype(BF)
            s.dkv[1, 0:keys] += dot(probs.astype(BF), up)
            s.dkv[0, 0:keys] += dot(back_scores, both)
            query = dot(k_t[:, 0:keys], back_scores)
            query = jnp.concatenate([query[0:64, 0:128], query[64:128, 128:256]], axis=0)
            s.ffb[0, rows, dims] = (query.T * HD**-0.5).astype(BF)
        s.ffb[1, :, dims] = (s.dkv[0] * HD**-0.5).astype(BF)
        s.ffb[2, :, dims] = s.dkv[1].astype(BF)
        return carry

    core_copy(7, s.outx, s.outx).wait_recv()

    def add_out(i, carry):
        for yy in range(2):
            for xx in range(2):
                total = s.wout[i, yy, xx, r].astype(F32) + s.outx[i, yy, xx].astype(F32)
                s.wout[i, yy, xx, r] = total.astype(BF)
        return carry

    lax.fori_loop(0, 4, add_out, 0)

    lax.fori_loop(0, 1, attend_back, 0)
    step(4)
    lax.fori_loop(1, 3, attend_back, 0)
    step(5)
    lax.fori_loop(3, 4, attend_back, 0)

    core_copy(5, s.out_acc.at[o], s.cross.at[1]).wait_send()

    def back_in(n, carry):
        cols = pl.ds(pl.multiple_of(n * 256, 256), 256)
        total = dot_nt(s.ffb[0, :, 0:256], s.win[0, n].reshape(256, 256))
        for part in range(1, 6):
            at = (part % 2) * 256
            total = total + dot_nt(s.ffb[part // 2, :, at : at + 256], s.win[part, n].reshape(256, 256))
        s.out_acc[:, :, cols] = total.reshape(2, 384, 256)
        return carry

    lax.fori_loop(0, 4, back_in, 0)
    core_copy(8, s.out_acc.at[o], s.cross.at[0]).start()
    step(6)
    for part in range(6):
        sent(i_w[part])
        at = (part % 2) * 256
        grad = dot(s.n1t[...], s.ffb[part // 2, :, at : at + 256]).astype(BF)
        s.win[part] = grad.reshape(4, 2, 2, 64, 256)
        if part == 2:
            step(7)
    step(8)
    step(9)

    core_copy(8, s.out_acc.at[o], s.cross.at[0]).wait_recv()

    def frame_back(i, carry):
        rows = pl.ds(pl.multiple_of(i * 128, 128), 128)
        unit, rate = centre(s.frames_all[r, rows].astype(F32))
        upstream = s.out_acc[r, rows] + s.cross[0, rows]
        back = s.bn_acc[r, rows] + norm_back(unit, rate, vec_row(0), upstream)
        fgrad_ref[rows] = back.astype(BF)
        gain_t, shift_t = carry
        return (
            gain_t + jnp.sum(upstream * unit, axis=0, keepdims=True),
            shift_t + jnp.sum(upstream, axis=0, keepdims=True),
        )

    gain_t, shift_t = lax.fori_loop(0, 3, frame_back, (zero_row,) * 2)
    s.gvec[0:1] = gain_t
    s.gvec[1:2] = shift_t
    s.gvec[2:4] = jnp.zeros((2, 1024), F32)
    s.gvec[2:3, my_half] = jnp.sum(s.ffb[0].astype(F32), axis=0, keepdims=True)
    s.gvec[3:4, my_half] = jnp.sum(s.ffb[2].astype(F32), axis=0, keepdims=True)
    s.sg[...] = jnp.zeros_like(s.sg)
    for zz in range(4):
        for yy in range(2):
            for xx in range(2):
                at = (zz * 2 + yy) * 128
                s.sg[zz, yy, xx, 0:8] = s.gvec[:, at : at + 128]
                at = (yy * 2 + xx) * 128
                s.sg[zz, yy, xx, 8:9] = s.gexp[zz, 0:1, at : at + 128]

    for i in range(10, len(order) + 4):
        step(i)

    for item in pre:
        item.wait_send()
    sent(i_small)
    core_copy(1, s.half_t.at[o], s.half_t.at[o]).wait_send()
    core_copy(3, s.n_all.at[r], s.n_all.at[r]).wait_send()
    core_copy(4, s.bn_acc.at[o], s.cross.at[0]).wait_send()
    core_copy(6, s.half.at[o], s.ba_all.at[r]).wait_send()
    core_copy(7, s.wout.at[:, :, :, o], s.outx).wait_send()
    core_copy(8, s.out_acc.at[o], s.cross.at[0]).wait_send()
    for it in order:
        all_sent(it)


def hand_on(*refs):
    given, taken, held = refs[0:6], refs[6:12], refs[12:18]
    sems = refs[18]
    inward = [pltpu.make_async_copy(given[i], held[i], sems.at[0, i]) for i in range(6)]
    outward = [pltpu.make_async_copy(held[i], taken[i], sems.at[1, i]) for i in range(6)]
    for item in inward:
        item.start()
    for i in range(6):
        inward[i].wait()
        outward[i].start()
    for item in outward:
        item.wait()


def fused_shards(
    frames, frames_cotangent, phoneme_len, prompt_len, target_segment, first_gain, first_shift, inward_weight,
    query_bias, value_bias, outward_weight, outward_bias, second_gain, second_shift, expand_weight, expand_bias,
    reduce_weight, reduce_bias,
):
    number = lax.axis_index("dp") * 2 + lax.axis_index("role")
    quarter = number % 4
    rows = jnp.stack(
        [first_gain, first_shift, query_bias, value_bias, outward_bias, second_gain, second_shift, reduce_bias]
    )
    lane = jnp.arange(128) // 32
    rows = jnp.where(lane[None] == quarter, jnp.tile(rows, (1, 4)), jnp.zeros((), BF))
    small = jnp.concatenate([rows, expand_bias[None], jnp.zeros((7, 128), BF)], axis=0)

    scratch = scratch_list()
    vmem = pl.BlockSpec(memory_space=pltpu.VMEM)
    smem = pl.BlockSpec(memory_space=pltpu.SMEM)
    hbm = pl.BlockSpec(memory_space=pl.ANY)
    outs = pl.pallas_call(
        functools.partial(layer_kernel, tuple(scratch)),
        out_shape=[
            jax.ShapeDtypeStruct((384, 1024), BF),
            jax.ShapeDtypeStruct((384, 1024), BF),
            jax.ShapeDtypeStruct((32, 3072), F32),
            jax.ShapeDtypeStruct((32, 1024), F32),
            jax.ShapeDtypeStruct((32, 4096), F32),
            jax.ShapeDtypeStruct((128, 1024), F32),
            jax.ShapeDtypeStruct((16, 128), F32),
        ],
        in_specs=[smem, smem, vmem, hbm, hbm] + [vmem] * 5,
        out_specs=[vmem] * 7,
        scratch_shapes=list(scratch.values()),
        compiler_params=pltpu.CompilerParams(
            collective_id=0, has_side_effects=True, vmem_limit_bytes=62 * 1024 * 1024
        ),
    )(
        phoneme_len, prompt_len, target_segment, frames[0], frames_cotangent[0], small, inward_weight,
        outward_weight, expand_weight, reduce_weight,
    )
    d_small = outs[6]
    result, frames_gradient, d_in, d_out, d_exp, d_red = pl.pallas_call(
        hand_on,
        out_shape=[jax.ShapeDtypeStruct(item.shape, item.dtype) for item in outs[:6]],
        in_specs=[hbm] * 6,
        out_specs=[hbm] * 6,
        scratch_shapes=[pltpu.VMEM(item.shape, item.dtype) for item in outs[:6]]
        + [pltpu.SemaphoreType.DMA((2, 6))],
    )(*outs[:6])
    mine = lax.dynamic_slice(d_small, (0, quarter * 32), (8, 32))
    return (
        result[None], frames_gradient[None], mine[0], mine[1], d_in, mine[2], mine[3], d_out, mine[4], mine[5],
        mine[6], d_exp, d_small[8], d_red, mine[7],
    )


def passed_along(block, axis, distance):
    devices = range(lax.axis_size(axis))
    route = [(i - distance, i) for i in devices if i - distance in devices]
    return lax.ppermute(block, axis, route)


def normalize(values, gain, shift):
    mean_value = jnp.mean(values, axis=-1, keepdims=True)
    centered = values - mean_value
    spread = jnp.mean(centered * centered, axis=-1, keepdims=True)
    return centered * lax.rsqrt(spread + EPS) * gain + shift


def smooth_gate(values):
    return jax.nn.gelu(values, approximate=False)


def inner_rows(left, right):
    return lax.dot_general(
        left, right, (((0,), (0,)), ((), ())), preferred_element_type=jnp.float32
    )


def outer_cols(left, right):
    return lax.dot_general(
        left, right, (((1,), (1,)), ((), ())), preferred_element_type=jnp.float32
    )


def plain_shards(
    frames,
    frames_cotangent,
    phoneme_len,
    prompt_len,
    target_segment,
    first_gain,
    first_shift,
    inward_weight,
    query_bias,
    value_bias,
    outward_weight,
    outward_bias,
    second_gain,
    second_shift,
    expand_weight,
    expand_bias,
    reduce_weight,
    reduce_bias,
):
    attention_part = (
        lax.all_gather(first_gain, ("dp", "role"), axis=0, tiled=True),
        lax.all_gather(first_shift, ("dp", "role"), axis=0, tiled=True),
        lax.all_gather(inward_weight, ("dp", "role"), axis=0, tiled=True),
        lax.all_gather(query_bias, ("dp", "role"), axis=0, tiled=True),
        lax.all_gather(value_bias, ("dp", "role"), axis=0, tiled=True),
        lax.all_gather(outward_weight, ("dp", "role"), axis=0, tiled=True),
        lax.all_gather(outward_bias, ("dp", "role"), axis=0, tiled=True),
    )
    (
        full_gain,
        full_shift,
        full_inward,
        full_query_bias,
        full_value_bias,
        full_outward,
        full_outward_bias,
    ) = attention_part
    side = lax.axis_index("role")
    local_rows = frames.shape[1]
    scale = HD ** (-0.5)
    current = frames[0].astype(jnp.float32)
    normed = normalize(
        current, full_gain.astype(jnp.float32), full_shift.astype(jnp.float32)
    ).astype(jnp.bfloat16)
    mixed = jnp.dot(normed, full_inward, preferred_element_type=jnp.float32)
    queries = (mixed[:, :D] + full_query_bias.astype(jnp.float32)).astype(jnp.bfloat16)
    keys_own = mixed[:, D : 2 * D].astype(jnp.bfloat16)
    values_own = (mixed[:, 2 * D :] + full_value_bias.astype(jnp.float32)).astype(jnp.bfloat16)
    remote_keys, remote_values = passed_along((keys_own, values_own), "role", 1)
    keys_all = jnp.concatenate([remote_keys, keys_own], axis=0)
    values_all = jnp.concatenate([remote_values, values_own], axis=0)
    row_index = jnp.arange(local_rows)[:, None]
    col_index = jnp.arange(2 * local_rows)[None, :]
    own_col = col_index - local_rows
    prefix_length = phoneme_len[0] + prompt_len[0]
    segment = target_segment[0]
    key_segment = jnp.concatenate([jnp.full((local_rows,), -1, jnp.int32), segment])
    prompt_rows = (own_col >= 0) & (own_col <= row_index) & (own_col < prefix_length)
    target_rows = (col_index < prefix_length) | (own_col >= 0) & (own_col <= row_index) & (
        key_segment[None, :] == segment[:, None]
    )
    allowed = jnp.where(side == 0, prompt_rows, target_rows)

    def attend(index):
        start = index * HD
        head_query = lax.dynamic_slice_in_dim(queries, start, HD, 1)
        head_key = lax.dynamic_slice_in_dim(keys_all, start, HD, 1)
        head_value = lax.dynamic_slice_in_dim(values_all, start, HD, 1)
        scores = outer_cols(head_query, head_key) * scale
        masked = jnp.where(allowed, scores, MASKED)
        peak = jnp.max(masked, axis=1, keepdims=True)
        expo = jnp.exp(masked - peak)
        total = jnp.sum(expo, axis=1, keepdims=True)
        probs = (expo / total).astype(jnp.bfloat16)
        return (
            jnp.dot(probs, head_value, preferred_element_type=jnp.float32),
            (peak + jnp.log(total))[:, 0],
        )

    head_outs, log_totals = lax.map(attend, jnp.arange(H))
    attended = head_outs.transpose(1, 0, 2).reshape(local_rows, D).astype(jnp.bfloat16)
    middle = (
        current
        + jnp.dot(attended, full_outward, preferred_element_type=jnp.float32)
        + full_outward_bias.astype(jnp.float32)
    )
    feed_part = (
        lax.all_gather(second_gain, ("dp", "role"), axis=0, tiled=True),
        lax.all_gather(second_shift, ("dp", "role"), axis=0, tiled=True),
        lax.all_gather(expand_weight, ("dp", "role"), axis=0, tiled=True),
        lax.all_gather(expand_bias, ("dp", "role"), axis=0, tiled=True),
        lax.all_gather(reduce_weight, ("dp", "role"), axis=0, tiled=True),
        lax.all_gather(reduce_bias, ("dp", "role"), axis=0, tiled=True),
    )
    full_gain_two, full_shift_two, full_expand, full_expand_bias, full_reduce, full_reduce_bias = (
        feed_part
    )
    gain_two = full_gain_two.astype(jnp.float32)
    shift_two = full_shift_two.astype(jnp.float32)
    normed_two = normalize(middle, gain_two, shift_two).astype(jnp.bfloat16)
    inner = jnp.dot(
        normed_two, full_expand, preferred_element_type=jnp.float32
    ) + full_expand_bias.astype(jnp.float32)
    active = smooth_gate(inner).astype(jnp.bfloat16)
    output = (
        middle
        + jnp.dot(active, full_reduce, preferred_element_type=jnp.float32)
        + full_reduce_bias.astype(jnp.float32)
    )
    result = output.astype(jnp.bfloat16)[None]
    again_expand = feed_part[2]
    again_reduce = feed_part[4]
    again_gain = attention_part[0].astype(jnp.float32)
    again_shift = attention_part[1].astype(jnp.float32)
    again_inward = attention_part[2]
    again_outward = attention_part[5]
    upstream = frames_cotangent[0]
    upstream_float = upstream.astype(jnp.float32)
    reduce_bias_term = jnp.sum(upstream_float, axis=0)
    reduce_weight_term = inner_rows(active, upstream)
    back_active = outer_cols(upstream, again_reduce)
    gate_pull = jax.vjp(smooth_gate, inner)[1]
    back_inner = gate_pull(back_active)[0].astype(jnp.bfloat16)
    expand_bias_term = jnp.sum(back_inner.astype(jnp.float32), axis=0)
    expand_weight_term = inner_rows(normed_two, back_inner)
    back_normed_two = outer_cols(back_inner, again_expand)
    second_pull = jax.vjp(normalize, middle, gain_two, shift_two)[1]
    middle_part, second_gain_term, second_shift_term = second_pull(back_normed_two)
    back_middle = upstream_float + middle_part
    back_branch = back_middle.astype(jnp.bfloat16)
    outward_bias_term = jnp.sum(back_branch.astype(jnp.float32), axis=0)
    outward_weight_term = inner_rows(attended, back_branch)
    back_attended = outer_cols(back_branch, again_outward).astype(jnp.bfloat16)

    def attend_back(inputs):
        index, log_total = inputs
        start = index * HD
        head_query = lax.dynamic_slice_in_dim(queries, start, HD, 1)
        head_key = lax.dynamic_slice_in_dim(keys_all, start, HD, 1)
        head_value = lax.dynamic_slice_in_dim(values_all, start, HD, 1)
        head_upstream = lax.dynamic_slice_in_dim(back_attended, start, HD, 1)
        scores = outer_cols(head_query, head_key) * scale
        probs = jnp.where(allowed, jnp.exp(scores - log_total[:, None]), 0.0)
        back_probs = outer_cols(head_upstream, head_value)
        centre = jnp.sum(probs * back_probs, axis=1, keepdims=True)
        back_scores = (probs * (back_probs - centre)).astype(jnp.bfloat16)
        back_query = jnp.dot(back_scores, head_key, preferred_element_type=jnp.float32) * scale
        back_key = inner_rows(back_scores, head_query) * scale
        back_value = inner_rows(probs.astype(jnp.bfloat16), head_upstream)
        return (back_query, back_key, back_value)

    head_query_grads, head_key_grads, head_value_grads = lax.map(
        attend_back, (jnp.arange(H), log_totals)
    )
    back_queries = head_query_grads.transpose(1, 0, 2).reshape(local_rows, D)
    back_keys_all = head_key_grads.transpose(1, 0, 2).reshape(2 * local_rows, D)
    back_values_all = head_value_grads.transpose(1, 0, 2).reshape(2 * local_rows, D)
    returned_keys, returned_values = (
        passed_along(back_keys_all[:local_rows].astype(jnp.bfloat16), "role", -1).astype(
            jnp.float32
        ),
        passed_along(back_values_all[:local_rows].astype(jnp.bfloat16), "role", -1).astype(
            jnp.float32
        ),
    )
    query_low = back_queries.astype(jnp.bfloat16)
    key_low = (back_keys_all[local_rows:] + returned_keys).astype(jnp.bfloat16)
    value_low = (back_values_all[local_rows:] + returned_values).astype(jnp.bfloat16)
    back_mixed = jnp.concatenate([query_low, key_low, value_low], axis=1)
    query_bias_term = jnp.sum(query_low.astype(jnp.float32), axis=0)
    value_bias_term = jnp.sum(value_low.astype(jnp.float32), axis=0)
    inward_weight_term = inner_rows(normed, back_mixed)
    back_normed = outer_cols(back_mixed, again_inward)
    first_pull = jax.vjp(normalize, current, again_gain, again_shift)[1]
    frame_part, first_gain_term, first_shift_term = first_pull(back_normed)
    frames_gradient = (back_middle + frame_part).astype(jnp.bfloat16)[None]
    totals = (
        lax.psum_scatter(first_gain_term, ("dp", "role"), scatter_dimension=0, tiled=True),
        lax.psum_scatter(first_shift_term, ("dp", "role"), scatter_dimension=0, tiled=True),
        lax.psum_scatter(inward_weight_term, ("dp", "role"), scatter_dimension=0, tiled=True),
        lax.psum_scatter(query_bias_term, ("dp", "role"), scatter_dimension=0, tiled=True),
        lax.psum_scatter(value_bias_term, ("dp", "role"), scatter_dimension=0, tiled=True),
        lax.psum_scatter(outward_weight_term, ("dp", "role"), scatter_dimension=0, tiled=True),
        lax.psum_scatter(outward_bias_term, ("dp", "role"), scatter_dimension=0, tiled=True),
        lax.psum_scatter(second_gain_term, ("dp", "role"), scatter_dimension=0, tiled=True),
        lax.psum_scatter(second_shift_term, ("dp", "role"), scatter_dimension=0, tiled=True),
        lax.psum_scatter(expand_weight_term, ("dp", "role"), scatter_dimension=0, tiled=True),
        lax.psum_scatter(expand_bias_term, ("dp", "role"), scatter_dimension=0, tiled=True),
        lax.psum_scatter(reduce_weight_term, ("dp", "role"), scatter_dimension=0, tiled=True),
        lax.psum_scatter(reduce_bias_term, ("dp", "role"), scatter_dimension=0, tiled=True),
    )
    return (
        result,
        frames_gradient,
        totals[0],
        totals[1],
        totals[2],
        totals[3],
        totals[4],
        totals[5],
        totals[6],
        totals[7],
        totals[8],
        totals[9],
        totals[10],
        totals[11],
        totals[12],
    )


def solution(mesh):
    placed = (
        P("dp", "role", None),
        P("dp", "role", None),
        P("dp"),
        P("dp"),
        P("dp", None),
        P(("dp", "role")),
        P(("dp", "role")),
        P(("dp", "role"), None),
        P(("dp", "role")),
        P(("dp", "role")),
        P(("dp", "role"), None),
        P(("dp", "role")),
        P(("dp", "role")),
        P(("dp", "role")),
        P(("dp", "role"), None),
        P(("dp", "role")),
        P(("dp", "role"), None),
        P(("dp", "role")),
    )
    fused = mesh.shape["dp"] == 16 and mesh.shape["role"] == 2
    return jax.shard_map(
        fused_shards if fused else plain_shards,
        mesh=mesh,
        in_specs=placed,
        out_specs=(
            P("dp", "role", None),
            P("dp", "role", None),
            P(("dp", "role")),
            P(("dp", "role")),
            P(("dp", "role"), None),
            P(("dp", "role")),
            P(("dp", "role")),
            P(("dp", "role"), None),
            P(("dp", "role")),
            P(("dp", "role")),
            P(("dp", "role")),
            P(("dp", "role"), None),
            P(("dp", "role")),
            P(("dp", "role"), None),
            P(("dp", "role")),
        ),
        check_vma=False,
    )
```

```python
import functools

import jax
import jax.numpy as jnp
from jax import lax
from jax.experimental import pallas as pl
from jax.experimental.pallas import tpu as pltpu
from jax.sharding import PartitionSpec as P

D = 1024
H = 16
HD = 64
EPS = 1e-05
MASKED = -1e30
LOG2E = 1.4426950408889634
BF = jnp.bfloat16
F32 = jnp.float32
MESH = pl.DeviceIdType.MESH


def dot(left, right):
    return lax.dot_general(left, right, (((1,), (0,)), ((), ())), preferred_element_type=F32)


def dot_nt(left, right):
    return lax.dot_general(left, right, (((1,), (1,)), ((), ())), preferred_element_type=F32)


def flip(value):
    return value.astype(F32).T.astype(value.dtype)


def centre(values):
    mean_value = jnp.mean(values, axis=-1, keepdims=True)
    centered = values - mean_value
    spread = jnp.mean(centered * centered, axis=-1, keepdims=True)
    return centered * lax.rsqrt(spread + EPS), lax.rsqrt(spread + EPS)


def norm_back(unit, rate, gain, upstream):
    pulled = upstream * gain
    first = jnp.mean(pulled, axis=-1, keepdims=True)
    second = jnp.mean(pulled * unit, axis=-1, keepdims=True)
    return rate * (pulled - first - unit * second)


LEAD = 1
LOOK = 2
RED_SPLIT = (0, 0, 0, 0)


def scratch_list():
    dma = pltpu.SemaphoreType.DMA
    v = pltpu.VMEM
    return dict(
        small=v((4, 2, 2, 2, 16, 128), BF),
        vec=v((8, 1024), F32),
        ebias=v((4, 8, 512), F32),
        frames_all=v((2, 384, 1024), BF),
        c_all=v((2, 384, 1024), BF),
        n_all=v((2, 384, 1024), BF),
        n1t=v((1024, 768), BF),
        n2t=v((1024, 768), BF),
        win=v((6, 4, 2, 2, 64, 256), BF),
        wout=v((4, 2, 2, 2, 32, 1024), BF),
        wexp=v((4, 4, 2, 2, 64, 512), BF),
        wred=v((4, 4, 4, 32, 1024), BF),
        qkv=v((3, 4, 768, 128), BF),
        mask=v((768, 768), BF),
        lse=v((4, 6, 8, 256), F32),
        half=v((2, 384, 512), BF),
        half_t=v((2, 512, 384), BF),
        wide=v((384, 1024), BF),
        att_t=v((1024, 384), BF),
        middle=v((384, 1024), F32),
        out_acc=v((2, 384, 1024), F32),
        bn_acc=v((2, 384, 1024), F32),
        cross=v((384, 1024), F32),
        ffb=v((3, 768, 512), BF),
        act_t=v((512, 768), BF),
        ba_all=v((2, 384, 512), BF),
        dkv=v((2, 768, 128), F32),
        gvec=v((8, 1024), F32),
        gexp=v((4, 8, 512), F32),
        outx=v((4, 2, 2, 32, 1024), BF),
        rb=v((4, 2, 4, 64, 512), BF),
        ra=v((4, 64, 512), BF),
        rz=v((4, 6, 64, 512), BF),
        rx=v((4, 2, 64, 512), BF),
        ra_in=v((6, 4, 64, 256), BF),
        rz_in=v((6, 3, 64, 256), BF),
        rb_red=v((4, 2, 4, 32, 1024), BF),
        land=v((4, 7, 32, 1024), BF),
        rb_out=v((2, 4, 32, 1024), BF),
        ra_out=v((4, 32, 1024), BF),
        rz_out=v((3, 32, 1024), BF),
        sg=v((4, 2, 2, 16, 128), F32),
        rb_sg=v((2, 4, 16, 128), F32),
        ra_sg=v((4, 16, 128), F32),
        rz_sg=v((3, 16, 128), F32),
        fin=v((4, 64, 512), F32),
        fin_in=v((4, 32, 512), F32),
        fin_w=v((6, 64, 256), F32),
        fin_w_in=v((6, 32, 256), F32),
        sfin=v((16, 128), F32),
        sfin_in=v((16, 128), F32),
        own_s=dma((2,)),
        pre_s=dma((13,)),
        pre_r=dma((13,)),
        agz_s=dma((16, 3)),
        agz_r=dma((16, 3)),
        agy_s=dma((16, 3)),
        agy_r=dma((16, 3)),
        agx_s=dma((16, 2)),
        aga_s=dma((16,)),
        aga_r=dma((16,)),
        agb_s=dma((16, 2)),
        agb_r=dma((16, 2)),
        core_s=dma((9,)),
        core_r=dma((9,)),
        rsb_s=dma((16, 2)),
        rsb_r=dma((16, 2)),
        rsa_s=dma((16,)),
        rsa_r=dma((16,)),
        rsz_s=dma((16, 3)),
        rsz_r=dma((16, 3)),
        rsy_s=dma((16, 3)),
        rsy_r=dma((16, 3)),
        rsx_s=dma((16, 2)),
        rsx_r=dma((16, 2)),
        fin_s=dma((11,)),
        fin_r=dma((11,)),
    )


class Bag:
    def __init__(self, **kw):
        self.__dict__.update(kw)


N_IN = 10
N_OUT = 7


def layer_kernel(names, *refs):
    (phon_ref, prom_ref, seg_ref, frames_ref, cot_ref, small_in, win_in, wout_in, wexp_in, wred_in) = refs[:N_IN]
    (result_ref, fgrad_ref, dwin_ref, dwout_ref, dwexp_ref, dwred_ref, dsmall_ref) = refs[N_IN : N_IN + N_OUT]
    s = Bag(**dict(zip(names, refs[N_IN + N_OUT :])))

    dp = lax.axis_index("dp")
    r = lax.axis_index("role")
    o = 1 - r
    z, y, x = dp // 4, (dp // 2) % 2, dp % 2
    ya, xa = y + r * (1 - 2 * y), x + (1 - r) * (1 - 2 * x)
    yb, xb = y + (1 - r) * (1 - 2 * y), x + r * (1 - 2 * x)
    yc, xc = 1 - y, 1 - x
    core_dev = (dp, o)
    a_dev = (z * 4 + ya * 2 + xa, r)
    b_dev = (z * 4 + yb * 2 + xb, r)
    z_dev = [(((z + k) % 4) * 4 + y * 2 + x, r) for k in (1, 2, 3)]
    z_at = [(z + k) % 4 for k in (1, 2, 3)]
    z_from = [(z + 4 - k) % 4 for k in (1, 2, 3)]
    at_end = (z == 0) | (z == 3)
    in_middle = (z == 1) | (z == 2)
    far = z_from[1]
    far_end = (jnp.where(z == 2, 3, 0) * 4 + y * 2 + x, r)
    near_middle = (jnp.where(z == 0, 1, 2) * 4 + y * 2 + x, r)
    place = 2 * y + x

    def copy(src, dst, ss, rs, dev):
        return pltpu.make_async_remote_copy(
            src_ref=src, dst_ref=dst, send_sem=ss, recv_sem=rs, device_id=dev, device_id_type=MESH
        )

    barrier = pltpu.get_barrier_semaphore()
    for dev in z_dev + [a_dev, b_dev, core_dev]:
        pl.semaphore_signal(barrier, inc=1, device_id=dev, device_id_type=MESH)
    pl.semaphore_wait(barrier, 6)

    my_rows = pl.ds(pl.multiple_of(r * 32, 32), 32)
    o_rows = pl.ds(pl.multiple_of(o * 32, 32), 32)

    def part_cols(part, who):
        return pl.ds(pl.multiple_of((part // 2) * 1024 + who * 512 + (part % 2) * 256, 256), 256)

    group_32 = lax.broadcasted_iota(jnp.int32, (32, 128), 1) // 32

    def pick(parts, group):
        picked = parts[3]
        for g in range(3):
            picked = jnp.where(group == g, parts[g], picked)
        return picked

    for who in range(2):
        for block in range(4):
            source = [
                wexp_in[:, (2 * (4 * block + q) + who) * 128 : (2 * (4 * block + q) + who + 1) * 128].astype(F32)
                for q in range(4)
            ]
            for j in range(4):
                chosen = pick([source[(g + j) % 4] for g in range(4)], group_32)
                s.half[who, j * 32 : (j + 1) * 32, block * 128 : (block + 1) * 128] = chosen.astype(BF)
    pre = []
    pre.append(copy(small_in, s.small.at[z, y, x, r], s.pre_s.at[0], s.pre_r.at[0], core_dev))
    for i in range(6):
        pre.append(
            copy(
                win_in.at[:, part_cols(i, o)],
                s.win.at[i, z, y, x, my_rows],
                s.pre_s.at[1 + i],
                s.pre_r.at[1 + i],
                core_dev,
            )
        )
    pre.append(copy(frames_ref, s.frames_all.at[r], s.pre_s.at[7], s.pre_r.at[7], core_dev))
    for j in range(4):
        pre.append(
            copy(
                s.half.at[o, j * 32 : (j + 1) * 32],
                s.wexp.at[j, z, y, x, my_rows],
                s.pre_s.at[8 + j],
                s.pre_r.at[8 + j],
                core_dev,
            )
        )
    pre.append(copy(cot_ref, s.c_all.at[r], s.pre_s.at[12], s.pre_r.at[12], core_dev))
    for item in pre:
        item.start()
    own_frames = pltpu.make_async_copy(frames_ref, s.frames_all.at[r], s.own_s.at[0])
    own_cot = pltpu.make_async_copy(cot_ref, s.c_all.at[r], s.own_s.at[1])
    own_frames.start()
    own_cot.start()
    s.small[z, y, x, r] = small_in[...]
    for i in range(6):
        s.win[i, z, y, x, my_rows] = win_in[:, part_cols(i, r)]
    s.wout[z, y, x, r] = wout_in[...]
    for j in range(4):
        group = (place + 4 - j) % 4
        s.wred[j, z, group] = wred_in[pl.ds(pl.multiple_of(group * 32, 32), 32)]
    for j in range(4):
        s.wexp[j, z, y, x, my_rows] = s.half[r, j * 32 : (j + 1) * 32]

    def ag_item(t, piece, col, split):
        return Bag(t=t, piece=piece, col=col, split=split)

    def slot(j, b, c):
        return (2 * b + c + 4 - j) % 4

    gathers = [ag_item(0, lambda a, b, c: s.small.at[a, b, c], lambda b, c: s.small.at[:, b, c], False)]
    for i in range(6):
        gathers.append(
            ag_item(
                1 + i, lambda a, b, c, i=i: s.win.at[i, a, b, c], lambda b, c, i=i: s.win.at[i, :, b, c], False
            )
        )
    gathers.append(ag_item(7, lambda a, b, c: s.wout.at[a, b, c, r], lambda b, c: s.wout.at[:, b, c, r], False))
    for j in range(4):
        gathers.append(
            ag_item(
                8 + 2 * j, lambda a, b, c, j=j: s.wexp.at[j, a, b, c], lambda b, c, j=j: s.wexp.at[j, :, b, c], True
            )
        )
        gathers.append(
            ag_item(
                9 + 2 * j,
                lambda a, b, c, j=j: s.wred.at[j, a, slot(j, b, c)],
                lambda b, c, j=j: s.wred.at[j, :, slot(j, b, c)],
                bool(RED_SPLIT[j]),
            )
        )

    def when(cond, go):
        if isinstance(cond, bool):
            if cond:
                go()
        else:
            pl.when(cond)(go)

    def z_copies(it, yy, xx, ss, rs):
        p = it.piece(z, yy, xx)
        return [copy(p, p, ss.at[it.t, k], rs.at[it.t, k], z_dev[k]) for k in range(3)]

    def straight(it, k):
        if not it.split or k == 1:
            return True
        return z != 3 if k == 0 else z != 0

    def z_start(it, yy, xx, ss, rs):
        for k, c in enumerate(z_copies(it, yy, xx, ss, rs)):
            when(straight(it, k), c.start)

    def z_relay(it, yy, xx, rs, which):
        p = it.piece(far, yy, xx)

        @pl.when(in_middle)
        def _():
            copy(p, p, s.agx_s.at[it.t, which], rs.at[it.t, 1], far_end).wait_recv()
            copy(p, p, s.agx_s.at[it.t, which], rs.at[it.t, jnp.where(z == 2, 2, 0)], far_end).start()

    def z_wait(it, yy, xx, ss, rs):
        for k in range(3):
            p = it.piece(z_from[k], yy, xx)
            c = copy(p, p, ss.at[it.t, k], rs.at[it.t, k], z_dev[k])
            when(at_end if it.split and k == 1 else True, c.wait_recv)

    def z_sent(it, yy, xx, ss, rs, which):
        for k, c in enumerate(z_copies(it, yy, xx, ss, rs)):
            when(straight(it, k), c.wait_send)
        if it.split:
            p = it.piece(far, yy, xx)
            pl.when(in_middle)(copy(p, p, s.agx_s.at[it.t, which], rs.at[it.t, 0], far_end).wait_send)

    def a_piece(it, yy, xx):
        p = it.piece(z, yy, xx)
        return copy(p, p, s.aga_s.at[it.t], s.aga_r.at[it.t], a_dev)

    def a_copy(it, yy, xx):
        return copy(it.col(yy, xx), it.col(yy, xx), s.aga_s.at[it.t], s.aga_r.at[it.t], a_dev)

    def b_copy(it, which, yy, xx):
        return copy(it.col(yy, xx), it.col(yy, xx), s.agb_s.at[it.t, which], s.agb_r.at[it.t, which], b_dev)

    def e0(it):
        if it.split:
            a_piece(it, y, x).start()
        z_start(it, y, x, s.agz_s, s.agz_r)

    def e1(it):
        if it.split:
            z_relay(it, y, x, s.agz_r, 0)
            a_piece(it, ya, xa).wait_recv()
            z_start(it, ya, xa, s.agy_s, s.agy_r)
            return
        z_wait(it, y, x, s.agz_s, s.agz_r)
        a_copy(it, y, x).start()
        b_copy(it, 0, y, x).start()

    def e2(it):
        if it.split:
            z_relay(it, ya, xa, s.agy_r, 1)
            z_wait(it, y, x, s.agz_s, s.agz_r)
            b_copy(it, 0, y, x).start()
            z_wait(it, ya, xa, s.agy_s, s.agy_r)
            b_copy(it, 1, ya, xa).start()
            return
        a_copy(it, ya, xa).wait_recv()
        b_copy(it, 1, ya, xa).start()

    def e3(it):
        b_copy(it, 0, yb, xb).wait_recv()
        b_copy(it, 1, yc, xc).wait_recv()

    def sent(it):
        z_sent(it, y, x, s.agz_s, s.agz_r, 0)
        if it.split:
            a_piece(it, y, x).wait_send()
            z_sent(it, ya, xa, s.agy_s, s.agy_r, 1)
        else:
            a_copy(it, y, x).wait_send()
        b_copy(it, 0, y, x).wait_send()
        b_copy(it, 1, ya, xa).wait_send()

    def pre_in(index, dst):
        copy(dst, dst, s.pre_s.at[index], s.pre_r.at[index], core_dev).wait_recv()

    def ready(i):
        if i == 0:
            pre_in(0, s.small.at[z, y, x, o])
        elif i < 7:
            pre_in(i, s.win.at[i - 1, z, y, x, o_rows])
        elif i >= 8 and i % 2 == 0:
            j = (i - 8) // 2
            pre_in(8 + j, s.wexp.at[j, z, y, x, o_rows])

    def gather(i):
        for event, lag in ((e0, 0), (e1, LOOK), (e2, 2 * LOOK), (e3, 3 * LOOK)):
            if 0 <= i - lag < len(gathers):
                if lag == 0:
                    ready(i)
                event(gathers[i - lag])

    for i in range(3):
        gather(i)

    for edge, k in ((0, 0), (3, 2)):

        @pl.when(z == edge)
        def _(k=k):
            for base in (0, 3):
                s.rz[:, base + k] = jnp.zeros((4, 64, 512), BF)
                for j in range(4):
                    if RED_SPLIT[j]:
                        s.land[j, 1 + base + k] = jnp.zeros((32, 1024), BF)

    own_frames.wait()
    own_cot.wait()
    prefix = phon_ref[0] + prom_ref[0]
    seg_row = seg_ref[...].astype(F32)
    seg_wide = jnp.broadcast_to(seg_row, (384, 384))
    seg_tall = seg_wide.T
    key_at = lax.broadcasted_iota(jnp.int32, (384, 384), 0)
    row_at = lax.broadcasted_iota(jnp.int32, (384, 384), 1)
    causal = key_at <= row_at
    seen = key_at < prefix

    def as_bias(allowed):
        return jnp.where(allowed, 0.0, MASKED).astype(BF)

    s.mask[0:384, 0:384] = as_bias(causal & seen)
    s.mask[0:384, 384:768] = as_bias(seen)
    s.mask[384:768, 384:768] = as_bias(causal & (seg_wide == seg_tall))

    for i in range(3, 3 * LOOK + 1):
        gather(i)

    def tile_sum(q):
        total = jnp.zeros((16, 128), F32)
        for xx in range(2):
            for who in range(2):
                total = total + s.small[q // 2, q % 2, xx, who].astype(F32)
        return total

    for q in range(8):
        s.vec[:, q * 128 : (q + 1) * 128] = tile_sum(q)[0:8]
    group_1 = lax.broadcasted_iota(jnp.int32, (1, 128), 1) // 32
    for block in range(4):
        tiles = [s.small[block, q // 2, q % 2, r].astype(F32)[8:9] for q in range(4)]
        for j in range(4):
            s.ebias[j, 0:1, block * 128 : (block + 1) * 128] = pick([tiles[(g + j) % 4] for g in range(4)], group_1)

    def vec_row(i):
        return s.vec[i : i + 1, :]

    pre_in(7, s.frames_all.at[o])

    def norm_tile(i, carry):
        who, rows = i // 3, pl.ds(pl.multiple_of((i % 3) * 128, 128), 128)
        unit, _ = centre(s.frames_all[who, rows].astype(F32))
        normed = unit * vec_row(0) + vec_row(1)
        s.n_all[who, rows] = normed.astype(BF)
        s.n1t[:, pl.ds(pl.multiple_of(i * 128, 128), 128)] = normed.T.astype(BF)
        return carry

    lax.fori_loop(0, 6, norm_tile, 0)

    def project(part):
        section, n = part // 2, part % 2
        mixed = dot(s.n_all[...].reshape(768, 1024), s.win[part].reshape(1024, 256))
        if section != 1:
            bias_at = pl.ds(pl.multiple_of(r * 512 + n * 256, 256), 256)
            bias_row = 2 if section == 0 else 3
            mixed = mixed + s.vec[bias_row : bias_row + 1, bias_at]
        mixed = mixed.astype(BF)
        s.qkv[section, 2 * n] = mixed[:, 0:128]
        s.qkv[section, 2 * n + 1] = mixed[:, 128:256]

    for part in range(6):
        gather(3 * LOOK + 1 + part)
        project(part)

    factor = HD**-0.5 * LOG2E
    low_lane = lax.broadcasted_iota(jnp.int32, (128, 128), 1) < 64

    def pair_rows(block):
        zero = jnp.zeros_like(block)
        return jnp.concatenate([jnp.where(low_lane, block, zero), jnp.where(low_lane, zero, block)], axis=0)

    def pair_mask(keys, rb):
        bias = s.mask[0:keys, rb * 128 : (rb + 1) * 128].astype(F32)
        return jnp.concatenate([bias, bias], axis=1)

    def key_count(rb):
        return (rb + 1) * 128 if rb < 3 else 384 + (rb - 2) * 128

    def attend(hp, carry):
        v_t = flip(s.qkv[2, hp])
        dims = pl.ds(pl.multiple_of(hp * 128, 128), 128)
        for rb in range(6):
            keys = key_count(rb)
            both = pair_rows(s.qkv[0, hp, rb * 128 : (rb + 1) * 128])
            scores = dot_nt(s.qkv[1, hp, 0:keys], both) * factor + pair_mask(keys, rb)
            peak = jnp.max(scores, axis=0, keepdims=True)
            expo = jnp.exp2(scores - peak)
            total = jnp.sum(expo, axis=0, keepdims=True)
            heads = dot(v_t[:, 0:keys], expo.astype(BF)) / total
            s.lse[hp, rb] = jnp.broadcast_to(peak + jnp.log2(total), (8, 256))
            out = jnp.concatenate([heads[0:64, 0:128], heads[64:128, 128:256]], axis=0)
            at = (rb % 3) * 128
            s.half_t[rb // 3, dims, at : at + 128] = out.astype(BF)
            s.half[rb // 3, at : at + 128, dims] = out.T.astype(BF)
        return carry

    for j in range(4):
        pre[8 + j].wait_send()
    lax.fori_loop(0, 4, attend, 0)

    my_half = pl.ds(pl.multiple_of(r * 512, 512), 512)
    o_half = pl.ds(pl.multiple_of(o * 512, 512), 512)

    def core_copy(index, src, dst):
        return copy(src, dst, s.core_s.at[index], s.core_r.at[index], core_dev)

    core_copy(0, s.half.at[o], s.wide.at[:, my_half]).start()
    core_copy(1, s.half_t.at[o], s.att_t.at[my_half]).start()
    s.wide[:, my_half] = s.half[r]
    s.att_t[my_half] = s.half_t[r]
    gather(3 * LOOK + 7)
    out_swap = core_copy(2, s.wout.at[:, :, :, r], s.wout.at[:, :, :, r])
    out_swap.start()
    core_copy(0, s.wide.at[:, o_half], s.wide.at[:, o_half]).wait_recv()
    core_copy(1, s.att_t.at[o_half], s.att_t.at[o_half]).wait_recv()
    core_copy(2, s.wout.at[:, :, :, o], s.wout.at[:, :, :, o]).wait_recv()
    def out_tile(n, carry):
        cols = pl.ds(pl.multiple_of(n * 256, 256), 256)
        branch = dot(s.wide[...], s.wout[:, :, :, :, :, cols].reshape(1024, 256))
        s.middle[:, cols] = s.frames_all[r, :, cols].astype(F32) + branch + s.vec[4:5, cols]
        return carry

    lax.fori_loop(0, 4, out_tile, 0)

    def norm_two(i, carry):
        rows = pl.ds(pl.multiple_of(i * 128, 128), 128)
        unit, _ = centre(s.middle[rows])
        s.n_all[r, rows] = (unit * vec_row(5) + vec_row(6)).astype(BF)
        return carry

    lax.fori_loop(0, 3, norm_two, 0)
    core_copy(3, s.n_all.at[r], s.n_all.at[r]).start()
    pre_in(12, s.c_all.at[o])
    s.out_acc[...] = jnp.zeros_like(s.out_acc)
    s.bn_acc[...] = jnp.zeros_like(s.bn_acc)
    core_copy(3, s.n_all.at[o], s.n_all.at[o]).wait_recv()
    core_copy(3, s.n_all.at[r], s.n_all.at[r]).wait_send()

    def flip_two(i, carry):
        who, rows = i // 3, pl.ds(pl.multiple_of((i % 3) * 128, 128), 128)
        s.n2t[:, pl.ds(pl.multiple_of(i * 128, 128), 128)] = flip(s.n_all[who, rows])
        return carry

    lax.fori_loop(0, 6, flip_two, 0)

    def rs_exp(j):
        return Bag(
            t=j, fin=j, split=True, piece=lambda a, b, c: s.wexp.at[j, a, b, c],
            col=lambda b, c: s.wexp.at[j, :, b, c], rb=lambda w: s.rb.at[j, w], ra=s.ra.at[j],
            rz=lambda k: s.rz.at[j, k], rx=lambda w: s.rx.at[j, w],
        )

    def rs_in(i):
        slot, part = ((0, 0), (1, 0), (0, 1), (1, 1), (2, 0), (2, 1))[i]
        half = slice(256 * part, 256 * part + 256)
        return Bag(
            t=9 + i, fin=4 + i, split=False, piece=lambda a, b, c: s.win.at[i, a, b, c],
            col=lambda b, c: s.win.at[i, :, b, c], rb=lambda w: s.rb.at[slot, w, :, :, half],
            ra=s.ra_in.at[i], rz=lambda k: s.rz_in.at[i, k],
        )

    def rs_red(j):
        split = bool(RED_SPLIT[j])
        return Bag(
            t=4 + j, fin=None, split=split, piece=lambda a, b, c: s.wred.at[j, a, slot(j, b, c)],
            col=lambda b, c: s.wred.at[j, :, slot(j, b, c)], rb=lambda w: s.rb_red.at[j, w],
            ra=s.land.at[j, 0] if split else s.land.at[j, 0:4],
            rz=lambda k: s.land.at[j, k + (1 if split else 4)], rx=lambda w: s.land.at[j, 7 + w],
        )

    def rs_out():
        return Bag(
            t=8, fin=None, split=False, piece=lambda a, b, c: s.wout.at[a, b, c, r],
            col=lambda b, c: s.wout.at[:, b, c, r], rb=lambda w: s.rb_out.at[w], ra=s.ra_out,
            rz=lambda k: s.rz_out.at[k],
        )

    def rs_small():
        return Bag(
            t=15, fin=None, split=False, piece=lambda a, b, c: s.sg.at[a, b, c],
            col=lambda b, c: s.sg.at[:, b, c], rb=lambda w: s.rb_sg.at[w], ra=s.ra_sg,
            rz=lambda k: s.rz_sg.at[k],
        )

    def rb_copy(it, which, yy, xx):
        return copy(it.col(yy, xx), it.rb(which), s.rsb_s.at[it.t, which], s.rsb_r.at[it.t, which], b_dev)

    def ra_copy(it):
        src = it.piece(z, ya, xa) if it.split else it.col(ya, xa)
        return copy(src, it.ra, s.rsa_s.at[it.t], s.rsa_r.at[it.t], a_dev)

    def add_into(it, yy, xx, sources):
        target = it.col(yy, xx)
        kind = F32 if it.t == 15 else BF

        def body(i, carry):
            total = target[i].astype(F32)
            for src in sources:
                total = total + src[i].astype(F32)
            target[i] = total.astype(kind)
            return carry

        lax.fori_loop(0, 4, body, 0)

    def own_copy(it, k, yy, xx, base, ss, rs):
        return copy(it.piece(z_at[k], yy, xx), it.rz(base + k), ss.at[it.t, k], rs.at[it.t, k], z_dev[k])

    def far_copy(it, k, yy, xx, which):
        return copy(
            it.piece(z_at[k], yy, xx), it.rx(which), s.rsx_s.at[it.t, which], s.rsx_r.at[it.t, which], near_middle
        )

    def own_start(it, yy, xx, base, ss, rs, which):
        for k in range(3):
            c = own_copy(it, k, yy, xx, base, ss, rs)
            if not it.split:
                c.start()
            elif k == 1:
                pl.when(at_end)(c.start)
            else:
                edge = 3 if k == 0 else 0
                pl.when(z != edge)(c.start)
                pl.when(z == edge)(far_copy(it, k, yy, xx, which).start)

    def own_relay(it, yy, xx, base, ss, rs, which):
        @pl.when(in_middle)
        def _():
            far_copy(it, 1, yy, xx, which).wait_recv()
            held = it.piece(z_at[1], yy, xx)
            held[...] = (held[...].astype(F32) + it.rx(which)[...].astype(F32)).astype(BF)
            own_copy(it, 1, yy, xx, base, ss, rs).start()

    def own_wait(it, yy, xx, base, ss, rs):
        for k in range(3):
            c = own_copy(it, k, yy, xx, base, ss, rs)
            if not it.split or k == 1:
                c.wait_recv()
            else:
                pl.when(z != (0 if k == 0 else 3))(c.wait_recv)

    def own_sent(it, yy, xx, base, ss, rs, which):
        for k in range(3):
            c = own_copy(it, k, yy, xx, base, ss, rs)
            if not it.split or k == 1:
                c.wait_send()
            else:
                edge = 3 if k == 0 else 0
                pl.when(z != edge)(c.wait_send)
                pl.when(z == edge)(far_copy(it, k, yy, xx, which).wait_send)

    def z_args(it, second):
        if second:
            return (ya, xa, 3, s.rsy_s, s.rsy_r)
        return (y, x, 0, s.rsz_s, s.rsz_r)

    def z_total(it, second):
        yy, xx, base, ss, rs = z_args(it, second)
        own_wait(it, yy, xx, base, ss, rs)
        total = it.piece(z, yy, xx)[...].astype(F32)
        for k in range(3):
            total = total + it.rz(base + k)[...].astype(F32)
        return total

    def f0(it):
        rb_copy(it, 0, yc, xc).start()
        rb_copy(it, 1, yb, xb).start()

    def f1(it):
        rb_copy(it, 0, yc, xc).wait_recv()
        add_into(it, ya, xa, [it.rb(0)])
        if not it.split:
            ra_copy(it).start()
            return
        own_start(it, *z_args(it, True), 1)
        rb_copy(it, 1, yb, xb).wait_recv()
        add_into(it, y, x, [it.rb(1)])
        own_start(it, *z_args(it, False), 0)

    def f2(it):
        if it.split:
            own_relay(it, *z_args(it, True), 1)
            own_relay(it, *z_args(it, False), 0)
            return
        rb_copy(it, 1, yb, xb).wait_recv()
        ra_copy(it).wait_recv()
        add_into(it, y, x, [it.rb(1), it.ra])
        own_start(it, *z_args(it, False), 0)

    def f3(it):
        if it.split:
            total = z_total(it, True)
            it.piece(z, ya, xa)[...] = total.astype(BF)
            ra_copy(it).start()

    def full_total(it):
        total = z_total(it, False)
        if it.split:
            ra_copy(it).wait_recv()
            total = total + it.ra[...].astype(F32)
        return total

    def fin_refs(index):
        if index < 4:
            return s.fin.at[index], s.fin_in.at[index]
        return s.fin_w.at[index - 4], s.fin_w_in.at[index - 4]

    def fin_copy(index):
        out, back = fin_refs(index)
        return copy(out.at[o_rows], back, s.fin_s.at[index], s.fin_r.at[index], core_dev)

    def small_fin():
        return copy(s.sfin, s.sfin_in, s.fin_s.at[10], s.fin_r.at[10], core_dev)

    def put_in(i, value, who):
        dwin_ref[:, part_cols(i, who)] = value

    def put_exp(source, who):
        for block in range(4):
            at = slice(block * 128, (block + 1) * 128)
            chunk = [source(j)[:, at] for j in range(4)]
            for q in range(4):
                cols = pl.ds(pl.multiple_of((2 * (4 * block + q) + who) * 128, 128), 128)
                dwexp_ref[:, cols] = pick([chunk[(q - g) % 4] for g in range(4)], group_32)

    def f4(it):
        if 4 <= it.t < 8:
            group = (place + 8 - it.t) % 4
            dwred_ref[pl.ds(pl.multiple_of(group * 32, 32), 32)] = full_total(it)
        elif it.t == 8:
            dwout_ref[...] = full_total(it)
        elif it.t == 15:
            s.sfin[...] = full_total(it)
            small_fin().start()
        else:
            out, _ = fin_refs(it.fin)
            out[...] = full_total(it)
            fin_copy(it.fin).start()
            if it.fin >= 4:
                put_in(it.fin - 4, out[my_rows], r)

    def f5(it):
        if it.fin is not None:
            fin_copy(it.fin).wait_recv()
            if it.fin >= 4:
                put_in(it.fin - 4, fin_refs(it.fin)[1][...], o)
            elif it.fin == 3:
                put_exp(lambda j: s.fin[j, my_rows], r)
                put_exp(lambda j: s.fin_in[j], o)
        elif it.t == 15:
            small_fin().wait_recv()
            row = lax.broadcasted_iota(jnp.int32, (16, 128), 0)
            own = s.sfin[...]
            dsmall_ref[...] = jnp.where(row < 8, own + s.sfin_in[...], own)

    def all_sent(it):
        rb_copy(it, 0, yc, xc).wait_send()
        rb_copy(it, 1, yb, xb).wait_send()
        ra_copy(it).wait_send()
        own_sent(it, *z_args(it, False), 0)
        if it.split:
            own_sent(it, *z_args(it, True), 1)
        if it.fin is not None:
            fin_copy(it.fin).wait_send()
        elif it.t == 15:
            small_fin().wait_send()

    order = []
    for j in range(4):
        order += [rs_red(j), rs_exp(j)]
    order += [rs_out()] + [rs_in(i) for i in range(6)] + [rs_small()]

    def step(i):
        for event, lag in ((f0, -LEAD), (f1, 1), (f2, 2), (f3, 3), (f4, 4), (f5, 5)):
            if 0 <= i - lag < len(order):
                event(order[i - lag])

    def feed(j, between):
        gather(3 * LOOK + 8 + 2 * j)
        gather(3 * LOOK + 9 + 2 * j)
        sent(gathers[8 + 2 * j])
        sent(gathers[9 + 2 * j])
        between(0)

        def hidden(n, inside):
            cols = pl.ds(pl.multiple_of(n * 256, 256), 256)
            left = s.n_all[...].reshape(768, 1024)
            inner = dot(left, s.wexp[j, :, :, :, :, cols].reshape(1024, 256)) + s.ebias[j, 0:1, cols]
            phi = 0.5 + 0.5 * lax.erf(inner * (2.0**-0.5))
            active = inner * phi
            s.ffb[0, :, cols] = active.astype(BF)
            s.act_t[cols] = active.T.astype(BF)
            slope = phi + inner * (jnp.exp(-0.5 * inner * inner) * 0.3989422804014327)
            up = s.c_all[...].reshape(768, 1024)
            weight = s.wred[j, pl.ds(2 * n, 2)].reshape(256, 1024)
            back = (dot_nt(up, weight) * slope).astype(BF)
            s.ffb[1, :, cols] = back
            s.gexp[j, 0:1, cols] = jnp.sum(back.astype(F32), axis=0, keepdims=True)
            return inside

        lax.fori_loop(0, 2, hidden, 0)

        def wide_tile(n, inside):
            cols = pl.ds(pl.multiple_of(n * 256, 256), 256)
            part = dot(s.ffb[0], s.wred[j, :, :, :, cols].reshape(512, 256))
            s.out_acc[:, :, cols] += part.reshape(2, 384, 256)
            back = dot_nt(s.ffb[1], s.wexp[j, n].reshape(256, 512))
            s.bn_acc[:, :, cols] += back.reshape(2, 384, 256)
            return inside

        lax.fori_loop(0, 4, wide_tile, 0)
        between(1)

        def grad_red(n, inside):
            cols = pl.ds(pl.multiple_of(n * 256, 256), 256)
            up = s.c_all[:, :, cols].reshape(768, 256)
            s.wred[j, :, :, :, cols] = dot(s.act_t[...], up).astype(BF).reshape(4, 4, 32, 256)
            return inside

        lax.fori_loop(0, 4, grad_red, 0)

        def grad_exp(n, inside):
            cols = pl.ds(pl.multiple_of(n * 256, 256), 256)
            grad = dot(s.n2t[...], s.ffb[1, :, cols]).astype(BF)
            s.wexp[j, :, :, :, :, cols] = grad.reshape(4, 2, 2, 64, 256)
            return inside

        lax.fori_loop(0, 2, grad_exp, 0)
        between(2)

    for j in range(3):
        feed(j, lambda place: None)

    def start_reduction(place_in):
        if place_in == 0:
            for it in order[:LEAD]:
                f0(it)
            step(0)
        elif place_in == 1:
            core_copy(4, s.bn_acc.at[o], s.cross).start()
            step(1)
        else:
            step(2)

    feed(3, start_reduction)

    core_copy(4, s.bn_acc.at[o], s.cross).wait_recv()
    s.n_all[o] = s.out_acc[o].astype(BF)
    core_copy(5, s.n_all.at[o], s.n_all.at[o]).start()

    def middle_back(i, carry):
        rows = pl.ds(pl.multiple_of(i * 128, 128), 128)
        unit, rate = centre(s.middle[rows])
        upstream = s.bn_acc[r, rows] + s.cross[rows]
        cot = s.c_all[r, rows].astype(F32)
        back = cot + norm_back(unit, rate, vec_row(5), upstream)
        s.bn_acc[r, rows] = back
        branch = back.astype(BF)
        s.wide[rows] = branch
        gain_t, shift_t, out_t, red_t = carry
        return (
            gain_t + jnp.sum(upstream * unit, axis=0, keepdims=True),
            shift_t + jnp.sum(upstream, axis=0, keepdims=True),
            out_t + jnp.sum(branch.astype(F32), axis=0, keepdims=True),
            red_t + jnp.sum(cot, axis=0, keepdims=True),
        )

    zero_row = jnp.zeros((1, 1024), F32)
    gain_t, shift_t, out_t, red_t = lax.fori_loop(0, 3, middle_back, (zero_row,) * 4)
    s.gvec[5:6] = gain_t
    s.gvec[6:7] = shift_t
    s.gvec[4:5] = out_t
    s.gvec[7:8] = red_t

    core_copy(0, s.half.at[o], s.half.at[o]).wait_send()
    core_copy(2, s.wout.at[:, :, :, r], s.wout.at[:, :, :, r]).wait_send()

    def back_att(n, carry):
        weight = s.wout[n].reshape(256, 1024)
        cols = pl.ds(pl.multiple_of((n % 2) * 256, 256), 256)
        s.half[n // 2, :, cols] = dot_nt(s.wide[...], weight).astype(BF)
        return carry

    lax.fori_loop(0, 4, back_att, 0)
    core_copy(6, s.half.at[o], s.ba_all.at[r]).start()
    s.ba_all[r] = s.half[r]
    step(3)
    sent(gathers[7])

    def grad_out(n, carry):
        cols = pl.ds(pl.multiple_of(n * 256, 256), 256)
        grad = dot(s.att_t[...], s.wide[:, cols]).astype(BF)
        s.wout[:, :, :, :, :, cols] = grad.reshape(4, 2, 2, 2, 32, 256)
        return carry

    lax.fori_loop(0, 4, grad_out, 0)
    core_copy(7, s.wout.at[:, :, :, o], s.outx).start()
    core_copy(5, s.n_all.at[r], s.n_all.at[r]).wait_recv()

    def result_tile(i, carry):
        rows = pl.ds(pl.multiple_of(i * 128, 128), 128)
        total = s.middle[rows] + s.out_acc[r, rows] + s.n_all[r, rows].astype(F32) + vec_row(7)
        result_ref[rows] = total.astype(BF)
        return carry

    lax.fori_loop(0, 3, result_tile, 0)
    core_copy(6, s.ba_all.at[o], s.ba_all.at[o]).wait_recv()

    def attend_back(hp, carry):
        k_t = flip(s.qkv[1, hp])
        dims = pl.ds(pl.multiple_of(hp * 128, 128), 128)
        s.dkv[...] = jnp.zeros_like(s.dkv)
        for rb in range(6):
            keys = key_count(rb)
            rows = slice(rb * 128, (rb + 1) * 128)
            both = pair_rows(s.qkv[0, hp, rows])
            at = (rb % 3) * 128
            up = pair_rows(s.ba_all[rb // 3, at : at + 128, dims])
            scores = dot_nt(s.qkv[1, hp, 0:keys], both) * factor + pair_mask(keys, rb)
            probs = jnp.exp2(scores - s.lse[hp, rb, 0:1])
            back_probs = dot_nt(s.qkv[2, hp, 0:keys], up)
            weighted = probs * back_probs
            centre_row = jnp.sum(weighted, axis=0, keepdims=True)
            back_scores = (weighted - probs * centre_row).astype(BF)
            s.dkv[1, 0:keys] += dot(probs.astype(BF), up)
            s.dkv[0, 0:keys] += dot(back_scores, both)
            query = dot(k_t[:, 0:keys], back_scores)
            query = jnp.concatenate([query[0:64, 0:128], query[64:128, 128:256]], axis=0)
            s.ffb[0, rows, dims] = (query.T * HD**-0.5).astype(BF)
        s.ffb[1, :, dims] = (s.dkv[0] * HD**-0.5).astype(BF)
        s.ffb[2, :, dims] = s.dkv[1].astype(BF)
        return carry

    core_copy(7, s.outx, s.outx).wait_recv()

    def add_out(i, carry):
        for yy in range(2):
            for xx in range(2):
                total = s.wout[i, yy, xx, r].astype(F32) + s.outx[i, yy, xx].astype(F32)
                s.wout[i, yy, xx, r] = total.astype(BF)
        return carry

    lax.fori_loop(0, 4, add_out, 0)

    lax.fori_loop(0, 1, attend_back, 0)
    step(4)
    lax.fori_loop(1, 3, attend_back, 0)
    step(5)
    lax.fori_loop(3, 4, attend_back, 0)

    core_copy(5, s.n_all.at[o], s.n_all.at[o]).wait_send()

    def back_in(n, carry):
        cols = pl.ds(pl.multiple_of(n * 256, 256), 256)
        total = dot_nt(s.ffb[0, :, 0:256], s.win[0, n].reshape(256, 256))
        for part in range(1, 6):
            at = (part % 2) * 256
            total = total + dot_nt(s.ffb[part // 2, :, at : at + 256], s.win[part, n].reshape(256, 256))
        s.out_acc[:, :, cols] = total.reshape(2, 384, 256)
        return carry

    lax.fori_loop(0, 4, back_in, 0)
    core_copy(8, s.out_acc.at[o], s.cross).start()
    step(6)
    for part in range(6):
        sent(gathers[1 + part])
        at = (part % 2) * 256
        grad = dot(s.n1t[...], s.ffb[part // 2, :, at : at + 256]).astype(BF)
        s.win[part] = grad.reshape(4, 2, 2, 64, 256)
        if part == 2:
            step(7)
    step(8)
    step(9)

    core_copy(8, s.out_acc.at[o], s.cross).wait_recv()

    def frame_back(i, carry):
        rows = pl.ds(pl.multiple_of(i * 128, 128), 128)
        unit, rate = centre(s.frames_all[r, rows].astype(F32))
        upstream = s.out_acc[r, rows] + s.cross[rows]
        back = s.bn_acc[r, rows] + norm_back(unit, rate, vec_row(0), upstream)
        fgrad_ref[rows] = back.astype(BF)
        gain_t, shift_t = carry
        return (
            gain_t + jnp.sum(upstream * unit, axis=0, keepdims=True),
            shift_t + jnp.sum(upstream, axis=0, keepdims=True),
        )

    gain_t, shift_t = lax.fori_loop(0, 3, frame_back, (zero_row,) * 2)
    s.gvec[0:1] = gain_t
    s.gvec[1:2] = shift_t
    s.gvec[2:4] = jnp.zeros((2, 1024), F32)
    s.gvec[2:3, my_half] = jnp.sum(s.ffb[0].astype(F32), axis=0, keepdims=True)
    s.gvec[3:4, my_half] = jnp.sum(s.ffb[2].astype(F32), axis=0, keepdims=True)
    s.sg[...] = jnp.zeros_like(s.sg)
    for zz in range(4):
        for yy in range(2):
            for xx in range(2):
                at = (zz * 2 + yy) * 128
                s.sg[zz, yy, xx, 0:8] = s.gvec[:, at : at + 128]
                q = 2 * yy + xx
                block = slice(zz * 128, (zz + 1) * 128)
                chunk = [s.gexp[j, 0:1, block] for j in range(4)]
                s.sg[zz, yy, xx, 8:9] = pick([chunk[(q - g) % 4] for g in range(4)], group_1)

    for i in range(10, len(order) + 5):
        step(i)

    for i, item in enumerate(pre):
        if not 8 <= i < 12:
            item.wait_send()
    sent(gathers[0])
    core_copy(1, s.half_t.at[o], s.half_t.at[o]).wait_send()
    core_copy(4, s.bn_acc.at[o], s.cross).wait_send()
    core_copy(6, s.half.at[o], s.ba_all.at[r]).wait_send()
    core_copy(7, s.wout.at[:, :, :, o], s.outx).wait_send()
    core_copy(8, s.out_acc.at[o], s.cross).wait_send()
    for it in order:
        all_sent(it)


def hand_on(*refs):
    given, taken, held = refs[0:6], refs[6:12], refs[12:18]
    sems = refs[18]
    inward = [pltpu.make_async_copy(given[i], held[i], sems.at[0, i]) for i in range(6)]
    outward = [pltpu.make_async_copy(held[i], taken[i], sems.at[1, i]) for i in range(6)]
    for item in inward:
        item.start()
    for i in range(6):
        inward[i].wait()
        outward[i].start()
    for item in outward:
        item.wait()


def fused_shards(
    frames, frames_cotangent, phoneme_len, prompt_len, target_segment, first_gain, first_shift, inward_weight,
    query_bias, value_bias, outward_weight, outward_bias, second_gain, second_shift, expand_weight, expand_bias,
    reduce_weight, reduce_bias,
):
    number = lax.axis_index("dp") * 2 + lax.axis_index("role")
    quarter = number % 4
    rows = jnp.stack(
        [first_gain, first_shift, query_bias, value_bias, outward_bias, second_gain, second_shift, reduce_bias]
    )
    lane = jnp.arange(128) // 32
    rows = jnp.where(lane[None] == quarter, jnp.tile(rows, (1, 4)), jnp.zeros((), BF))
    small = jnp.concatenate([rows, expand_bias[None], jnp.zeros((7, 128), BF)], axis=0)

    scratch = scratch_list()
    vmem = pl.BlockSpec(memory_space=pltpu.VMEM)
    smem = pl.BlockSpec(memory_space=pltpu.SMEM)
    hbm = pl.BlockSpec(memory_space=pl.ANY)
    outs = pl.pallas_call(
        functools.partial(layer_kernel, tuple(scratch)),
        out_shape=[
            jax.ShapeDtypeStruct((384, 1024), BF),
            jax.ShapeDtypeStruct((384, 1024), BF),
            jax.ShapeDtypeStruct((32, 3072), F32),
            jax.ShapeDtypeStruct((32, 1024), F32),
            jax.ShapeDtypeStruct((32, 4096), F32),
            jax.ShapeDtypeStruct((128, 1024), F32),
            jax.ShapeDtypeStruct((16, 128), F32),
        ],
        in_specs=[smem, smem, vmem, hbm, hbm] + [vmem] * 5,
        out_specs=[vmem] * 7,
        scratch_shapes=list(scratch.values()),
        compiler_params=pltpu.CompilerParams(
            collective_id=0, has_side_effects=True, vmem_limit_bytes=62 * 1024 * 1024
        ),
    )(
        phoneme_len, prompt_len, target_segment, frames[0], frames_cotangent[0], small, inward_weight,
        outward_weight, expand_weight, reduce_weight,
    )
    d_small = outs[6]
    result, frames_gradient, d_in, d_out, d_exp, d_red = pl.pallas_call(
        hand_on,
        out_shape=[jax.ShapeDtypeStruct(item.shape, item.dtype) for item in outs[:6]],
        in_specs=[hbm] * 6,
        out_specs=[hbm] * 6,
        scratch_shapes=[pltpu.VMEM(item.shape, item.dtype) for item in outs[:6]]
        + [pltpu.SemaphoreType.DMA((2, 6))],
    )(*outs[:6])
    mine = lax.dynamic_slice(d_small, (0, quarter * 32), (8, 32))
    return (
        result[None], frames_gradient[None], mine[0], mine[1], d_in, mine[2], mine[3], d_out, mine[4], mine[5],
        mine[6], d_exp, d_small[8], d_red, mine[7],
    )


def passed_along(block, axis, distance):
    devices = range(lax.axis_size(axis))
    route = [(i - distance, i) for i in devices if i - distance in devices]
    return lax.ppermute(block, axis, route)


def normalize(values, gain, shift):
    mean_value = jnp.mean(values, axis=-1, keepdims=True)
    centered = values - mean_value
    spread = jnp.mean(centered * centered, axis=-1, keepdims=True)
    return centered * lax.rsqrt(spread + EPS) * gain + shift


def smooth_gate(values):
    return jax.nn.gelu(values, approximate=False)


def inner_rows(left, right):
    return lax.dot_general(
        left, right, (((0,), (0,)), ((), ())), preferred_element_type=jnp.float32
    )


def outer_cols(left, right):
    return lax.dot_general(
        left, right, (((1,), (1,)), ((), ())), preferred_element_type=jnp.float32
    )


def plain_shards(
    frames,
    frames_cotangent,
    phoneme_len,
    prompt_len,
    target_segment,
    first_gain,
    first_shift,
    inward_weight,
    query_bias,
    value_bias,
    outward_weight,
    outward_bias,
    second_gain,
    second_shift,
    expand_weight,
    expand_bias,
    reduce_weight,
    reduce_bias,
):
    attention_part = (
        lax.all_gather(first_gain, ("dp", "role"), axis=0, tiled=True),
        lax.all_gather(first_shift, ("dp", "role"), axis=0, tiled=True),
        lax.all_gather(inward_weight, ("dp", "role"), axis=0, tiled=True),
        lax.all_gather(query_bias, ("dp", "role"), axis=0, tiled=True),
        lax.all_gather(value_bias, ("dp", "role"), axis=0, tiled=True),
        lax.all_gather(outward_weight, ("dp", "role"), axis=0, tiled=True),
        lax.all_gather(outward_bias, ("dp", "role"), axis=0, tiled=True),
    )
    (
        full_gain,
        full_shift,
        full_inward,
        full_query_bias,
        full_value_bias,
        full_outward,
        full_outward_bias,
    ) = attention_part
    side = lax.axis_index("role")
    local_rows = frames.shape[1]
    scale = HD ** (-0.5)
    current = frames[0].astype(jnp.float32)
    normed = normalize(
        current, full_gain.astype(jnp.float32), full_shift.astype(jnp.float32)
    ).astype(jnp.bfloat16)
    mixed = jnp.dot(normed, full_inward, preferred_element_type=jnp.float32)
    queries = (mixed[:, :D] + full_query_bias.astype(jnp.float32)).astype(jnp.bfloat16)
    keys_own = mixed[:, D : 2 * D].astype(jnp.bfloat16)
    values_own = (mixed[:, 2 * D :] + full_value_bias.astype(jnp.float32)).astype(jnp.bfloat16)
    remote_keys, remote_values = passed_along((keys_own, values_own), "role", 1)
    keys_all = jnp.concatenate([remote_keys, keys_own], axis=0)
    values_all = jnp.concatenate([remote_values, values_own], axis=0)
    row_index = jnp.arange(local_rows)[:, None]
    col_index = jnp.arange(2 * local_rows)[None, :]
    own_col = col_index - local_rows
    prefix_length = phoneme_len[0] + prompt_len[0]
    segment = target_segment[0]
    key_segment = jnp.concatenate([jnp.full((local_rows,), -1, jnp.int32), segment])
    prompt_rows = (own_col >= 0) & (own_col <= row_index) & (own_col < prefix_length)
    target_rows = (col_index < prefix_length) | (own_col >= 0) & (own_col <= row_index) & (
        key_segment[None, :] == segment[:, None]
    )
    allowed = jnp.where(side == 0, prompt_rows, target_rows)

    def attend(index):
        start = index * HD
        head_query = lax.dynamic_slice_in_dim(queries, start, HD, 1)
        head_key = lax.dynamic_slice_in_dim(keys_all, start, HD, 1)
        head_value = lax.dynamic_slice_in_dim(values_all, start, HD, 1)
        scores = outer_cols(head_query, head_key) * scale
        masked = jnp.where(allowed, scores, MASKED)
        peak = jnp.max(masked, axis=1, keepdims=True)
        expo = jnp.exp(masked - peak)
        total = jnp.sum(expo, axis=1, keepdims=True)
        probs = (expo / total).astype(jnp.bfloat16)
        return (
            jnp.dot(probs, head_value, preferred_element_type=jnp.float32),
            (peak + jnp.log(total))[:, 0],
        )

    head_outs, log_totals = lax.map(attend, jnp.arange(H))
    attended = head_outs.transpose(1, 0, 2).reshape(local_rows, D).astype(jnp.bfloat16)
    middle = (
        current
        + jnp.dot(attended, full_outward, preferred_element_type=jnp.float32)
        + full_outward_bias.astype(jnp.float32)
    )
    feed_part = (
        lax.all_gather(second_gain, ("dp", "role"), axis=0, tiled=True),
        lax.all_gather(second_shift, ("dp", "role"), axis=0, tiled=True),
        lax.all_gather(expand_weight, ("dp", "role"), axis=0, tiled=True),
        lax.all_gather(expand_bias, ("dp", "role"), axis=0, tiled=True),
        lax.all_gather(reduce_weight, ("dp", "role"), axis=0, tiled=True),
        lax.all_gather(reduce_bias, ("dp", "role"), axis=0, tiled=True),
    )
    full_gain_two, full_shift_two, full_expand, full_expand_bias, full_reduce, full_reduce_bias = (
        feed_part
    )
    gain_two = full_gain_two.astype(jnp.float32)
    shift_two = full_shift_two.astype(jnp.float32)
    normed_two = normalize(middle, gain_two, shift_two).astype(jnp.bfloat16)
    inner = jnp.dot(
        normed_two, full_expand, preferred_element_type=jnp.float32
    ) + full_expand_bias.astype(jnp.float32)
    active = smooth_gate(inner).astype(jnp.bfloat16)
    output = (
        middle
        + jnp.dot(active, full_reduce, preferred_element_type=jnp.float32)
        + full_reduce_bias.astype(jnp.float32)
    )
    result = output.astype(jnp.bfloat16)[None]
    again_expand = feed_part[2]
    again_reduce = feed_part[4]
    again_gain = attention_part[0].astype(jnp.float32)
    again_shift = attention_part[1].astype(jnp.float32)
    again_inward = attention_part[2]
    again_outward = attention_part[5]
    upstream = frames_cotangent[0]
    upstream_float = upstream.astype(jnp.float32)
    reduce_bias_term = jnp.sum(upstream_float, axis=0)
    reduce_weight_term = inner_rows(active, upstream)
    back_active = outer_cols(upstream, again_reduce)
    gate_pull = jax.vjp(smooth_gate, inner)[1]
    back_inner = gate_pull(back_active)[0].astype(jnp.bfloat16)
    expand_bias_term = jnp.sum(back_inner.astype(jnp.float32), axis=0)
    expand_weight_term = inner_rows(normed_two, back_inner)
    back_normed_two = outer_cols(back_inner, again_expand)
    second_pull = jax.vjp(normalize, middle, gain_two, shift_two)[1]
    middle_part, second_gain_term, second_shift_term = second_pull(back_normed_two)
    back_middle = upstream_float + middle_part
    back_branch = back_middle.astype(jnp.bfloat16)
    outward_bias_term = jnp.sum(back_branch.astype(jnp.float32), axis=0)
    outward_weight_term = inner_rows(attended, back_branch)
    back_attended = outer_cols(back_branch, again_outward).astype(jnp.bfloat16)

    def attend_back(inputs):
        index, log_total = inputs
        start = index * HD
        head_query = lax.dynamic_slice_in_dim(queries, start, HD, 1)
        head_key = lax.dynamic_slice_in_dim(keys_all, start, HD, 1)
        head_value = lax.dynamic_slice_in_dim(values_all, start, HD, 1)
        head_upstream = lax.dynamic_slice_in_dim(back_attended, start, HD, 1)
        scores = outer_cols(head_query, head_key) * scale
        probs = jnp.where(allowed, jnp.exp(scores - log_total[:, None]), 0.0)
        back_probs = outer_cols(head_upstream, head_value)
        centre = jnp.sum(probs * back_probs, axis=1, keepdims=True)
        back_scores = (probs * (back_probs - centre)).astype(jnp.bfloat16)
        back_query = jnp.dot(back_scores, head_key, preferred_element_type=jnp.float32) * scale
        back_key = inner_rows(back_scores, head_query) * scale
        back_value = inner_rows(probs.astype(jnp.bfloat16), head_upstream)
        return (back_query, back_key, back_value)

    head_query_grads, head_key_grads, head_value_grads = lax.map(
        attend_back, (jnp.arange(H), log_totals)
    )
    back_queries = head_query_grads.transpose(1, 0, 2).reshape(local_rows, D)
    back_keys_all = head_key_grads.transpose(1, 0, 2).reshape(2 * local_rows, D)
    back_values_all = head_value_grads.transpose(1, 0, 2).reshape(2 * local_rows, D)
    returned_keys, returned_values = (
        passed_along(back_keys_all[:local_rows].astype(jnp.bfloat16), "role", -1).astype(
            jnp.float32
        ),
        passed_along(back_values_all[:local_rows].astype(jnp.bfloat16), "role", -1).astype(
            jnp.float32
        ),
    )
    query_low = back_queries.astype(jnp.bfloat16)
    key_low = (back_keys_all[local_rows:] + returned_keys).astype(jnp.bfloat16)
    value_low = (back_values_all[local_rows:] + returned_values).astype(jnp.bfloat16)
    back_mixed = jnp.concatenate([query_low, key_low, value_low], axis=1)
    query_bias_term = jnp.sum(query_low.astype(jnp.float32), axis=0)
    value_bias_term = jnp.sum(value_low.astype(jnp.float32), axis=0)
    inward_weight_term = inner_rows(normed, back_mixed)
    back_normed = outer_cols(back_mixed, again_inward)
    first_pull = jax.vjp(normalize, current, again_gain, again_shift)[1]
    frame_part, first_gain_term, first_shift_term = first_pull(back_normed)
    frames_gradient = (back_middle + frame_part).astype(jnp.bfloat16)[None]
    totals = (
        lax.psum_scatter(first_gain_term, ("dp", "role"), scatter_dimension=0, tiled=True),
        lax.psum_scatter(first_shift_term, ("dp", "role"), scatter_dimension=0, tiled=True),
        lax.psum_scatter(inward_weight_term, ("dp", "role"), scatter_dimension=0, tiled=True),
        lax.psum_scatter(query_bias_term, ("dp", "role"), scatter_dimension=0, tiled=True),
        lax.psum_scatter(value_bias_term, ("dp", "role"), scatter_dimension=0, tiled=True),
        lax.psum_scatter(outward_weight_term, ("dp", "role"), scatter_dimension=0, tiled=True),
        lax.psum_scatter(outward_bias_term, ("dp", "role"), scatter_dimension=0, tiled=True),
        lax.psum_scatter(second_gain_term, ("dp", "role"), scatter_dimension=0, tiled=True),
        lax.psum_scatter(second_shift_term, ("dp", "role"), scatter_dimension=0, tiled=True),
        lax.psum_scatter(expand_weight_term, ("dp", "role"), scatter_dimension=0, tiled=True),
        lax.psum_scatter(expand_bias_term, ("dp", "role"), scatter_dimension=0, tiled=True),
        lax.psum_scatter(reduce_weight_term, ("dp", "role"), scatter_dimension=0, tiled=True),
        lax.psum_scatter(reduce_bias_term, ("dp", "role"), scatter_dimension=0, tiled=True),
    )
    return (
        result,
        frames_gradient,
        totals[0],
        totals[1],
        totals[2],
        totals[3],
        totals[4],
        totals[5],
        totals[6],
        totals[7],
        totals[8],
        totals[9],
        totals[10],
        totals[11],
        totals[12],
    )


def solution(mesh):
    placed = (
        P("dp", "role", None),
        P("dp", "role", None),
        P("dp"),
        P("dp"),
        P("dp", None),
        P(("dp", "role")),
        P(("dp", "role")),
        P(("dp", "role"), None),
        P(("dp", "role")),
        P(("dp", "role")),
        P(("dp", "role"), None),
        P(("dp", "role")),
        P(("dp", "role")),
        P(("dp", "role")),
        P(("dp", "role"), None),
        P(("dp", "role")),
        P(("dp", "role"), None),
        P(("dp", "role")),
    )
    fused = mesh.shape["dp"] == 16 and mesh.shape["role"] == 2
    return jax.shard_map(
        fused_shards if fused else plain_shards,
        mesh=mesh,
        in_specs=placed,
        out_specs=(
            P("dp", "role", None),
            P("dp", "role", None),
            P(("dp", "role")),
            P(("dp", "role")),
            P(("dp", "role"), None),
            P(("dp", "role")),
            P(("dp", "role")),
            P(("dp", "role"), None),
            P(("dp", "role")),
            P(("dp", "role")),
            P(("dp", "role")),
            P(("dp", "role"), None),
            P(("dp", "role")),
            P(("dp", "role"), None),
            P(("dp", "role")),
        ),
        check_vma=False,
    )
```

```python
import functools

import jax
import jax.numpy as jnp
from jax import lax
from jax.experimental import pallas as pl
from jax.experimental.pallas import tpu as pltpu
from jax.sharding import PartitionSpec as P

D = 1024
H = 16
HD = 64
EPS = 1e-05
MASKED = -1e30
LOG2E = 1.4426950408889634
BF = jnp.bfloat16
F32 = jnp.float32
MESH = pl.DeviceIdType.MESH


def dot(left, right):
    return lax.dot_general(left, right, (((1,), (0,)), ((), ())), preferred_element_type=F32)


def dot_nt(left, right):
    return lax.dot_general(left, right, (((1,), (1,)), ((), ())), preferred_element_type=F32)


def flip(value):
    return value.astype(F32).T.astype(value.dtype)


def centre(values):
    mean_value = jnp.mean(values, axis=-1, keepdims=True)
    centered = values - mean_value
    spread = jnp.mean(centered * centered, axis=-1, keepdims=True)
    return centered * lax.rsqrt(spread + EPS), lax.rsqrt(spread + EPS)


def norm_back(unit, rate, gain, upstream):
    pulled = upstream * gain
    first = jnp.mean(pulled, axis=-1, keepdims=True)
    second = jnp.mean(pulled * unit, axis=-1, keepdims=True)
    return rate * (pulled - first - unit * second)


LEAD = 1
EARLY_CHUNK = 2
LOOK = 2
LAG_IN = 7
LAG_FF = 7
RED_SPLIT = (0, 0, 0, 0)


def scratch_list():
    dma = pltpu.SemaphoreType.DMA
    v = pltpu.VMEM
    return dict(
        small=v((4, 2, 2, 2, 16, 128), BF),
        vec=v((8, 1024), F32),
        ebias=v((4, 8, 512), F32),
        frames_all=v((2, 384, 1024), BF),
        c_all=v((2, 384, 1024), BF),
        n_all=v((2, 384, 1024), BF),
        n1t=v((1024, 768), BF),
        n2t=v((1024, 768), BF),
        win=v((6, 4, 2, 2, 64, 256), BF),
        wout=v((4, 2, 2, 2, 32, 1024), BF),
        wexp=v((4, 4, 2, 2, 64, 512), BF),
        wred=v((4, 4, 4, 32, 1024), BF),
        qkv=v((3, 4, 768, 128), BF),
        mask=v((768, 768), BF),
        lse=v((4, 6, 8, 256), F32),
        half=v((2, 384, 512), BF),
        half_t=v((2, 512, 384), BF),
        wide=v((384, 1024), BF),
        att_t=v((1024, 384), BF),
        middle=v((384, 1024), F32),
        out_acc=v((2, 384, 1024), F32),
        bn_acc=v((2, 384, 1024), F32),
        cross=v((384, 1024), F32),
        ffb=v((3, 768, 512), BF),
        act_t=v((512, 768), BF),
        ba_all=v((2, 384, 512), BF),
        dkv=v((2, 768, 128), F32),
        gvec=v((8, 1024), F32),
        gexp=v((4, 8, 512), F32),
        outx=v((4, 2, 2, 32, 1024), BF),
        rb=v((4, 2, 4, 64, 512), BF),
        ra=v((4, 64, 512), BF),
        rz=v((4, 6, 64, 512), BF),
        rx=v((4, 2, 64, 512), BF),
        ra_in=v((6, 4, 64, 256), BF),
        rz_in=v((6, 3, 64, 256), BF),
        rb_red=v((4, 2, 4, 32, 1024), BF),
        land=v((4, 7, 32, 1024), BF),
        rb_out=v((2, 4, 32, 1024), BF),
        ra_out=v((4, 32, 1024), BF),
        rz_out=v((3, 32, 1024), BF),
        sg=v((4, 2, 2, 16, 128), F32),
        rb_sg=v((2, 4, 16, 128), F32),
        ra_sg=v((4, 16, 128), F32),
        rz_sg=v((3, 16, 128), F32),
        fin=v((4, 64, 512), F32),
        fin_in=v((4, 32, 512), F32),
        fin_w=v((6, 64, 256), F32),
        fin_w_in=v((6, 32, 256), F32),
        sfin=v((16, 128), F32),
        sfin_in=v((16, 128), F32),
        own_s=dma((2,)),
        pre_s=dma((13,)),
        pre_r=dma((13,)),
        agz_s=dma((16, 3)),
        agz_r=dma((16, 3)),
        agy_s=dma((16, 3)),
        agy_r=dma((16, 3)),
        agx_s=dma((16, 2)),
        aga_s=dma((16,)),
        aga_r=dma((16,)),
        agb_s=dma((16, 2)),
        agb_r=dma((16, 2)),
        core_s=dma((9,)),
        core_r=dma((9,)),
        rsb_s=dma((16, 2)),
        rsb_r=dma((16, 2)),
        rsa_s=dma((16,)),
        rsa_r=dma((16,)),
        rsz_s=dma((16, 3)),
        rsz_r=dma((16, 3)),
        rsy_s=dma((16, 3)),
        rsy_r=dma((16, 3)),
        rsx_s=dma((16, 2)),
        rsx_r=dma((16, 2)),
        fin_s=dma((11,)),
        fin_r=dma((11,)),
    )


class Bag:
    def __init__(self, **kw):
        self.__dict__.update(kw)


N_IN = 10
N_OUT = 7


def layer_kernel(names, *refs):
    (phon_ref, prom_ref, seg_ref, frames_ref, cot_ref, small_in, win_in, wout_in, wexp_in, wred_in) = refs[:N_IN]
    (result_ref, fgrad_ref, dwin_ref, dwout_ref, dwexp_ref, dwred_ref, dsmall_ref) = refs[N_IN : N_IN + N_OUT]
    s = Bag(**dict(zip(names, refs[N_IN + N_OUT :])))

    dp = lax.axis_index("dp")
    r = lax.axis_index("role")
    o = 1 - r
    z, y, x = dp // 4, (dp // 2) % 2, dp % 2
    ya, xa = y + r * (1 - 2 * y), x + (1 - r) * (1 - 2 * x)
    yb, xb = y + (1 - r) * (1 - 2 * y), x + r * (1 - 2 * x)
    yc, xc = 1 - y, 1 - x
    core_dev = (dp, o)
    a_dev = (z * 4 + ya * 2 + xa, r)
    b_dev = (z * 4 + yb * 2 + xb, r)
    z_dev = [(((z + k) % 4) * 4 + y * 2 + x, r) for k in (1, 2, 3)]
    z_at = [(z + k) % 4 for k in (1, 2, 3)]
    z_from = [(z + 4 - k) % 4 for k in (1, 2, 3)]
    at_end = (z == 0) | (z == 3)
    in_middle = (z == 1) | (z == 2)
    far = z_from[1]
    far_end = (jnp.where(z == 2, 3, 0) * 4 + y * 2 + x, r)
    near_middle = (jnp.where(z == 0, 1, 2) * 4 + y * 2 + x, r)
    place = 2 * y + x

    def copy(src, dst, ss, rs, dev):
        return pltpu.make_async_remote_copy(
            src_ref=src, dst_ref=dst, send_sem=ss, recv_sem=rs, device_id=dev, device_id_type=MESH
        )

    barrier = pltpu.get_barrier_semaphore()
    for dev in z_dev + [a_dev, b_dev, core_dev]:
        pl.semaphore_signal(barrier, inc=1, device_id=dev, device_id_type=MESH)
    pl.semaphore_wait(barrier, 6)

    my_rows = pl.ds(pl.multiple_of(r * 32, 32), 32)
    o_rows = pl.ds(pl.multiple_of(o * 32, 32), 32)

    def part_cols(part, who):
        return pl.ds(pl.multiple_of((part // 2) * 1024 + who * 512 + (part % 2) * 256, 256), 256)

    pre = []
    pre.append(copy(small_in, s.small.at[z, y, x, r], s.pre_s.at[0], s.pre_r.at[0], core_dev))
    for i in range(6):
        pre.append(
            copy(
                win_in.at[:, part_cols(i, o)],
                s.win.at[i, z, y, x, my_rows],
                s.pre_s.at[1 + i],
                s.pre_r.at[1 + i],
                core_dev,
            )
        )
    pre.append(copy(frames_ref, s.frames_all.at[r], s.pre_s.at[7], s.pre_r.at[7], core_dev))
    for j in range(4):
        pre.append(
            copy(
                s.half.at[o, j * 32 : (j + 1) * 32],
                s.wexp.at[j, z, y, x, my_rows],
                s.pre_s.at[8 + j],
                s.pre_r.at[8 + j],
                core_dev,
            )
        )
    pre.append(copy(cot_ref, s.c_all.at[r], s.pre_s.at[12], s.pre_r.at[12], core_dev))
    for item in pre[:8]:
        item.start()
    group_32 = lax.broadcasted_iota(jnp.int32, (32, 128), 1) // 32

    def pick(parts, group):
        picked = parts[3]
        for g in range(3):
            picked = jnp.where(group == g, parts[g], picked)
        return picked

    for who in range(2):
        for block in range(4):
            source = [
                wexp_in[:, (2 * (4 * block + q) + who) * 128 : (2 * (4 * block + q) + who + 1) * 128].astype(F32)
                for q in range(4)
            ]
            for j in range(4):
                chosen = pick([source[(g + j) % 4] for g in range(4)], group_32)
                s.half[who, j * 32 : (j + 1) * 32, block * 128 : (block + 1) * 128] = chosen.astype(BF)
    for item in pre[8:]:
        item.start()
    own_frames = pltpu.make_async_copy(frames_ref, s.frames_all.at[r], s.own_s.at[0])
    own_cot = pltpu.make_async_copy(cot_ref, s.c_all.at[r], s.own_s.at[1])
    own_frames.start()
    own_cot.start()
    s.small[z, y, x, r] = small_in[...]
    for i in range(6):
        s.win[i, z, y, x, my_rows] = win_in[:, part_cols(i, r)]
    s.wout[z, y, x, r] = wout_in[...]
    for j in range(4):
        group = (place + 4 - j) % 4
        s.wred[j, z, group] = wred_in[pl.ds(pl.multiple_of(group * 32, 32), 32)]
    for j in range(4):
        s.wexp[j, z, y, x, my_rows] = s.half[r, j * 32 : (j + 1) * 32]

    def ag_item(t, piece, col, split):
        return Bag(t=t, piece=piece, col=col, split=split)

    def slot(j, b, c):
        return (2 * b + c + 4 - j) % 4

    gathers = [ag_item(0, lambda a, b, c: s.small.at[a, b, c], lambda b, c: s.small.at[:, b, c], False)]
    for i in range(6):
        gathers.append(
            ag_item(
                1 + i, lambda a, b, c, i=i: s.win.at[i, a, b, c], lambda b, c, i=i: s.win.at[i, :, b, c], False
            )
        )
    gathers.append(ag_item(7, lambda a, b, c: s.wout.at[a, b, c, r], lambda b, c: s.wout.at[:, b, c, r], False))
    for j in range(4):
        gathers.append(
            ag_item(
                8 + 2 * j, lambda a, b, c, j=j: s.wexp.at[j, a, b, c], lambda b, c, j=j: s.wexp.at[j, :, b, c], True
            )
        )
        gathers.append(
            ag_item(
                9 + 2 * j,
                lambda a, b, c, j=j: s.wred.at[j, a, slot(j, b, c)],
                lambda b, c, j=j: s.wred.at[j, :, slot(j, b, c)],
                bool(RED_SPLIT[j]),
            )
        )

    def when(cond, go):
        if isinstance(cond, bool):
            if cond:
                go()
        else:
            pl.when(cond)(go)

    def z_copies(it, yy, xx, ss, rs):
        p = it.piece(z, yy, xx)
        return [copy(p, p, ss.at[it.t, k], rs.at[it.t, k], z_dev[k]) for k in range(3)]

    def straight(it, k):
        if not it.split or k == 1:
            return True
        return z != 3 if k == 0 else z != 0

    def z_start(it, yy, xx, ss, rs):
        for k, c in enumerate(z_copies(it, yy, xx, ss, rs)):
            when(straight(it, k), c.start)

    def z_relay(it, yy, xx, rs, which):
        p = it.piece(far, yy, xx)

        @pl.when(in_middle)
        def _():
            copy(p, p, s.agx_s.at[it.t, which], rs.at[it.t, 1], far_end).wait_recv()
            copy(p, p, s.agx_s.at[it.t, which], rs.at[it.t, jnp.where(z == 2, 2, 0)], far_end).start()

    def z_wait(it, yy, xx, ss, rs):
        for k in range(3):
            p = it.piece(z_from[k], yy, xx)
            c = copy(p, p, ss.at[it.t, k], rs.at[it.t, k], z_dev[k])
            when(at_end if it.split and k == 1 else True, c.wait_recv)

    def z_sent(it, yy, xx, ss, rs, which):
        for k, c in enumerate(z_copies(it, yy, xx, ss, rs)):
            when(straight(it, k), c.wait_send)
        if it.split:
            p = it.piece(far, yy, xx)
            pl.when(in_middle)(copy(p, p, s.agx_s.at[it.t, which], rs.at[it.t, 0], far_end).wait_send)

    def a_piece(it, yy, xx):
        p = it.piece(z, yy, xx)
        return copy(p, p, s.aga_s.at[it.t], s.aga_r.at[it.t], a_dev)

    def a_copy(it, yy, xx):
        return copy(it.col(yy, xx), it.col(yy, xx), s.aga_s.at[it.t], s.aga_r.at[it.t], a_dev)

    def b_copy(it, which, yy, xx):
        return copy(it.col(yy, xx), it.col(yy, xx), s.agb_s.at[it.t, which], s.agb_r.at[it.t, which], b_dev)

    def e0(it):
        if it.split:
            a_piece(it, y, x).start()
        z_start(it, y, x, s.agz_s, s.agz_r)

    def e1(it):
        if it.split:
            z_relay(it, y, x, s.agz_r, 0)
            a_piece(it, ya, xa).wait_recv()
            z_start(it, ya, xa, s.agy_s, s.agy_r)
            return
        z_wait(it, y, x, s.agz_s, s.agz_r)
        a_copy(it, y, x).start()
        b_copy(it, 0, y, x).start()

    def e2(it):
        if it.split:
            z_relay(it, ya, xa, s.agy_r, 1)
            z_wait(it, y, x, s.agz_s, s.agz_r)
            b_copy(it, 0, y, x).start()
            z_wait(it, ya, xa, s.agy_s, s.agy_r)
            b_copy(it, 1, ya, xa).start()
            return
        a_copy(it, ya, xa).wait_recv()
        b_copy(it, 1, ya, xa).start()

    def e3(it):
        b_copy(it, 0, yb, xb).wait_recv()
        b_copy(it, 1, yc, xc).wait_recv()

    def sent(it):
        z_sent(it, y, x, s.agz_s, s.agz_r, 0)
        if it.split:
            a_piece(it, y, x).wait_send()
            z_sent(it, ya, xa, s.agy_s, s.agy_r, 1)
        else:
            a_copy(it, y, x).wait_send()
        b_copy(it, 0, y, x).wait_send()
        b_copy(it, 1, ya, xa).wait_send()

    def pre_in(index, dst):
        copy(dst, dst, s.pre_s.at[index], s.pre_r.at[index], core_dev).wait_recv()

    def ready(i):
        if i == 0:
            pre_in(0, s.small.at[z, y, x, o])
        elif i < 7:
            pre_in(i, s.win.at[i - 1, z, y, x, o_rows])
        elif i >= 8 and i % 2 == 0:
            j = (i - 8) // 2
            pre_in(8 + j, s.wexp.at[j, z, y, x, o_rows])

    done = []

    def ahead(count):
        for i in range(len(done), count + 1):
            done.append(i)
            for event, lag in ((e0, 0), (e1, LOOK), (e2, 2 * LOOK)):
                if 0 <= i - lag < len(gathers):
                    if lag == 0:
                        ready(i)
                    event(gathers[i - lag])

    def arrive(i, lag):
        ahead(i + lag)
        e3(gathers[i])

    ahead(2)

    for edge, k in ((0, 0), (3, 2)):

        @pl.when(z == edge)
        def _(k=k):
            for base in (0, 3):
                s.rz[:, base + k] = jnp.zeros((4, 64, 512), BF)
                for j in range(4):
                    if RED_SPLIT[j]:
                        s.land[j, 1 + base + k] = jnp.zeros((32, 1024), BF)

    own_frames.wait()
    own_cot.wait()
    prefix = phon_ref[0] + prom_ref[0]
    seg_row = seg_ref[...].astype(F32)
    seg_wide = jnp.broadcast_to(seg_row, (384, 384))
    seg_tall = seg_wide.T
    key_at = lax.broadcasted_iota(jnp.int32, (384, 384), 0)
    row_at = lax.broadcasted_iota(jnp.int32, (384, 384), 1)
    causal = key_at <= row_at
    seen = key_at < prefix

    def as_bias(allowed):
        return jnp.where(allowed, 0.0, MASKED).astype(BF)

    s.mask[0:384, 0:384] = as_bias(causal & seen)
    s.mask[0:384, 384:768] = as_bias(seen)
    s.mask[384:768, 384:768] = as_bias(causal & (seg_wide == seg_tall))

    arrive(0, LAG_IN)

    def tile_sum(q):
        total = jnp.zeros((16, 128), F32)
        for xx in range(2):
            for who in range(2):
                total = total + s.small[q // 2, q % 2, xx, who].astype(F32)
        return total

    for q in range(8):
        s.vec[:, q * 128 : (q + 1) * 128] = tile_sum(q)[0:8]
    group_1 = lax.broadcasted_iota(jnp.int32, (1, 128), 1) // 32
    for block in range(4):
        tiles = [s.small[block, q // 2, q % 2, r].astype(F32)[8:9] for q in range(4)]
        for j in range(4):
            s.ebias[j, 0:1, block * 128 : (block + 1) * 128] = pick([tiles[(g + j) % 4] for g in range(4)], group_1)

    def vec_row(i):
        return s.vec[i : i + 1, :]

    pre_in(7, s.frames_all.at[o])

    def norm_tile(i, carry):
        who, rows = i // 3, pl.ds(pl.multiple_of((i % 3) * 128, 128), 128)
        unit, _ = centre(s.frames_all[who, rows].astype(F32))
        normed = unit * vec_row(0) + vec_row(1)
        s.n_all[who, rows] = normed.astype(BF)
        s.n1t[:, pl.ds(pl.multiple_of(i * 128, 128), 128)] = normed.T.astype(BF)
        return carry

    lax.fori_loop(0, 6, norm_tile, 0)

    def project(part):
        section, n = part // 2, part % 2
        mixed = dot(s.n_all[...].reshape(768, 1024), s.win[part].reshape(1024, 256))
        if section != 1:
            bias_at = pl.ds(pl.multiple_of(r * 512 + n * 256, 256), 256)
            bias_row = 2 if section == 0 else 3
            mixed = mixed + s.vec[bias_row : bias_row + 1, bias_at]
        mixed = mixed.astype(BF)
        s.qkv[section, 2 * n] = mixed[:, 0:128]
        s.qkv[section, 2 * n + 1] = mixed[:, 128:256]

    for part in range(6):
        arrive(1 + part, LAG_IN)
        project(part)

    factor = HD**-0.5 * LOG2E
    low_lane = lax.broadcasted_iota(jnp.int32, (128, 128), 1) < 64

    def pair_rows(block):
        zero = jnp.zeros_like(block)
        return jnp.concatenate([jnp.where(low_lane, block, zero), jnp.where(low_lane, zero, block)], axis=0)

    def pair_mask(keys, rb):
        bias = s.mask[0:keys, rb * 128 : (rb + 1) * 128].astype(F32)
        return jnp.concatenate([bias, bias], axis=1)

    def key_count(rb):
        return (rb + 1) * 128 if rb < 3 else 384 + (rb - 2) * 128

    def attend(hp, carry):
        v_t = flip(s.qkv[2, hp])
        dims = pl.ds(pl.multiple_of(hp * 128, 128), 128)
        for rb in range(6):
            keys = key_count(rb)
            both = pair_rows(s.qkv[0, hp, rb * 128 : (rb + 1) * 128])
            scores = dot_nt(s.qkv[1, hp, 0:keys], both) * factor + pair_mask(keys, rb)
            peak = jnp.max(scores, axis=0, keepdims=True)
            expo = jnp.exp2(scores - peak)
            total = jnp.sum(expo, axis=0, keepdims=True)
            heads = dot(v_t[:, 0:keys], expo.astype(BF)) / total
            s.lse[hp, rb] = jnp.broadcast_to(peak + jnp.log2(total), (8, 256))
            out = jnp.concatenate([heads[0:64, 0:128], heads[64:128, 128:256]], axis=0)
            at = (rb % 3) * 128
            s.half_t[rb // 3, dims, at : at + 128] = out.astype(BF)
            s.half[rb // 3, at : at + 128, dims] = out.T.astype(BF)
        return carry

    for j in range(4):
        pre[8 + j].wait_send()
    lax.fori_loop(0, 2, attend, 0)
    ahead(6 + LAG_IN + 1)
    lax.fori_loop(2, 4, attend, 0)
    ahead(6 + LAG_IN + 2)

    my_half = pl.ds(pl.multiple_of(r * 512, 512), 512)
    o_half = pl.ds(pl.multiple_of(o * 512, 512), 512)

    def core_copy(index, src, dst):
        return copy(src, dst, s.core_s.at[index], s.core_r.at[index], core_dev)

    core_copy(0, s.half.at[o], s.wide.at[:, my_half]).start()
    core_copy(1, s.half_t.at[o], s.att_t.at[my_half]).start()
    s.wide[:, my_half] = s.half[r]
    s.att_t[my_half] = s.half_t[r]
    arrive(7, LAG_FF)
    out_swap = core_copy(2, s.wout.at[:, :, :, r], s.wout.at[:, :, :, r])
    out_swap.start()
    core_copy(0, s.wide.at[:, o_half], s.wide.at[:, o_half]).wait_recv()
    core_copy(1, s.att_t.at[o_half], s.att_t.at[o_half]).wait_recv()
    core_copy(2, s.wout.at[:, :, :, o], s.wout.at[:, :, :, o]).wait_recv()
    def out_tile(n, carry):
        cols = pl.ds(pl.multiple_of(n * 256, 256), 256)
        branch = dot(s.wide[...], s.wout[:, :, :, :, :, cols].reshape(1024, 256))
        s.middle[:, cols] = s.frames_all[r, :, cols].astype(F32) + branch + s.vec[4:5, cols]
        return carry

    lax.fori_loop(0, 4, out_tile, 0)

    def norm_two(i, carry):
        rows = pl.ds(pl.multiple_of(i * 128, 128), 128)
        unit, _ = centre(s.middle[rows])
        s.n_all[r, rows] = (unit * vec_row(5) + vec_row(6)).astype(BF)
        return carry

    lax.fori_loop(0, 3, norm_two, 0)
    core_copy(3, s.n_all.at[r], s.n_all.at[r]).start()
    pre_in(12, s.c_all.at[o])
    s.out_acc[...] = jnp.zeros_like(s.out_acc)
    s.bn_acc[...] = jnp.zeros_like(s.bn_acc)
    core_copy(3, s.n_all.at[o], s.n_all.at[o]).wait_recv()
    core_copy(3, s.n_all.at[r], s.n_all.at[r]).wait_send()

    def flip_two(i, carry):
        who, rows = i // 3, pl.ds(pl.multiple_of((i % 3) * 128, 128), 128)
        s.n2t[:, pl.ds(pl.multiple_of(i * 128, 128), 128)] = flip(s.n_all[who, rows])
        return carry

    lax.fori_loop(0, 6, flip_two, 0)

    def rs_exp(j):
        return Bag(
            t=j, fin=j, split=True, piece=lambda a, b, c: s.wexp.at[j, a, b, c],
            col=lambda b, c: s.wexp.at[j, :, b, c], rb=lambda w: s.rb.at[j, w], ra=s.ra.at[j],
            rz=lambda k: s.rz.at[j, k], rx=lambda w: s.rx.at[j, w],
        )

    def rs_in(i):
        slot, part = ((0, 0), (0, 1), (1, 0), (1, 1), (2, 0), (2, 1))[i]
        half = slice(256 * part, 256 * part + 256)
        return Bag(
            t=9 + i, fin=4 + i, split=False, piece=lambda a, b, c: s.win.at[i, a, b, c],
            col=lambda b, c: s.win.at[i, :, b, c], rb=lambda w: s.rb.at[slot, w, :, :, half],
            ra=s.ra_in.at[i], rz=lambda k: s.rz_in.at[i, k],
        )

    def rs_red(j):
        split = bool(RED_SPLIT[j])
        return Bag(
            t=4 + j, fin=None, split=split, piece=lambda a, b, c: s.wred.at[j, a, slot(j, b, c)],
            col=lambda b, c: s.wred.at[j, :, slot(j, b, c)], rb=lambda w: s.rb_red.at[j, w],
            ra=s.land.at[j, 0] if split else s.land.at[j, 0:4],
            rz=lambda k: s.land.at[j, k + (1 if split else 4)], rx=lambda w: s.land.at[j, 7 + w],
        )

    def rs_out():
        return Bag(
            t=8, fin=None, split=False, piece=lambda a, b, c: s.wout.at[a, b, c, r],
            col=lambda b, c: s.wout.at[:, b, c, r], rb=lambda w: s.rb_out.at[w], ra=s.ra_out,
            rz=lambda k: s.rz_out.at[k],
        )

    def rs_small():
        return Bag(
            t=15, fin=None, split=False, piece=lambda a, b, c: s.sg.at[a, b, c],
            col=lambda b, c: s.sg.at[:, b, c], rb=lambda w: s.rb_sg.at[w], ra=s.ra_sg,
            rz=lambda k: s.rz_sg.at[k],
        )

    def rb_copy(it, which, yy, xx):
        return copy(it.col(yy, xx), it.rb(which), s.rsb_s.at[it.t, which], s.rsb_r.at[it.t, which], b_dev)

    def ra_copy(it):
        src = it.piece(z, ya, xa) if it.split else it.col(ya, xa)
        return copy(src, it.ra, s.rsa_s.at[it.t], s.rsa_r.at[it.t], a_dev)

    def add_into(it, yy, xx, sources):
        target = it.col(yy, xx)
        kind = F32 if it.t == 15 else BF

        def body(i, carry):
            total = target[i].astype(F32)
            for src in sources:
                total = total + src[i].astype(F32)
            target[i] = total.astype(kind)
            return carry

        lax.fori_loop(0, 4, body, 0)

    def own_copy(it, k, yy, xx, base, ss, rs):
        return copy(it.piece(z_at[k], yy, xx), it.rz(base + k), ss.at[it.t, k], rs.at[it.t, k], z_dev[k])

    def far_copy(it, k, yy, xx, which):
        return copy(
            it.piece(z_at[k], yy, xx), it.rx(which), s.rsx_s.at[it.t, which], s.rsx_r.at[it.t, which], near_middle
        )

    def own_start(it, yy, xx, base, ss, rs, which):
        for k in range(3):
            c = own_copy(it, k, yy, xx, base, ss, rs)
            if not it.split:
                c.start()
            elif k == 1:
                pl.when(at_end)(c.start)
            else:
                edge = 3 if k == 0 else 0
                pl.when(z != edge)(c.start)
                pl.when(z == edge)(far_copy(it, k, yy, xx, which).start)

    def own_relay(it, yy, xx, base, ss, rs, which):
        @pl.when(in_middle)
        def _():
            far_copy(it, 1, yy, xx, which).wait_recv()
            held = it.piece(z_at[1], yy, xx)
            held[...] = (held[...].astype(F32) + it.rx(which)[...].astype(F32)).astype(BF)
            own_copy(it, 1, yy, xx, base, ss, rs).start()

    def own_wait(it, yy, xx, base, ss, rs):
        for k in range(3):
            c = own_copy(it, k, yy, xx, base, ss, rs)
            if not it.split or k == 1:
                c.wait_recv()
            else:
                pl.when(z != (0 if k == 0 else 3))(c.wait_recv)

    def own_sent(it, yy, xx, base, ss, rs, which):
        for k in range(3):
            c = own_copy(it, k, yy, xx, base, ss, rs)
            if not it.split or k == 1:
                c.wait_send()
            else:
                edge = 3 if k == 0 else 0
                pl.when(z != edge)(c.wait_send)
                pl.when(z == edge)(far_copy(it, k, yy, xx, which).wait_send)

    def z_args(it, second):
        if second:
            return (ya, xa, 3, s.rsy_s, s.rsy_r)
        return (y, x, 0, s.rsz_s, s.rsz_r)

    def z_total(it, second):
        yy, xx, base, ss, rs = z_args(it, second)
        own_wait(it, yy, xx, base, ss, rs)
        total = it.piece(z, yy, xx)[...].astype(F32)
        for k in range(3):
            total = total + it.rz(base + k)[...].astype(F32)
        return total

    def f0(it):
        rb_copy(it, 0, yc, xc).start()
        rb_copy(it, 1, yb, xb).start()

    def f1(it):
        rb_copy(it, 0, yc, xc).wait_recv()
        add_into(it, ya, xa, [it.rb(0)])
        if not it.split:
            ra_copy(it).start()
            return
        own_start(it, *z_args(it, True), 1)
        rb_copy(it, 1, yb, xb).wait_recv()
        add_into(it, y, x, [it.rb(1)])
        own_start(it, *z_args(it, False), 0)

    def f2(it):
        if it.split:
            own_relay(it, *z_args(it, True), 1)
            own_relay(it, *z_args(it, False), 0)
            return
        rb_copy(it, 1, yb, xb).wait_recv()
        ra_copy(it).wait_recv()
        add_into(it, y, x, [it.rb(1), it.ra])
        own_start(it, *z_args(it, False), 0)

    def f3(it):
        if it.split:
            total = z_total(it, True)
            it.piece(z, ya, xa)[...] = total.astype(BF)
            ra_copy(it).start()

    def full_total(it):
        total = z_total(it, False)
        if it.split:
            ra_copy(it).wait_recv()
            total = total + it.ra[...].astype(F32)
        return total

    def fin_refs(index):
        if index < 4:
            return s.fin.at[index], s.fin_in.at[index]
        return s.fin_w.at[index - 4], s.fin_w_in.at[index - 4]

    def fin_copy(index):
        out, back = fin_refs(index)
        return copy(out.at[o_rows], back, s.fin_s.at[index], s.fin_r.at[index], core_dev)

    def small_fin():
        return copy(s.sfin, s.sfin_in, s.fin_s.at[10], s.fin_r.at[10], core_dev)

    def put_in(i, value, who):
        dwin_ref[:, part_cols(i, who)] = value

    def put_exp(source, who):
        for block in range(4):
            at = slice(block * 128, (block + 1) * 128)
            chunk = [source(j)[:, at] for j in range(4)]
            for q in range(4):
                cols = pl.ds(pl.multiple_of((2 * (4 * block + q) + who) * 128, 128), 128)
                dwexp_ref[:, cols] = pick([chunk[(q - g) % 4] for g in range(4)], group_32)

    def f4(it):
        if 4 <= it.t < 8:
            group = (place + 8 - it.t) % 4
            dwred_ref[pl.ds(pl.multiple_of(group * 32, 32), 32)] = full_total(it)
        elif it.t == 8:
            dwout_ref[...] = full_total(it)
        elif it.t == 15:
            s.sfin[...] = full_total(it)
            small_fin().start()
        else:
            out, _ = fin_refs(it.fin)
            out[...] = full_total(it)
            fin_copy(it.fin).start()
            if it.fin >= 4:
                put_in(it.fin - 4, out[my_rows], r)

    def f5(it):
        if it.fin is not None:
            fin_copy(it.fin).wait_recv()
            if it.fin >= 4:
                put_in(it.fin - 4, fin_refs(it.fin)[1][...], o)
            elif it.fin == 3:
                put_exp(lambda j: s.fin[j, my_rows], r)
                put_exp(lambda j: s.fin_in[j], o)
        elif it.t == 15:
            small_fin().wait_recv()
            row = lax.broadcasted_iota(jnp.int32, (16, 128), 0)
            own = s.sfin[...]
            dsmall_ref[...] = jnp.where(row < 8, own + s.sfin_in[...], own)

    def all_sent(it):
        rb_copy(it, 0, yc, xc).wait_send()
        rb_copy(it, 1, yb, xb).wait_send()
        ra_copy(it).wait_send()
        own_sent(it, *z_args(it, False), 0)
        if it.split:
            own_sent(it, *z_args(it, True), 1)
        if it.fin is not None:
            fin_copy(it.fin).wait_send()
        elif it.t == 15:
            small_fin().wait_send()

    order = []
    for j in range(4):
        order += [rs_red(j), rs_exp(j)]
    order += [rs_out()] + [rs_in(i) for i in range(6)] + [rs_small()]

    def step(i):
        for event, lag in ((f0, -LEAD), (f1, 1), (f2, 2), (f3, 3), (f4, 4), (f5, 5)):
            if 0 <= i - lag < len(order):
                event(order[i - lag])

    stepped = []

    def next_step():
        step(len(stepped))
        stepped.append(True)

    def feed(j, between):
        if j == 3 and EARLY_CHUNK == 3:
            for it in order[:LEAD]:
                f0(it)
        arrive(8 + 2 * j, LAG_FF)
        arrive(9 + 2 * j, LAG_FF)
        sent(gathers[8 + 2 * j])
        sent(gathers[9 + 2 * j])
        between(0)

        def hidden(n, inside):
            cols = pl.ds(pl.multiple_of(n * 256, 256), 256)
            left = s.n_all[...].reshape(768, 1024)
            inner = dot(left, s.wexp[j, :, :, :, :, cols].reshape(1024, 256)) + s.ebias[j, 0:1, cols]
            phi = 0.5 + 0.5 * lax.erf(inner * (2.0**-0.5))
            active = inner * phi
            s.ffb[0, :, cols] = active.astype(BF)
            s.act_t[cols] = active.T.astype(BF)
            slope = phi + inner * (jnp.exp(-0.5 * inner * inner) * 0.3989422804014327)
            up = s.c_all[...].reshape(768, 1024)
            weight = s.wred[j, pl.ds(2 * n, 2)].reshape(256, 1024)
            back = (dot_nt(up, weight) * slope).astype(BF)
            s.ffb[1, :, cols] = back
            s.gexp[j, 0:1, cols] = jnp.sum(back.astype(F32), axis=0, keepdims=True)
            return inside

        lax.fori_loop(0, 2, hidden, 0)

        def wide_tile(n, inside):
            cols = pl.ds(pl.multiple_of(n * 256, 256), 256)
            part = dot(s.ffb[0], s.wred[j, :, :, :, cols].reshape(512, 256))
            s.out_acc[:, :, cols] += part.reshape(2, 384, 256)
            back = dot_nt(s.ffb[1], s.wexp[j, n].reshape(256, 512))
            s.bn_acc[:, :, cols] += back.reshape(2, 384, 256)
            return inside

        ahead(9 + 2 * j + LAG_FF + 1)
        if j == EARLY_CHUNK == 2:
            for it in order[:LEAD]:
                f0(it)
        lax.fori_loop(0, 4, wide_tile, 0)
        between(1)

        def grad_red(n, inside):
            cols = pl.ds(pl.multiple_of(n * 256, 256), 256)
            up = s.c_all[:, :, cols].reshape(768, 256)
            s.wred[j, :, :, :, cols] = dot(s.act_t[...], up).astype(BF).reshape(4, 4, 32, 256)
            return inside

        lax.fori_loop(0, 4, grad_red, 0)

        def grad_exp(n, inside):
            cols = pl.ds(pl.multiple_of(n * 256, 256), 256)
            grad = dot(s.n2t[...], s.ffb[1, :, cols]).astype(BF)
            s.wexp[j, :, :, :, :, cols] = grad.reshape(4, 2, 2, 64, 256)
            return inside

        lax.fori_loop(0, 2, grad_exp, 0)
        between(2)

    for j in range(3):
        feed(j, lambda place: None)

    def start_reduction(place_in):
        if place_in == 0:
            next_step()
        elif place_in == 1:
            core_copy(4, s.bn_acc.at[o], s.cross).start()
            next_step()
        else:
            next_step()

    feed(3, start_reduction)

    core_copy(4, s.bn_acc.at[o], s.cross).wait_recv()
    s.n_all[o] = s.out_acc[o].astype(BF)
    core_copy(5, s.n_all.at[o], s.n_all.at[o]).start()

    def middle_back(i, carry):
        rows = pl.ds(pl.multiple_of(i * 128, 128), 128)
        unit, rate = centre(s.middle[rows])
        upstream = s.bn_acc[r, rows] + s.cross[rows]
        cot = s.c_all[r, rows].astype(F32)
        back = cot + norm_back(unit, rate, vec_row(5), upstream)
        s.bn_acc[r, rows] = back
        branch = back.astype(BF)
        s.wide[rows] = branch
        gain_t, shift_t, out_t, red_t = carry
        return (
            gain_t + jnp.sum(upstream * unit, axis=0, keepdims=True),
            shift_t + jnp.sum(upstream, axis=0, keepdims=True),
            out_t + jnp.sum(branch.astype(F32), axis=0, keepdims=True),
            red_t + jnp.sum(cot, axis=0, keepdims=True),
        )

    zero_row = jnp.zeros((1, 1024), F32)
    gain_t, shift_t, out_t, red_t = lax.fori_loop(0, 3, middle_back, (zero_row,) * 4)
    s.gvec[5:6] = gain_t
    s.gvec[6:7] = shift_t
    s.gvec[4:5] = out_t
    s.gvec[7:8] = red_t

    core_copy(0, s.half.at[o], s.half.at[o]).wait_send()
    core_copy(2, s.wout.at[:, :, :, r], s.wout.at[:, :, :, r]).wait_send()

    def back_att(n, carry):
        weight = s.wout[n].reshape(256, 1024)
        cols = pl.ds(pl.multiple_of((n % 2) * 256, 256), 256)
        s.half[n // 2, :, cols] = dot_nt(s.wide[...], weight).astype(BF)
        return carry

    lax.fori_loop(0, 4, back_att, 0)
    core_copy(6, s.half.at[o], s.ba_all.at[r]).start()
    s.ba_all[r] = s.half[r]
    next_step()
    sent(gathers[7])

    def grad_out(n, carry):
        cols = pl.ds(pl.multiple_of(n * 256, 256), 256)
        grad = dot(s.att_t[...], s.wide[:, cols]).astype(BF)
        s.wout[:, :, :, :, :, cols] = grad.reshape(4, 2, 2, 2, 32, 256)
        return carry

    lax.fori_loop(0, 4, grad_out, 0)
    core_copy(7, s.wout.at[:, :, :, o], s.outx).start()
    core_copy(5, s.n_all.at[r], s.n_all.at[r]).wait_recv()

    def result_tile(i, carry):
        rows = pl.ds(pl.multiple_of(i * 128, 128), 128)
        total = s.middle[rows] + s.out_acc[r, rows] + s.n_all[r, rows].astype(F32) + vec_row(7)
        result_ref[rows] = total.astype(BF)
        return carry

    lax.fori_loop(0, 3, result_tile, 0)
    core_copy(6, s.ba_all.at[o], s.ba_all.at[o]).wait_recv()

    def attend_back(hp, carry):
        k_t = flip(s.qkv[1, hp])
        dims = pl.ds(pl.multiple_of(hp * 128, 128), 128)
        s.dkv[...] = jnp.zeros_like(s.dkv)
        for rb in range(6):
            keys = key_count(rb)
            rows = slice(rb * 128, (rb + 1) * 128)
            both = pair_rows(s.qkv[0, hp, rows])
            at = (rb % 3) * 128
            up = pair_rows(s.ba_all[rb // 3, at : at + 128, dims])
            scores = dot_nt(s.qkv[1, hp, 0:keys], both) * factor + pair_mask(keys, rb)
            probs = jnp.exp2(scores - s.lse[hp, rb, 0:1])
            back_probs = dot_nt(s.qkv[2, hp, 0:keys], up)
            weighted = probs * back_probs
            centre_row = jnp.sum(weighted, axis=0, keepdims=True)
            back_scores = (weighted - probs * centre_row).astype(BF)
            s.dkv[1, 0:keys] += dot(probs.astype(BF), up)
            s.dkv[0, 0:keys] += dot(back_scores, both)
            query = dot(k_t[:, 0:keys], back_scores)
            query = jnp.concatenate([query[0:64, 0:128], query[64:128, 128:256]], axis=0)
            s.ffb[0, rows, dims] = (query.T * HD**-0.5).astype(BF)
        s.ffb[1, :, dims] = (s.dkv[0] * HD**-0.5).astype(BF)
        s.ffb[2, :, dims] = s.dkv[1].astype(BF)
        return carry

    core_copy(7, s.outx, s.outx).wait_recv()

    def add_out(i, carry):
        for yy in range(2):
            for xx in range(2):
                total = s.wout[i, yy, xx, r].astype(F32) + s.outx[i, yy, xx].astype(F32)
                s.wout[i, yy, xx, r] = total.astype(BF)
        return carry

    lax.fori_loop(0, 4, add_out, 0)

    lax.fori_loop(0, 1, attend_back, 0)
    next_step()
    lax.fori_loop(1, 3, attend_back, 0)
    next_step()
    lax.fori_loop(3, 4, attend_back, 0)

    core_copy(5, s.n_all.at[o], s.n_all.at[o]).wait_send()

    def back_in(n, carry):
        cols = pl.ds(pl.multiple_of(n * 256, 256), 256)
        total = dot_nt(s.ffb[0, :, 0:256], s.win[0, n].reshape(256, 256))
        for part in range(1, 6):
            at = (part % 2) * 256
            total = total + dot_nt(s.ffb[part // 2, :, at : at + 256], s.win[part, n].reshape(256, 256))
        s.out_acc[:, :, cols] = total.reshape(2, 384, 256)
        return carry

    lax.fori_loop(0, 4, back_in, 0)
    core_copy(8, s.out_acc.at[o], s.cross).start()
    next_step()
    for part in range(6):
        sent(gathers[1 + part])
        at = (part % 2) * 256
        grad = dot(s.n1t[...], s.ffb[part // 2, :, at : at + 256]).astype(BF)
        s.win[part] = grad.reshape(4, 2, 2, 64, 256)
        if part == 2:
            next_step()
    next_step()
    next_step()

    core_copy(8, s.out_acc.at[o], s.cross).wait_recv()

    def frame_back(i, carry):
        rows = pl.ds(pl.multiple_of(i * 128, 128), 128)
        unit, rate = centre(s.frames_all[r, rows].astype(F32))
        upstream = s.out_acc[r, rows] + s.cross[rows]
        back = s.bn_acc[r, rows] + norm_back(unit, rate, vec_row(0), upstream)
        fgrad_ref[rows] = back.astype(BF)
        gain_t, shift_t = carry
        return (
            gain_t + jnp.sum(upstream * unit, axis=0, keepdims=True),
            shift_t + jnp.sum(upstream, axis=0, keepdims=True),
        )

    gain_t, shift_t = lax.fori_loop(0, 3, frame_back, (zero_row,) * 2)
    s.gvec[0:1] = gain_t
    s.gvec[1:2] = shift_t
    s.gvec[2:4] = jnp.zeros((2, 1024), F32)
    s.gvec[2:3, my_half] = jnp.sum(s.ffb[0].astype(F32), axis=0, keepdims=True)
    s.gvec[3:4, my_half] = jnp.sum(s.ffb[2].astype(F32), axis=0, keepdims=True)
    s.sg[...] = jnp.zeros_like(s.sg)
    for zz in range(4):
        for yy in range(2):
            for xx in range(2):
                at = (zz * 2 + yy) * 128
                s.sg[zz, yy, xx, 0:8] = s.gvec[:, at : at + 128]
                q = 2 * yy + xx
                block = slice(zz * 128, (zz + 1) * 128)
                chunk = [s.gexp[j, 0:1, block] for j in range(4)]
                s.sg[zz, yy, xx, 8:9] = pick([chunk[(q - g) % 4] for g in range(4)], group_1)

    while len(stepped) < len(order) + 5:
        next_step()

    for i, item in enumerate(pre):
        if not 8 <= i < 12:
            item.wait_send()
    sent(gathers[0])
    core_copy(1, s.half_t.at[o], s.half_t.at[o]).wait_send()
    core_copy(4, s.bn_acc.at[o], s.cross).wait_send()
    core_copy(6, s.half.at[o], s.ba_all.at[r]).wait_send()
    core_copy(7, s.wout.at[:, :, :, o], s.outx).wait_send()
    core_copy(8, s.out_acc.at[o], s.cross).wait_send()
    for it in order:
        all_sent(it)


def hand_on(*refs):
    given, taken, held = refs[0:6], refs[6:12], refs[12:18]
    sems = refs[18]
    inward = [pltpu.make_async_copy(given[i], held[i], sems.at[0, i]) for i in range(6)]
    outward = [pltpu.make_async_copy(held[i], taken[i], sems.at[1, i]) for i in range(6)]
    for item in inward:
        item.start()
    for i in range(6):
        inward[i].wait()
        outward[i].start()
    for item in outward:
        item.wait()


def fused_shards(
    frames, frames_cotangent, phoneme_len, prompt_len, target_segment, first_gain, first_shift, inward_weight,
    query_bias, value_bias, outward_weight, outward_bias, second_gain, second_shift, expand_weight, expand_bias,
    reduce_weight, reduce_bias,
):
    number = lax.axis_index("dp") * 2 + lax.axis_index("role")
    quarter = number % 4
    rows = jnp.stack(
        [first_gain, first_shift, query_bias, value_bias, outward_bias, second_gain, second_shift, reduce_bias]
    )
    lane = jnp.arange(128) // 32
    rows = jnp.where(lane[None] == quarter, jnp.tile(rows, (1, 4)), jnp.zeros((), BF))
    small = jnp.concatenate([rows, expand_bias[None], jnp.zeros((7, 128), BF)], axis=0)

    scratch = scratch_list()
    vmem = pl.BlockSpec(memory_space=pltpu.VMEM)
    smem = pl.BlockSpec(memory_space=pltpu.SMEM)
    hbm = pl.BlockSpec(memory_space=pl.ANY)
    outs = pl.pallas_call(
        functools.partial(layer_kernel, tuple(scratch)),
        out_shape=[
            jax.ShapeDtypeStruct((384, 1024), BF),
            jax.ShapeDtypeStruct((384, 1024), BF),
            jax.ShapeDtypeStruct((32, 3072), F32),
            jax.ShapeDtypeStruct((32, 1024), F32),
            jax.ShapeDtypeStruct((32, 4096), F32),
            jax.ShapeDtypeStruct((128, 1024), F32),
            jax.ShapeDtypeStruct((16, 128), F32),
        ],
        in_specs=[smem, smem, vmem, hbm, hbm] + [vmem] * 5,
        out_specs=[vmem] * 7,
        scratch_shapes=list(scratch.values()),
        compiler_params=pltpu.CompilerParams(
            collective_id=0, has_side_effects=True, vmem_limit_bytes=62 * 1024 * 1024
        ),
    )(
        phoneme_len, prompt_len, target_segment, frames[0], frames_cotangent[0], small, inward_weight,
        outward_weight, expand_weight, reduce_weight,
    )
    d_small = outs[6]
    result, frames_gradient, d_in, d_out, d_exp, d_red = pl.pallas_call(
        hand_on,
        out_shape=[jax.ShapeDtypeStruct(item.shape, item.dtype) for item in outs[:6]],
        in_specs=[hbm] * 6,
        out_specs=[hbm] * 6,
        scratch_shapes=[pltpu.VMEM(item.shape, item.dtype) for item in outs[:6]]
        + [pltpu.SemaphoreType.DMA((2, 6))],
    )(*outs[:6])
    mine = lax.dynamic_slice(d_small, (0, quarter * 32), (8, 32))
    return (
        result[None], frames_gradient[None], mine[0], mine[1], d_in, mine[2], mine[3], d_out, mine[4], mine[5],
        mine[6], d_exp, d_small[8], d_red, mine[7],
    )


def passed_along(block, axis, distance):
    devices = range(lax.axis_size(axis))
    route = [(i - distance, i) for i in devices if i - distance in devices]
    return lax.ppermute(block, axis, route)


def normalize(values, gain, shift):
    mean_value = jnp.mean(values, axis=-1, keepdims=True)
    centered = values - mean_value
    spread = jnp.mean(centered * centered, axis=-1, keepdims=True)
    return centered * lax.rsqrt(spread + EPS) * gain + shift


def smooth_gate(values):
    return jax.nn.gelu(values, approximate=False)


def inner_rows(left, right):
    return lax.dot_general(
        left, right, (((0,), (0,)), ((), ())), preferred_element_type=jnp.float32
    )


def outer_cols(left, right):
    return lax.dot_general(
        left, right, (((1,), (1,)), ((), ())), preferred_element_type=jnp.float32
    )


def plain_shards(
    frames,
    frames_cotangent,
    phoneme_len,
    prompt_len,
    target_segment,
    first_gain,
    first_shift,
    inward_weight,
    query_bias,
    value_bias,
    outward_weight,
    outward_bias,
    second_gain,
    second_shift,
    expand_weight,
    expand_bias,
    reduce_weight,
    reduce_bias,
):
    attention_part = (
        lax.all_gather(first_gain, ("dp", "role"), axis=0, tiled=True),
        lax.all_gather(first_shift, ("dp", "role"), axis=0, tiled=True),
        lax.all_gather(inward_weight, ("dp", "role"), axis=0, tiled=True),
        lax.all_gather(query_bias, ("dp", "role"), axis=0, tiled=True),
        lax.all_gather(value_bias, ("dp", "role"), axis=0, tiled=True),
        lax.all_gather(outward_weight, ("dp", "role"), axis=0, tiled=True),
        lax.all_gather(outward_bias, ("dp", "role"), axis=0, tiled=True),
    )
    (
        full_gain,
        full_shift,
        full_inward,
        full_query_bias,
        full_value_bias,
        full_outward,
        full_outward_bias,
    ) = attention_part
    side = lax.axis_index("role")
    local_rows = frames.shape[1]
    scale = HD ** (-0.5)
    current = frames[0].astype(jnp.float32)
    normed = normalize(
        current, full_gain.astype(jnp.float32), full_shift.astype(jnp.float32)
    ).astype(jnp.bfloat16)
    mixed = jnp.dot(normed, full_inward, preferred_element_type=jnp.float32)
    queries = (mixed[:, :D] + full_query_bias.astype(jnp.float32)).astype(jnp.bfloat16)
    keys_own = mixed[:, D : 2 * D].astype(jnp.bfloat16)
    values_own = (mixed[:, 2 * D :] + full_value_bias.astype(jnp.float32)).astype(jnp.bfloat16)
    remote_keys, remote_values = passed_along((keys_own, values_own), "role", 1)
    keys_all = jnp.concatenate([remote_keys, keys_own], axis=0)
    values_all = jnp.concatenate([remote_values, values_own], axis=0)
    row_index = jnp.arange(local_rows)[:, None]
    col_index = jnp.arange(2 * local_rows)[None, :]
    own_col = col_index - local_rows
    prefix_length = phoneme_len[0] + prompt_len[0]
    segment = target_segment[0]
    key_segment = jnp.concatenate([jnp.full((local_rows,), -1, jnp.int32), segment])
    prompt_rows = (own_col >= 0) & (own_col <= row_index) & (own_col < prefix_length)
    target_rows = (col_index < prefix_length) | (own_col >= 0) & (own_col <= row_index) & (
        key_segment[None, :] == segment[:, None]
    )
    allowed = jnp.where(side == 0, prompt_rows, target_rows)

    def attend(index):
        start = index * HD
        head_query = lax.dynamic_slice_in_dim(queries, start, HD, 1)
        head_key = lax.dynamic_slice_in_dim(keys_all, start, HD, 1)
        head_value = lax.dynamic_slice_in_dim(values_all, start, HD, 1)
        scores = outer_cols(head_query, head_key) * scale
        masked = jnp.where(allowed, scores, MASKED)
        peak = jnp.max(masked, axis=1, keepdims=True)
        expo = jnp.exp(masked - peak)
        total = jnp.sum(expo, axis=1, keepdims=True)
        probs = (expo / total).astype(jnp.bfloat16)
        return (
            jnp.dot(probs, head_value, preferred_element_type=jnp.float32),
            (peak + jnp.log(total))[:, 0],
        )

    head_outs, log_totals = lax.map(attend, jnp.arange(H))
    attended = head_outs.transpose(1, 0, 2).reshape(local_rows, D).astype(jnp.bfloat16)
    middle = (
        current
        + jnp.dot(attended, full_outward, preferred_element_type=jnp.float32)
        + full_outward_bias.astype(jnp.float32)
    )
    feed_part = (
        lax.all_gather(second_gain, ("dp", "role"), axis=0, tiled=True),
        lax.all_gather(second_shift, ("dp", "role"), axis=0, tiled=True),
        lax.all_gather(expand_weight, ("dp", "role"), axis=0, tiled=True),
        lax.all_gather(expand_bias, ("dp", "role"), axis=0, tiled=True),
        lax.all_gather(reduce_weight, ("dp", "role"), axis=0, tiled=True),
        lax.all_gather(reduce_bias, ("dp", "role"), axis=0, tiled=True),
    )
    full_gain_two, full_shift_two, full_expand, full_expand_bias, full_reduce, full_reduce_bias = (
        feed_part
    )
    gain_two = full_gain_two.astype(jnp.float32)
    shift_two = full_shift_two.astype(jnp.float32)
    normed_two = normalize(middle, gain_two, shift_two).astype(jnp.bfloat16)
    inner = jnp.dot(
        normed_two, full_expand, preferred_element_type=jnp.float32
    ) + full_expand_bias.astype(jnp.float32)
    active = smooth_gate(inner).astype(jnp.bfloat16)
    output = (
        middle
        + jnp.dot(active, full_reduce, preferred_element_type=jnp.float32)
        + full_reduce_bias.astype(jnp.float32)
    )
    result = output.astype(jnp.bfloat16)[None]
    again_expand = feed_part[2]
    again_reduce = feed_part[4]
    again_gain = attention_part[0].astype(jnp.float32)
    again_shift = attention_part[1].astype(jnp.float32)
    again_inward = attention_part[2]
    again_outward = attention_part[5]
    upstream = frames_cotangent[0]
    upstream_float = upstream.astype(jnp.float32)
    reduce_bias_term = jnp.sum(upstream_float, axis=0)
    reduce_weight_term = inner_rows(active, upstream)
    back_active = outer_cols(upstream, again_reduce)
    gate_pull = jax.vjp(smooth_gate, inner)[1]
    back_inner = gate_pull(back_active)[0].astype(jnp.bfloat16)
    expand_bias_term = jnp.sum(back_inner.astype(jnp.float32), axis=0)
    expand_weight_term = inner_rows(normed_two, back_inner)
    back_normed_two = outer_cols(back_inner, again_expand)
    second_pull = jax.vjp(normalize, middle, gain_two, shift_two)[1]
    middle_part, second_gain_term, second_shift_term = second_pull(back_normed_two)
    back_middle = upstream_float + middle_part
    back_branch = back_middle.astype(jnp.bfloat16)
    outward_bias_term = jnp.sum(back_branch.astype(jnp.float32), axis=0)
    outward_weight_term = inner_rows(attended, back_branch)
    back_attended = outer_cols(back_branch, again_outward).astype(jnp.bfloat16)

    def attend_back(inputs):
        index, log_total = inputs
        start = index * HD
        head_query = lax.dynamic_slice_in_dim(queries, start, HD, 1)
        head_key = lax.dynamic_slice_in_dim(keys_all, start, HD, 1)
        head_value = lax.dynamic_slice_in_dim(values_all, start, HD, 1)
        head_upstream = lax.dynamic_slice_in_dim(back_attended, start, HD, 1)
        scores = outer_cols(head_query, head_key) * scale
        probs = jnp.where(allowed, jnp.exp(scores - log_total[:, None]), 0.0)
        back_probs = outer_cols(head_upstream, head_value)
        centre = jnp.sum(probs * back_probs, axis=1, keepdims=True)
        back_scores = (probs * (back_probs - centre)).astype(jnp.bfloat16)
        back_query = jnp.dot(back_scores, head_key, preferred_element_type=jnp.float32) * scale
        back_key = inner_rows(back_scores, head_query) * scale
        back_value = inner_rows(probs.astype(jnp.bfloat16), head_upstream)
        return (back_query, back_key, back_value)

    head_query_grads, head_key_grads, head_value_grads = lax.map(
        attend_back, (jnp.arange(H), log_totals)
    )
    back_queries = head_query_grads.transpose(1, 0, 2).reshape(local_rows, D)
    back_keys_all = head_key_grads.transpose(1, 0, 2).reshape(2 * local_rows, D)
    back_values_all = head_value_grads.transpose(1, 0, 2).reshape(2 * local_rows, D)
    returned_keys, returned_values = (
        passed_along(back_keys_all[:local_rows].astype(jnp.bfloat16), "role", -1).astype(
            jnp.float32
        ),
        passed_along(back_values_all[:local_rows].astype(jnp.bfloat16), "role", -1).astype(
            jnp.float32
        ),
    )
    query_low = back_queries.astype(jnp.bfloat16)
    key_low = (back_keys_all[local_rows:] + returned_keys).astype(jnp.bfloat16)
    value_low = (back_values_all[local_rows:] + returned_values).astype(jnp.bfloat16)
    back_mixed = jnp.concatenate([query_low, key_low, value_low], axis=1)
    query_bias_term = jnp.sum(query_low.astype(jnp.float32), axis=0)
    value_bias_term = jnp.sum(value_low.astype(jnp.float32), axis=0)
    inward_weight_term = inner_rows(normed, back_mixed)
    back_normed = outer_cols(back_mixed, again_inward)
    first_pull = jax.vjp(normalize, current, again_gain, again_shift)[1]
    frame_part, first_gain_term, first_shift_term = first_pull(back_normed)
    frames_gradient = (back_middle + frame_part).astype(jnp.bfloat16)[None]
    totals = (
        lax.psum_scatter(first_gain_term, ("dp", "role"), scatter_dimension=0, tiled=True),
        lax.psum_scatter(first_shift_term, ("dp", "role"), scatter_dimension=0, tiled=True),
        lax.psum_scatter(inward_weight_term, ("dp", "role"), scatter_dimension=0, tiled=True),
        lax.psum_scatter(query_bias_term, ("dp", "role"), scatter_dimension=0, tiled=True),
        lax.psum_scatter(value_bias_term, ("dp", "role"), scatter_dimension=0, tiled=True),
        lax.psum_scatter(outward_weight_term, ("dp", "role"), scatter_dimension=0, tiled=True),
        lax.psum_scatter(outward_bias_term, ("dp", "role"), scatter_dimension=0, tiled=True),
        lax.psum_scatter(second_gain_term, ("dp", "role"), scatter_dimension=0, tiled=True),
        lax.psum_scatter(second_shift_term, ("dp", "role"), scatter_dimension=0, tiled=True),
        lax.psum_scatter(expand_weight_term, ("dp", "role"), scatter_dimension=0, tiled=True),
        lax.psum_scatter(expand_bias_term, ("dp", "role"), scatter_dimension=0, tiled=True),
        lax.psum_scatter(reduce_weight_term, ("dp", "role"), scatter_dimension=0, tiled=True),
        lax.psum_scatter(reduce_bias_term, ("dp", "role"), scatter_dimension=0, tiled=True),
    )
    return (
        result,
        frames_gradient,
        totals[0],
        totals[1],
        totals[2],
        totals[3],
        totals[4],
        totals[5],
        totals[6],
        totals[7],
        totals[8],
        totals[9],
        totals[10],
        totals[11],
        totals[12],
    )


def solution(mesh):
    placed = (
        P("dp", "role", None),
        P("dp", "role", None),
        P("dp"),
        P("dp"),
        P("dp", None),
        P(("dp", "role")),
        P(("dp", "role")),
        P(("dp", "role"), None),
        P(("dp", "role")),
        P(("dp", "role")),
        P(("dp", "role"), None),
        P(("dp", "role")),
        P(("dp", "role")),
        P(("dp", "role")),
        P(("dp", "role"), None),
        P(("dp", "role")),
        P(("dp", "role"), None),
        P(("dp", "role")),
    )
    fused = mesh.shape["dp"] == 16 and mesh.shape["role"] == 2
    return jax.shard_map(
        fused_shards if fused else plain_shards,
        mesh=mesh,
        in_specs=placed,
        out_specs=(
            P("dp", "role", None),
            P("dp", "role", None),
            P(("dp", "role")),
            P(("dp", "role")),
            P(("dp", "role"), None),
            P(("dp", "role")),
            P(("dp", "role")),
            P(("dp", "role"), None),
            P(("dp", "role")),
            P(("dp", "role")),
            P(("dp", "role")),
            P(("dp", "role"), None),
            P(("dp", "role")),
            P(("dp", "role"), None),
            P(("dp", "role")),
        ),
        check_vma=False,
    )
```

```python
import functools

import jax
import jax.numpy as jnp
from jax import lax
from jax.experimental import pallas as pl
from jax.experimental.pallas import tpu as pltpu
from jax.sharding import PartitionSpec as P

D = 1024
H = 16
HD = 64
EPS = 1e-05
MASKED = -1e30
LOG2E = 1.4426950408889634
BF = jnp.bfloat16
F32 = jnp.float32
MESH = pl.DeviceIdType.MESH


def dot(left, right):
    return lax.dot_general(left, right, (((1,), (0,)), ((), ())), preferred_element_type=F32)


def dot_nt(left, right):
    return lax.dot_general(left, right, (((1,), (1,)), ((), ())), preferred_element_type=F32)


def flip(value):
    return value.astype(F32).T.astype(value.dtype)


def centre(values):
    mean_value = jnp.mean(values, axis=-1, keepdims=True)
    centered = values - mean_value
    spread = jnp.mean(centered * centered, axis=-1, keepdims=True)
    return centered * lax.rsqrt(spread + EPS), lax.rsqrt(spread + EPS)


def norm_back(unit, rate, gain, upstream):
    pulled = upstream * gain
    first = jnp.mean(pulled, axis=-1, keepdims=True)
    second = jnp.mean(pulled * unit, axis=-1, keepdims=True)
    return rate * (pulled - first - unit * second)


LEAD = 1
EARLY_CHUNK = 2
LOOK = 2
LAG_IN = 7
LAG_FF = 7
RED_SPLIT = (0, 0, 0, 0)


def scratch_list():
    dma = pltpu.SemaphoreType.DMA
    v = pltpu.VMEM
    return dict(
        small=v((4, 2, 2, 2, 16, 128), BF),
        vec=v((8, 1024), F32),
        ebias=v((4, 8, 512), F32),
        frames_all=v((2, 384, 1024), BF),
        c_all=v((2, 384, 1024), BF),
        n_all=v((2, 384, 1024), BF),
        n1t=v((1024, 768), BF),
        n2t=v((1024, 768), BF),
        win=v((6, 4, 2, 2, 64, 256), BF),
        wout=v((4, 2, 2, 2, 32, 1024), BF),
        wexp=v((4, 4, 2, 2, 64, 512), BF),
        wred=v((4, 4, 4, 32, 1024), BF),
        qkv=v((3, 4, 768, 128), BF),
        mask=v((768, 768), BF),
        lse=v((4, 6, 8, 256), F32),
        half=v((2, 384, 512), BF),
        half_t=v((2, 512, 384), BF),
        wide=v((384, 1024), BF),
        att_t=v((1024, 384), BF),
        middle=v((384, 1024), F32),
        out_acc=v((2, 384, 1024), F32),
        bn_acc=v((2, 384, 1024), F32),
        cross=v((384, 1024), F32),
        ffb=v((3, 768, 512), BF),
        act_t=v((512, 768), BF),
        ba_all=v((2, 384, 512), BF),
        dkv=v((2, 768, 128), F32),
        gvec=v((8, 1024), F32),
        gexp=v((4, 8, 512), F32),
        outx=v((4, 2, 2, 32, 1024), BF),
        rb=v((4, 2, 4, 64, 512), BF),
        ra=v((4, 64, 512), BF),
        rz=v((4, 6, 64, 512), BF),
        rx=v((4, 2, 64, 512), BF),
        ra_in=v((6, 4, 64, 256), BF),
        rz_in=v((6, 3, 64, 256), BF),
        rb_red=v((4, 2, 4, 32, 1024), BF),
        land=v((4, 7, 32, 1024), BF),
        rb_out=v((2, 4, 32, 1024), BF),
        ra_out=v((4, 32, 1024), BF),
        rz_out=v((3, 32, 1024), BF),
        sg=v((4, 2, 2, 16, 128), F32),
        rb_sg=v((2, 4, 16, 128), F32),
        ra_sg=v((4, 16, 128), F32),
        rz_sg=v((3, 16, 128), F32),
        fin=v((4, 64, 512), F32),
        fin_in=v((4, 32, 512), F32),
        fin_w=v((6, 64, 256), F32),
        fin_w_in=v((6, 32, 256), F32),
        sfin=v((16, 128), F32),
        sfin_in=v((16, 128), F32),
        own_s=dma((7,)),
        pre_s=dma((13,)),
        pre_r=dma((13,)),
        agz_s=dma((16, 3)),
        agz_r=dma((16, 3)),
        agy_s=dma((16, 3)),
        agy_r=dma((16, 3)),
        agx_s=dma((16, 2)),
        aga_s=dma((16,)),
        aga_r=dma((16,)),
        agb_s=dma((16, 2)),
        agb_r=dma((16, 2)),
        core_s=dma((9,)),
        core_r=dma((9,)),
        rsb_s=dma((16, 2)),
        rsb_r=dma((16, 2)),
        rsa_s=dma((16,)),
        rsa_r=dma((16,)),
        rsz_s=dma((16, 3)),
        rsz_r=dma((16, 3)),
        rsy_s=dma((16, 3)),
        rsy_r=dma((16, 3)),
        rsx_s=dma((16, 2)),
        rsx_r=dma((16, 2)),
        fin_s=dma((11,)),
        fin_r=dma((11,)),
    )


class Bag:
    def __init__(self, **kw):
        self.__dict__.update(kw)


N_IN = 10
N_OUT = 7


def layer_kernel(names, *refs):
    (phon_ref, prom_ref, seg_ref, frames_ref, cot_ref, small_in, win_in, wout_in, wexp_in, wred_in) = refs[:N_IN]
    (result_ref, fgrad_ref, dwin_ref, dwout_ref, dwexp_ref, dwred_ref, dsmall_ref) = refs[N_IN : N_IN + N_OUT]
    s = Bag(**dict(zip(names, refs[N_IN + N_OUT :])))

    dp = lax.axis_index("dp")
    r = lax.axis_index("role")
    o = 1 - r
    z, y, x = dp // 4, (dp // 2) % 2, dp % 2
    ya, xa = y + r * (1 - 2 * y), x + (1 - r) * (1 - 2 * x)
    yb, xb = y + (1 - r) * (1 - 2 * y), x + r * (1 - 2 * x)
    yc, xc = 1 - y, 1 - x
    core_dev = (dp, o)
    a_dev = (z * 4 + ya * 2 + xa, r)
    b_dev = (z * 4 + yb * 2 + xb, r)
    z_dev = [(((z + k) % 4) * 4 + y * 2 + x, r) for k in (1, 2, 3)]
    z_at = [(z + k) % 4 for k in (1, 2, 3)]
    z_from = [(z + 4 - k) % 4 for k in (1, 2, 3)]
    at_end = (z == 0) | (z == 3)
    in_middle = (z == 1) | (z == 2)
    far = z_from[1]
    far_end = (jnp.where(z == 2, 3, 0) * 4 + y * 2 + x, r)
    near_middle = (jnp.where(z == 0, 1, 2) * 4 + y * 2 + x, r)
    place = 2 * y + x

    def copy(src, dst, ss, rs, dev):
        return pltpu.make_async_remote_copy(
            src_ref=src, dst_ref=dst, send_sem=ss, recv_sem=rs, device_id=dev, device_id_type=MESH
        )

    barrier = pltpu.get_barrier_semaphore()
    for dev in z_dev + [a_dev, b_dev, core_dev]:
        pl.semaphore_signal(barrier, inc=1, device_id=dev, device_id_type=MESH)
    pl.semaphore_wait(barrier, 6)

    my_rows = pl.ds(pl.multiple_of(r * 32, 32), 32)
    o_rows = pl.ds(pl.multiple_of(o * 32, 32), 32)

    def part_cols(part, who):
        return pl.ds(pl.multiple_of((part // 2) * 1024 + who * 512 + (part % 2) * 256, 256), 256)

    pre = []
    pre.append(copy(small_in, s.small.at[z, y, x, r], s.pre_s.at[0], s.pre_r.at[0], core_dev))
    for i in range(6):
        pre.append(
            copy(
                win_in.at[:, part_cols(i, o)],
                s.win.at[i, z, y, x, my_rows],
                s.pre_s.at[1 + i],
                s.pre_r.at[1 + i],
                core_dev,
            )
        )
    pre.append(copy(frames_ref, s.frames_all.at[r], s.pre_s.at[7], s.pre_r.at[7], core_dev))
    for j in range(4):
        pre.append(
            copy(
                s.half.at[o, j * 32 : (j + 1) * 32],
                s.wexp.at[j, z, y, x, my_rows],
                s.pre_s.at[8 + j],
                s.pre_r.at[8 + j],
                core_dev,
            )
        )
    pre.append(copy(cot_ref, s.c_all.at[r], s.pre_s.at[12], s.pre_r.at[12], core_dev))
    for item in pre[:8]:
        item.start()
    group_32 = lax.broadcasted_iota(jnp.int32, (32, 128), 1) // 32

    def pick(parts, group):
        picked = parts[3]
        for g in range(3):
            picked = jnp.where(group == g, parts[g], picked)
        return picked

    for who in range(2):
        for block in range(4):
            source = [
                wexp_in[:, (2 * (4 * block + q) + who) * 128 : (2 * (4 * block + q) + who + 1) * 128].astype(F32)
                for q in range(4)
            ]
            for j in range(4):
                chosen = pick([source[(g + j) % 4] for g in range(4)], group_32)
                s.half[who, j * 32 : (j + 1) * 32, block * 128 : (block + 1) * 128] = chosen.astype(BF)
    for item in pre[8:]:
        item.start()
    own_frames = pltpu.make_async_copy(frames_ref, s.frames_all.at[r], s.own_s.at[0])
    own_cot = pltpu.make_async_copy(cot_ref, s.c_all.at[r], s.own_s.at[1])
    own_frames.start()
    own_cot.start()
    own_more = [pltpu.make_async_copy(wout_in, s.wout.at[z, y, x, r], s.own_s.at[2])]
    for j in range(4):
        group = (place + 4 - j) % 4
        rows = pl.ds(pl.multiple_of(group * 32, 32), 32)
        own_more.append(pltpu.make_async_copy(wred_in.at[rows], s.wred.at[j, z, group], s.own_s.at[3 + j]))
    for item in own_more:
        item.start()
    s.small[z, y, x, r] = small_in[...]
    for i in range(6):
        s.win[i, z, y, x, my_rows] = win_in[:, part_cols(i, r)]
    for j in range(4):
        s.wexp[j, z, y, x, my_rows] = s.half[r, j * 32 : (j + 1) * 32]

    def ag_item(t, piece, col, split):
        return Bag(t=t, piece=piece, col=col, split=split)

    def slot(j, b, c):
        return (2 * b + c + 4 - j) % 4

    gathers = [ag_item(0, lambda a, b, c: s.small.at[a, b, c], lambda b, c: s.small.at[:, b, c], False)]
    for i in range(6):
        gathers.append(
            ag_item(
                1 + i, lambda a, b, c, i=i: s.win.at[i, a, b, c], lambda b, c, i=i: s.win.at[i, :, b, c], False
            )
        )
    gathers.append(ag_item(7, lambda a, b, c: s.wout.at[a, b, c, r], lambda b, c: s.wout.at[:, b, c, r], False))
    for j in range(4):
        gathers.append(
            ag_item(
                8 + 2 * j, lambda a, b, c, j=j: s.wexp.at[j, a, b, c], lambda b, c, j=j: s.wexp.at[j, :, b, c], True
            )
        )
        gathers.append(
            ag_item(
                9 + 2 * j,
                lambda a, b, c, j=j: s.wred.at[j, a, slot(j, b, c)],
                lambda b, c, j=j: s.wred.at[j, :, slot(j, b, c)],
                bool(RED_SPLIT[j]),
            )
        )

    def when(cond, go):
        if isinstance(cond, bool):
            if cond:
                go()
        else:
            pl.when(cond)(go)

    def z_copies(it, yy, xx, ss, rs):
        p = it.piece(z, yy, xx)
        return [copy(p, p, ss.at[it.t, k], rs.at[it.t, k], z_dev[k]) for k in range(3)]

    def straight(it, k):
        if not it.split or k == 1:
            return True
        return z != 3 if k == 0 else z != 0

    def z_start(it, yy, xx, ss, rs):
        for k, c in enumerate(z_copies(it, yy, xx, ss, rs)):
            when(straight(it, k), c.start)

    def z_relay(it, yy, xx, rs, which):
        p = it.piece(far, yy, xx)

        @pl.when(in_middle)
        def _():
            copy(p, p, s.agx_s.at[it.t, which], rs.at[it.t, 1], far_end).wait_recv()
            copy(p, p, s.agx_s.at[it.t, which], rs.at[it.t, jnp.where(z == 2, 2, 0)], far_end).start()

    def z_wait(it, yy, xx, ss, rs):
        for k in range(3):
            p = it.piece(z_from[k], yy, xx)
            c = copy(p, p, ss.at[it.t, k], rs.at[it.t, k], z_dev[k])
            when(at_end if it.split and k == 1 else True, c.wait_recv)

    def z_sent(it, yy, xx, ss, rs, which):
        for k, c in enumerate(z_copies(it, yy, xx, ss, rs)):
            when(straight(it, k), c.wait_send)
        if it.split:
            p = it.piece(far, yy, xx)
            pl.when(in_middle)(copy(p, p, s.agx_s.at[it.t, which], rs.at[it.t, 0], far_end).wait_send)

    def a_piece(it, yy, xx):
        p = it.piece(z, yy, xx)
        return copy(p, p, s.aga_s.at[it.t], s.aga_r.at[it.t], a_dev)

    def a_copy(it, yy, xx):
        return copy(it.col(yy, xx), it.col(yy, xx), s.aga_s.at[it.t], s.aga_r.at[it.t], a_dev)

    def b_copy(it, which, yy, xx):
        return copy(it.col(yy, xx), it.col(yy, xx), s.agb_s.at[it.t, which], s.agb_r.at[it.t, which], b_dev)

    def e0(it):
        if it.split:
            a_piece(it, y, x).start()
        z_start(it, y, x, s.agz_s, s.agz_r)

    def e1(it):
        if it.split:
            z_relay(it, y, x, s.agz_r, 0)
            a_piece(it, ya, xa).wait_recv()
            z_start(it, ya, xa, s.agy_s, s.agy_r)
            return
        z_wait(it, y, x, s.agz_s, s.agz_r)
        a_copy(it, y, x).start()
        b_copy(it, 0, y, x).start()

    def e2(it):
        if it.split:
            z_relay(it, ya, xa, s.agy_r, 1)
            z_wait(it, y, x, s.agz_s, s.agz_r)
            b_copy(it, 0, y, x).start()
            z_wait(it, ya, xa, s.agy_s, s.agy_r)
            b_copy(it, 1, ya, xa).start()
            return
        a_copy(it, ya, xa).wait_recv()
        b_copy(it, 1, ya, xa).start()

    def e3(it):
        b_copy(it, 0, yb, xb).wait_recv()
        b_copy(it, 1, yc, xc).wait_recv()

    def sent(it):
        z_sent(it, y, x, s.agz_s, s.agz_r, 0)
        if it.split:
            a_piece(it, y, x).wait_send()
            z_sent(it, ya, xa, s.agy_s, s.agy_r, 1)
        else:
            a_copy(it, y, x).wait_send()
        b_copy(it, 0, y, x).wait_send()
        b_copy(it, 1, ya, xa).wait_send()

    def pre_in(index, dst):
        copy(dst, dst, s.pre_s.at[index], s.pre_r.at[index], core_dev).wait_recv()

    def ready(i):
        if i == 0:
            pre_in(0, s.small.at[z, y, x, o])
        elif i < 7:
            pre_in(i, s.win.at[i - 1, z, y, x, o_rows])
        elif i >= 8 and i % 2 == 0:
            j = (i - 8) // 2
            pre_in(8 + j, s.wexp.at[j, z, y, x, o_rows])

    done = []

    def ahead(count):
        for i in range(len(done), count + 1):
            done.append(i)
            for event, lag in ((e0, 0), (e1, LOOK), (e2, 2 * LOOK)):
                if 0 <= i - lag < len(gathers):
                    if lag == 0:
                        ready(i)
                    event(gathers[i - lag])

    def arrive(i, lag):
        ahead(i + lag)
        e3(gathers[i])

    ahead(2)

    for edge, k in ((0, 0), (3, 2)):

        @pl.when(z == edge)
        def _(k=k):
            for base in (0, 3):
                s.rz[:, base + k] = jnp.zeros((4, 64, 512), BF)
                for j in range(4):
                    if RED_SPLIT[j]:
                        s.land[j, 1 + base + k] = jnp.zeros((32, 1024), BF)

    own_frames.wait()
    own_cot.wait()
    for item in own_more:
        item.wait()
    prefix = phon_ref[0] + prom_ref[0]
    seg_row = seg_ref[...].astype(F32)
    seg_wide = jnp.broadcast_to(seg_row, (384, 384))
    seg_tall = seg_wide.T
    key_at = lax.broadcasted_iota(jnp.int32, (384, 384), 0)
    row_at = lax.broadcasted_iota(jnp.int32, (384, 384), 1)
    causal = key_at <= row_at
    seen = key_at < prefix

    def as_bias(allowed):
        return jnp.where(allowed, 0.0, MASKED).astype(BF)

    s.mask[0:384, 0:384] = as_bias(causal & seen)
    s.mask[0:384, 384:768] = as_bias(seen)
    s.mask[384:768, 384:768] = as_bias(causal & (seg_wide == seg_tall))

    arrive(0, LAG_IN)

    def tile_sum(q):
        total = jnp.zeros((16, 128), F32)
        for xx in range(2):
            for who in range(2):
                total = total + s.small[q // 2, q % 2, xx, who].astype(F32)
        return total

    for q in range(8):
        s.vec[:, q * 128 : (q + 1) * 128] = tile_sum(q)[0:8]
    group_1 = lax.broadcasted_iota(jnp.int32, (1, 128), 1) // 32
    for block in range(4):
        tiles = [s.small[block, q // 2, q % 2, r].astype(F32)[8:9] for q in range(4)]
        for j in range(4):
            s.ebias[j, 0:1, block * 128 : (block + 1) * 128] = pick([tiles[(g + j) % 4] for g in range(4)], group_1)

    def vec_row(i):
        return s.vec[i : i + 1, :]

    pre_in(7, s.frames_all.at[o])

    def norm_tile(i, carry):
        who, rows = i // 3, pl.ds(pl.multiple_of((i % 3) * 128, 128), 128)
        unit, _ = centre(s.frames_all[who, rows].astype(F32))
        normed = unit * vec_row(0) + vec_row(1)
        s.n_all[who, rows] = normed.astype(BF)
        s.n1t[:, pl.ds(pl.multiple_of(i * 128, 128), 128)] = normed.T.astype(BF)
        return carry

    lax.fori_loop(0, 6, norm_tile, 0)

    def project(part):
        section, n = part // 2, part % 2
        mixed = dot(s.n_all[...].reshape(768, 1024), s.win[part].reshape(1024, 256))
        if section != 1:
            bias_at = pl.ds(pl.multiple_of(r * 512 + n * 256, 256), 256)
            bias_row = 2 if section == 0 else 3
            mixed = mixed + s.vec[bias_row : bias_row + 1, bias_at]
        mixed = mixed.astype(BF)
        s.qkv[section, 2 * n] = mixed[:, 0:128]
        s.qkv[section, 2 * n + 1] = mixed[:, 128:256]

    for part in range(6):
        arrive(1 + part, LAG_IN)
        project(part)

    factor = HD**-0.5 * LOG2E
    low_lane = lax.broadcasted_iota(jnp.int32, (128, 128), 1) < 64

    def pair_rows(block):
        zero = jnp.zeros_like(block)
        return jnp.concatenate([jnp.where(low_lane, block, zero), jnp.where(low_lane, zero, block)], axis=0)

    def pair_mask(keys, rb):
        bias = s.mask[0:keys, rb * 128 : (rb + 1) * 128].astype(F32)
        return jnp.concatenate([bias, bias], axis=1)

    def key_count(rb):
        return (rb + 1) * 128 if rb < 3 else 384 + (rb - 2) * 128

    def attend(hp, carry):
        v_t = flip(s.qkv[2, hp])
        dims = pl.ds(pl.multiple_of(hp * 128, 128), 128)
        for rb in range(6):
            keys = key_count(rb)
            both = pair_rows(s.qkv[0, hp, rb * 128 : (rb + 1) * 128])
            scores = dot_nt(s.qkv[1, hp, 0:keys], both) * factor + pair_mask(keys, rb)
            peak = jnp.max(scores, axis=0, keepdims=True)
            expo = jnp.exp2(scores - peak)
            total = jnp.sum(expo, axis=0, keepdims=True)
            heads = dot(v_t[:, 0:keys], expo.astype(BF)) / total
            s.lse[hp, rb] = jnp.broadcast_to(peak + jnp.log2(total), (8, 256))
            out = jnp.concatenate([heads[0:64, 0:128], heads[64:128, 128:256]], axis=0)
            at = (rb % 3) * 128
            s.half_t[rb // 3, dims, at : at + 128] = out.astype(BF)
            s.half[rb // 3, at : at + 128, dims] = out.T.astype(BF)
        return carry

    for j in range(4):
        pre[8 + j].wait_send()
    lax.fori_loop(0, 2, attend, 0)
    ahead(6 + LAG_IN + 1)
    lax.fori_loop(2, 4, attend, 0)
    ahead(6 + LAG_IN + 2)

    my_half = pl.ds(pl.multiple_of(r * 512, 512), 512)
    o_half = pl.ds(pl.multiple_of(o * 512, 512), 512)

    def core_copy(index, src, dst):
        return copy(src, dst, s.core_s.at[index], s.core_r.at[index], core_dev)

    core_copy(0, s.half.at[o], s.wide.at[:, my_half]).start()
    core_copy(1, s.half_t.at[o], s.att_t.at[my_half]).start()
    s.wide[:, my_half] = s.half[r]
    s.att_t[my_half] = s.half_t[r]
    arrive(7, LAG_FF)
    out_swap = core_copy(2, s.wout.at[:, :, :, r], s.wout.at[:, :, :, r])
    out_swap.start()
    core_copy(0, s.wide.at[:, o_half], s.wide.at[:, o_half]).wait_recv()
    core_copy(1, s.att_t.at[o_half], s.att_t.at[o_half]).wait_recv()
    core_copy(2, s.wout.at[:, :, :, o], s.wout.at[:, :, :, o]).wait_recv()
    def out_tile(n, carry):
        cols = pl.ds(pl.multiple_of(n * 256, 256), 256)
        branch = dot(s.wide[...], s.wout[:, :, :, :, :, cols].reshape(1024, 256))
        s.middle[:, cols] = s.frames_all[r, :, cols].astype(F32) + branch + s.vec[4:5, cols]
        return carry

    lax.fori_loop(0, 4, out_tile, 0)

    def norm_two(i, carry):
        rows = pl.ds(pl.multiple_of(i * 128, 128), 128)
        unit, _ = centre(s.middle[rows])
        s.n_all[r, rows] = (unit * vec_row(5) + vec_row(6)).astype(BF)
        return carry

    lax.fori_loop(0, 3, norm_two, 0)
    core_copy(3, s.n_all.at[r], s.n_all.at[r]).start()
    pre_in(12, s.c_all.at[o])
    s.out_acc[...] = jnp.zeros_like(s.out_acc)
    s.bn_acc[...] = jnp.zeros_like(s.bn_acc)
    core_copy(3, s.n_all.at[o], s.n_all.at[o]).wait_recv()
    core_copy(3, s.n_all.at[r], s.n_all.at[r]).wait_send()

    def flip_two(i, carry):
        who, rows = i // 3, pl.ds(pl.multiple_of((i % 3) * 128, 128), 128)
        s.n2t[:, pl.ds(pl.multiple_of(i * 128, 128), 128)] = flip(s.n_all[who, rows])
        return carry

    lax.fori_loop(0, 6, flip_two, 0)

    def rs_exp(j):
        return Bag(
            t=j, fin=j, split=True, piece=lambda a, b, c: s.wexp.at[j, a, b, c],
            col=lambda b, c: s.wexp.at[j, :, b, c], rb=lambda w: s.rb.at[j, w], ra=s.ra.at[j],
            rz=lambda k: s.rz.at[j, k], rx=lambda w: s.rx.at[j, w],
        )

    def rs_in(i):
        slot, part = ((0, 0), (0, 1), (1, 0), (1, 1), (2, 0), (2, 1))[i]
        half = slice(256 * part, 256 * part + 256)
        return Bag(
            t=9 + i, fin=4 + i, split=False, piece=lambda a, b, c: s.win.at[i, a, b, c],
            col=lambda b, c: s.win.at[i, :, b, c], rb=lambda w: s.rb.at[slot, w, :, :, half],
            ra=s.ra_in.at[i], rz=lambda k: s.rz_in.at[i, k],
        )

    def rs_red(j):
        split = bool(RED_SPLIT[j])
        return Bag(
            t=4 + j, fin=None, split=split, piece=lambda a, b, c: s.wred.at[j, a, slot(j, b, c)],
            col=lambda b, c: s.wred.at[j, :, slot(j, b, c)], rb=lambda w: s.rb_red.at[j, w],
            ra=s.land.at[j, 0] if split else s.land.at[j, 0:4],
            rz=lambda k: s.land.at[j, k + (1 if split else 4)], rx=lambda w: s.land.at[j, 7 + w],
        )

    def rs_out():
        return Bag(
            t=8, fin=None, split=False, piece=lambda a, b, c: s.wout.at[a, b, c, r],
            col=lambda b, c: s.wout.at[:, b, c, r], rb=lambda w: s.rb_out.at[w], ra=s.ra_out,
            rz=lambda k: s.rz_out.at[k],
        )

    def rs_small():
        return Bag(
            t=15, fin=None, split=False, piece=lambda a, b, c: s.sg.at[a, b, c],
            col=lambda b, c: s.sg.at[:, b, c], rb=lambda w: s.rb_sg.at[w], ra=s.ra_sg,
            rz=lambda k: s.rz_sg.at[k],
        )

    def rb_copy(it, which, yy, xx):
        return copy(it.col(yy, xx), it.rb(which), s.rsb_s.at[it.t, which], s.rsb_r.at[it.t, which], b_dev)

    def ra_copy(it):
        src = it.piece(z, ya, xa) if it.split else it.col(ya, xa)
        return copy(src, it.ra, s.rsa_s.at[it.t], s.rsa_r.at[it.t], a_dev)

    def add_into(it, yy, xx, sources):
        target = it.col(yy, xx)
        kind = F32 if it.t == 15 else BF

        def body(i, carry):
            total = target[i].astype(F32)
            for src in sources:
                total = total + src[i].astype(F32)
            target[i] = total.astype(kind)
            return carry

        lax.fori_loop(0, 4, body, 0)

    def own_copy(it, k, yy, xx, base, ss, rs):
        return copy(it.piece(z_at[k], yy, xx), it.rz(base + k), ss.at[it.t, k], rs.at[it.t, k], z_dev[k])

    def far_copy(it, k, yy, xx, which):
        return copy(
            it.piece(z_at[k], yy, xx), it.rx(which), s.rsx_s.at[it.t, which], s.rsx_r.at[it.t, which], near_middle
        )

    def own_start(it, yy, xx, base, ss, rs, which):
        for k in range(3):
            c = own_copy(it, k, yy, xx, base, ss, rs)
            if not it.split:
                c.start()
            elif k == 1:
                pl.when(at_end)(c.start)
            else:
                edge = 3 if k == 0 else 0
                pl.when(z != edge)(c.start)
                pl.when(z == edge)(far_copy(it, k, yy, xx, which).start)

    def own_relay(it, yy, xx, base, ss, rs, which):
        @pl.when(in_middle)
        def _():
            far_copy(it, 1, yy, xx, which).wait_recv()
            held = it.piece(z_at[1], yy, xx)
            held[...] = (held[...].astype(F32) + it.rx(which)[...].astype(F32)).astype(BF)
            own_copy(it, 1, yy, xx, base, ss, rs).start()

    def own_wait(it, yy, xx, base, ss, rs):
        for k in range(3):
            c = own_copy(it, k, yy, xx, base, ss, rs)
            if not it.split or k == 1:
                c.wait_recv()
            else:
                pl.when(z != (0 if k == 0 else 3))(c.wait_recv)

    def own_sent(it, yy, xx, base, ss, rs, which):
        for k in range(3):
            c = own_copy(it, k, yy, xx, base, ss, rs)
            if not it.split or k == 1:
                c.wait_send()
            else:
                edge = 3 if k == 0 else 0
                pl.when(z != edge)(c.wait_send)
                pl.when(z == edge)(far_copy(it, k, yy, xx, which).wait_send)

    def z_args(it, second):
        if second:
            return (ya, xa, 3, s.rsy_s, s.rsy_r)
        return (y, x, 0, s.rsz_s, s.rsz_r)

    def z_total(it, second):
        yy, xx, base, ss, rs = z_args(it, second)
        own_wait(it, yy, xx, base, ss, rs)
        total = it.piece(z, yy, xx)[...].astype(F32)
        for k in range(3):
            total = total + it.rz(base + k)[...].astype(F32)
        return total

    def f0(it):
        rb_copy(it, 0, yc, xc).start()
        rb_copy(it, 1, yb, xb).start()

    def f1(it):
        rb_copy(it, 0, yc, xc).wait_recv()
        add_into(it, ya, xa, [it.rb(0)])
        if not it.split:
            ra_copy(it).start()
            return
        own_start(it, *z_args(it, True), 1)
        rb_copy(it, 1, yb, xb).wait_recv()
        add_into(it, y, x, [it.rb(1)])
        own_start(it, *z_args(it, False), 0)

    def f2(it):
        if it.split:
            own_relay(it, *z_args(it, True), 1)
            own_relay(it, *z_args(it, False), 0)
            return
        rb_copy(it, 1, yb, xb).wait_recv()
        ra_copy(it).wait_recv()
        add_into(it, y, x, [it.rb(1), it.ra])
        own_start(it, *z_args(it, False), 0)

    def f3(it):
        if it.split:
            total = z_total(it, True)
            it.piece(z, ya, xa)[...] = total.astype(BF)
            ra_copy(it).start()

    def full_total(it):
        total = z_total(it, False)
        if it.split:
            ra_copy(it).wait_recv()
            total = total + it.ra[...].astype(F32)
        return total

    def fin_refs(index):
        if index < 4:
            return s.fin.at[index], s.fin_in.at[index]
        return s.fin_w.at[index - 4], s.fin_w_in.at[index - 4]

    def fin_copy(index):
        out, back = fin_refs(index)
        return copy(out.at[o_rows], back, s.fin_s.at[index], s.fin_r.at[index], core_dev)

    def small_fin():
        return copy(s.sfin, s.sfin_in, s.fin_s.at[10], s.fin_r.at[10], core_dev)

    def put_in(i, value, who):
        dwin_ref[:, part_cols(i, who)] = value

    def put_exp(source, who):
        for block in range(4):
            at = slice(block * 128, (block + 1) * 128)
            chunk = [source(j)[:, at] for j in range(4)]
            for q in range(4):
                cols = pl.ds(pl.multiple_of((2 * (4 * block + q) + who) * 128, 128), 128)
                dwexp_ref[:, cols] = pick([chunk[(q - g) % 4] for g in range(4)], group_32)

    def f4(it):
        if 4 <= it.t < 8:
            group = (place + 8 - it.t) % 4
            dwred_ref[pl.ds(pl.multiple_of(group * 32, 32), 32)] = full_total(it)
        elif it.t == 8:
            dwout_ref[...] = full_total(it)
        elif it.t == 15:
            s.sfin[...] = full_total(it)
            small_fin().start()
        else:
            out, _ = fin_refs(it.fin)
            out[...] = full_total(it)
            fin_copy(it.fin).start()
            if it.fin >= 4:
                put_in(it.fin - 4, out[my_rows], r)

    def f5(it):
        if it.fin is not None:
            fin_copy(it.fin).wait_recv()
            if it.fin >= 4:
                put_in(it.fin - 4, fin_refs(it.fin)[1][...], o)
            elif it.fin == 3:
                put_exp(lambda j: s.fin[j, my_rows], r)
                put_exp(lambda j: s.fin_in[j], o)
        elif it.t == 15:
            small_fin().wait_recv()
            row = lax.broadcasted_iota(jnp.int32, (16, 128), 0)
            own = s.sfin[...]
            dsmall_ref[...] = jnp.where(row < 8, own + s.sfin_in[...], own)

    def all_sent(it):
        rb_copy(it, 0, yc, xc).wait_send()
        rb_copy(it, 1, yb, xb).wait_send()
        ra_copy(it).wait_send()
        own_sent(it, *z_args(it, False), 0)
        if it.split:
            own_sent(it, *z_args(it, True), 1)
        if it.fin is not None:
            fin_copy(it.fin).wait_send()
        elif it.t == 15:
            small_fin().wait_send()

    order = []
    for j in range(4):
        order += [rs_red(j), rs_exp(j)]
    order += [rs_out()] + [rs_in(i) for i in range(3)] + [rs_small()] + [rs_in(i) for i in range(3, 6)]

    def step(i):
        for event, lag in ((f0, -LEAD), (f1, 1), (f2, 2), (f3, 3), (f4, 4), (f5, 5)):
            if 0 <= i - lag < len(order):
                event(order[i - lag])

    stepped = []

    def next_step():
        step(len(stepped))
        stepped.append(True)

    def feed(j, between):
        if j == 3 and EARLY_CHUNK == 3:
            for it in order[:LEAD]:
                f0(it)
        arrive(8 + 2 * j, LAG_FF)
        arrive(9 + 2 * j, LAG_FF)
        sent(gathers[8 + 2 * j])
        sent(gathers[9 + 2 * j])
        between(0)

        def hidden(n, inside):
            cols = pl.ds(pl.multiple_of(n * 256, 256), 256)
            left = s.n_all[...].reshape(768, 1024)
            inner = dot(left, s.wexp[j, :, :, :, :, cols].reshape(1024, 256)) + s.ebias[j, 0:1, cols]
            phi = 0.5 + 0.5 * lax.erf(inner * (2.0**-0.5))
            active = inner * phi
            s.ffb[0, :, cols] = active.astype(BF)
            s.act_t[cols] = active.T.astype(BF)
            slope = phi + inner * (jnp.exp(-0.5 * inner * inner) * 0.3989422804014327)
            up = s.c_all[...].reshape(768, 1024)
            weight = s.wred[j, pl.ds(2 * n, 2)].reshape(256, 1024)
            back = (dot_nt(up, weight) * slope).astype(BF)
            s.ffb[1, :, cols] = back
            s.gexp[j, 0:1, cols] = jnp.sum(back.astype(F32), axis=0, keepdims=True)
            return inside

        lax.fori_loop(0, 2, hidden, 0)

        def wide_tile(n, inside):
            cols = pl.ds(pl.multiple_of(n * 256, 256), 256)
            part = dot(s.ffb[0], s.wred[j, :, :, :, cols].reshape(512, 256))
            s.out_acc[:, :, cols] += part.reshape(2, 384, 256)
            back = dot_nt(s.ffb[1], s.wexp[j, n].reshape(256, 512))
            s.bn_acc[:, :, cols] += back.reshape(2, 384, 256)
            return inside

        ahead(9 + 2 * j + LAG_FF + 1)
        if j == EARLY_CHUNK == 2:
            for it in order[:LEAD]:
                f0(it)
        lax.fori_loop(0, 4, wide_tile, 0)
        between(1)

        def grad_red(n, inside):
            cols = pl.ds(pl.multiple_of(n * 256, 256), 256)
            up = s.c_all[:, :, cols].reshape(768, 256)
            s.wred[j, :, :, :, cols] = dot(s.act_t[...], up).astype(BF).reshape(4, 4, 32, 256)
            return inside

        lax.fori_loop(0, 4, grad_red, 0)

        def grad_exp(n, inside):
            cols = pl.ds(pl.multiple_of(n * 256, 256), 256)
            grad = dot(s.n2t[...], s.ffb[1, :, cols]).astype(BF)
            s.wexp[j, :, :, :, :, cols] = grad.reshape(4, 2, 2, 64, 256)
            return inside

        lax.fori_loop(0, 2, grad_exp, 0)
        between(2)

    for j in range(3):
        feed(j, lambda place: None)

    def start_reduction(place_in):
        if place_in == 0:
            next_step()
        elif place_in == 1:
            core_copy(4, s.bn_acc.at[o], s.cross).start()
            next_step()
        else:
            next_step()

    feed(3, start_reduction)

    core_copy(4, s.bn_acc.at[o], s.cross).wait_recv()
    s.n_all[o] = s.out_acc[o].astype(BF)
    core_copy(5, s.n_all.at[o], s.n_all.at[o]).start()

    def middle_back(i, carry):
        rows = pl.ds(pl.multiple_of(i * 128, 128), 128)
        unit, rate = centre(s.middle[rows])
        upstream = s.bn_acc[r, rows] + s.cross[rows]
        cot = s.c_all[r, rows].astype(F32)
        back = cot + norm_back(unit, rate, vec_row(5), upstream)
        s.bn_acc[r, rows] = back
        branch = back.astype(BF)
        s.wide[rows] = branch
        gain_t, shift_t, out_t, red_t = carry
        return (
            gain_t + jnp.sum(upstream * unit, axis=0, keepdims=True),
            shift_t + jnp.sum(upstream, axis=0, keepdims=True),
            out_t + jnp.sum(branch.astype(F32), axis=0, keepdims=True),
            red_t + jnp.sum(cot, axis=0, keepdims=True),
        )

    zero_row = jnp.zeros((1, 1024), F32)
    gain_t, shift_t, out_t, red_t = lax.fori_loop(0, 3, middle_back, (zero_row,) * 4)
    s.gvec[5:6] = gain_t
    s.gvec[6:7] = shift_t
    s.gvec[4:5] = out_t
    s.gvec[7:8] = red_t

    core_copy(0, s.half.at[o], s.half.at[o]).wait_send()
    core_copy(2, s.wout.at[:, :, :, r], s.wout.at[:, :, :, r]).wait_send()

    def back_att(n, carry):
        weight = s.wout[n].reshape(256, 1024)
        cols = pl.ds(pl.multiple_of((n % 2) * 256, 256), 256)
        s.half[n // 2, :, cols] = dot_nt(s.wide[...], weight).astype(BF)
        return carry

    lax.fori_loop(0, 4, back_att, 0)
    core_copy(6, s.half.at[o], s.ba_all.at[r]).start()
    s.ba_all[r] = s.half[r]
    next_step()
    sent(gathers[7])

    def grad_out(n, carry):
        cols = pl.ds(pl.multiple_of(n * 256, 256), 256)
        grad = dot(s.att_t[...], s.wide[:, cols]).astype(BF)
        s.wout[:, :, :, :, :, cols] = grad.reshape(4, 2, 2, 2, 32, 256)
        return carry

    lax.fori_loop(0, 4, grad_out, 0)
    core_copy(7, s.wout.at[:, :, :, o], s.outx).start()
    core_copy(5, s.n_all.at[r], s.n_all.at[r]).wait_recv()

    def result_tile(i, carry):
        rows = pl.ds(pl.multiple_of(i * 128, 128), 128)
        total = s.middle[rows] + s.out_acc[r, rows] + s.n_all[r, rows].astype(F32) + vec_row(7)
        result_ref[rows] = total.astype(BF)
        return carry

    lax.fori_loop(0, 3, result_tile, 0)
    core_copy(6, s.ba_all.at[o], s.ba_all.at[o]).wait_recv()

    def attend_back(hp, carry):
        k_t = flip(s.qkv[1, hp])
        dims = pl.ds(pl.multiple_of(hp * 128, 128), 128)
        s.dkv[...] = jnp.zeros_like(s.dkv)
        for rb in range(6):
            keys = key_count(rb)
            rows = slice(rb * 128, (rb + 1) * 128)
            both = pair_rows(s.qkv[0, hp, rows])
            at = (rb % 3) * 128
            up = pair_rows(s.ba_all[rb // 3, at : at + 128, dims])
            scores = dot_nt(s.qkv[1, hp, 0:keys], both) * factor + pair_mask(keys, rb)
            probs = jnp.exp2(scores - s.lse[hp, rb, 0:1])
            back_probs = dot_nt(s.qkv[2, hp, 0:keys], up)
            weighted = probs * back_probs
            centre_row = jnp.sum(weighted, axis=0, keepdims=True)
            back_scores = (weighted - probs * centre_row).astype(BF)
            s.dkv[1, 0:keys] += dot(probs.astype(BF), up)
            s.dkv[0, 0:keys] += dot(back_scores, both)
            query = dot(k_t[:, 0:keys], back_scores)
            query = jnp.concatenate([query[0:64, 0:128], query[64:128, 128:256]], axis=0)
            s.ffb[0, rows, dims] = (query.T * HD**-0.5).astype(BF)
        s.ffb[1, :, dims] = (s.dkv[0] * HD**-0.5).astype(BF)
        s.ffb[2, :, dims] = s.dkv[1].astype(BF)
        return carry

    core_copy(7, s.outx, s.outx).wait_recv()

    def add_out(i, carry):
        for yy in range(2):
            for xx in range(2):
                total = s.wout[i, yy, xx, r].astype(F32) + s.outx[i, yy, xx].astype(F32)
                s.wout[i, yy, xx, r] = total.astype(BF)
        return carry

    lax.fori_loop(0, 4, add_out, 0)

    lax.fori_loop(0, 1, attend_back, 0)
    next_step()
    lax.fori_loop(1, 3, attend_back, 0)
    next_step()
    lax.fori_loop(3, 4, attend_back, 0)

    core_copy(5, s.n_all.at[o], s.n_all.at[o]).wait_send()

    def back_in(n, carry):
        cols = pl.ds(pl.multiple_of(n * 256, 256), 256)
        total = dot_nt(s.ffb[0, :, 0:256], s.win[0, n].reshape(256, 256))
        for part in range(1, 6):
            at = (part % 2) * 256
            total = total + dot_nt(s.ffb[part // 2, :, at : at + 256], s.win[part, n].reshape(256, 256))
        s.out_acc[:, :, cols] = total.reshape(2, 384, 256)
        return carry

    lax.fori_loop(0, 4, back_in, 0)
    core_copy(8, s.out_acc.at[o], s.cross).start()
    next_step()
    for part in range(6):
        sent(gathers[1 + part])
        at = (part % 2) * 256
        grad = dot(s.n1t[...], s.ffb[part // 2, :, at : at + 256]).astype(BF)
        s.win[part] = grad.reshape(4, 2, 2, 64, 256)
        if part == 2:
            next_step()
    next_step()
    next_step()

    core_copy(8, s.out_acc.at[o], s.cross).wait_recv()

    def frame_back(i, carry):
        rows = pl.ds(pl.multiple_of(i * 128, 128), 128)
        unit, rate = centre(s.frames_all[r, rows].astype(F32))
        upstream = s.out_acc[r, rows] + s.cross[rows]
        back = s.bn_acc[r, rows] + norm_back(unit, rate, vec_row(0), upstream)
        fgrad_ref[rows] = back.astype(BF)
        gain_t, shift_t = carry
        return (
            gain_t + jnp.sum(upstream * unit, axis=0, keepdims=True),
            shift_t + jnp.sum(upstream, axis=0, keepdims=True),
        )

    gain_t, shift_t = lax.fori_loop(0, 3, frame_back, (zero_row,) * 2)
    s.gvec[0:1] = gain_t
    s.gvec[1:2] = shift_t
    s.gvec[2:4] = jnp.zeros((2, 1024), F32)
    s.gvec[2:3, my_half] = jnp.sum(s.ffb[0].astype(F32), axis=0, keepdims=True)
    s.gvec[3:4, my_half] = jnp.sum(s.ffb[2].astype(F32), axis=0, keepdims=True)
    s.sg[...] = jnp.zeros_like(s.sg)
    for zz in range(4):
        for yy in range(2):
            for xx in range(2):
                at = (zz * 2 + yy) * 128
                s.sg[zz, yy, xx, 0:8] = s.gvec[:, at : at + 128]
                q = 2 * yy + xx
                block = slice(zz * 128, (zz + 1) * 128)
                chunk = [s.gexp[j, 0:1, block] for j in range(4)]
                s.sg[zz, yy, xx, 8:9] = pick([chunk[(q - g) % 4] for g in range(4)], group_1)

    while len(stepped) < len(order) + 5:
        next_step()

    for i, item in enumerate(pre):
        if not 8 <= i < 12:
            item.wait_send()
    sent(gathers[0])
    core_copy(1, s.half_t.at[o], s.half_t.at[o]).wait_send()
    core_copy(4, s.bn_acc.at[o], s.cross).wait_send()
    core_copy(6, s.half.at[o], s.ba_all.at[r]).wait_send()
    core_copy(7, s.wout.at[:, :, :, o], s.outx).wait_send()
    core_copy(8, s.out_acc.at[o], s.cross).wait_send()
    for it in order:
        all_sent(it)


def hand_on(*refs):
    given, tile_ref, taken = refs[0:6], refs[6], refs[7:13]
    vectors, held, sems = refs[13:22], refs[22:28], refs[28]
    inward = [pltpu.make_async_copy(given[i], held[i], sems.at[0, i]) for i in range(6)]
    outward = [pltpu.make_async_copy(held[i], taken[i], sems.at[1, i]) for i in range(6)]
    for item in inward:
        item.start()
    quarter = (lax.axis_index("dp") * 2 + lax.axis_index("role")) % 4
    tile = tile_ref[...]
    turned = pltpu.roll(tile, (4 - quarter) % 4 * 32, 1)
    for row in range(8):
        vectors[row][...] = turned[row, 0:32]
    vectors[8][...] = tile[8]
    for i in range(6):
        inward[i].wait()
        outward[i].start()
    for item in outward:
        item.wait()


def fused_shards(
    frames, frames_cotangent, phoneme_len, prompt_len, target_segment, first_gain, first_shift, inward_weight,
    query_bias, value_bias, outward_weight, outward_bias, second_gain, second_shift, expand_weight, expand_bias,
    reduce_weight, reduce_bias,
):
    number = lax.axis_index("dp") * 2 + lax.axis_index("role")
    quarter = number % 4
    rows = jnp.stack(
        [first_gain, first_shift, query_bias, value_bias, outward_bias, second_gain, second_shift, reduce_bias]
    )
    lane = jnp.arange(128) // 32
    rows = jnp.where(lane[None] == quarter, jnp.tile(rows, (1, 4)), jnp.zeros((), BF))
    small = jnp.concatenate([rows, expand_bias[None], jnp.zeros((7, 128), BF)], axis=0)

    scratch = scratch_list()
    vmem = pl.BlockSpec(memory_space=pltpu.VMEM)
    smem = pl.BlockSpec(memory_space=pltpu.SMEM)
    hbm = pl.BlockSpec(memory_space=pl.ANY)
    outs = pl.pallas_call(
        functools.partial(layer_kernel, tuple(scratch)),
        out_shape=[
            jax.ShapeDtypeStruct((384, 1024), BF),
            jax.ShapeDtypeStruct((384, 1024), BF),
            jax.ShapeDtypeStruct((32, 3072), F32),
            jax.ShapeDtypeStruct((32, 1024), F32),
            jax.ShapeDtypeStruct((32, 4096), F32),
            jax.ShapeDtypeStruct((128, 1024), F32),
            jax.ShapeDtypeStruct((16, 128), F32),
        ],
        in_specs=[smem, smem, vmem, hbm, hbm, vmem, vmem, hbm, vmem, hbm],
        out_specs=[vmem] * 7,
        scratch_shapes=list(scratch.values()),
        compiler_params=pltpu.CompilerParams(
            collective_id=0, has_side_effects=True, vmem_limit_bytes=62 * 1024 * 1024
        ),
    )(
        phoneme_len, prompt_len, target_segment, frames[0], frames_cotangent[0], small, inward_weight,
        outward_weight, expand_weight, reduce_weight,
    )
    *moved, = pl.pallas_call(
        hand_on,
        out_shape=[jax.ShapeDtypeStruct(item.shape, item.dtype) for item in outs[:6]]
        + [jax.ShapeDtypeStruct((32,), F32)] * 8
        + [jax.ShapeDtypeStruct((128,), F32)],
        in_specs=[hbm] * 6 + [vmem],
        out_specs=[hbm] * 6 + [vmem] * 9,
        scratch_shapes=[pltpu.VMEM(item.shape, item.dtype) for item in outs[:6]]
        + [pltpu.SemaphoreType.DMA((2, 6))],
    )(*outs)
    result, frames_gradient, d_in, d_out, d_exp, d_red = moved[:6]
    mine, bias_row = moved[6:14], moved[14]
    return (
        result[None], frames_gradient[None], mine[0], mine[1], d_in, mine[2], mine[3], d_out, mine[4], mine[5],
        mine[6], d_exp, bias_row, d_red, mine[7],
    )


def passed_along(block, axis, distance):
    devices = range(lax.axis_size(axis))
    route = [(i - distance, i) for i in devices if i - distance in devices]
    return lax.ppermute(block, axis, route)


def normalize(values, gain, shift):
    mean_value = jnp.mean(values, axis=-1, keepdims=True)
    centered = values - mean_value
    spread = jnp.mean(centered * centered, axis=-1, keepdims=True)
    return centered * lax.rsqrt(spread + EPS) * gain + shift


def smooth_gate(values):
    return jax.nn.gelu(values, approximate=False)


def inner_rows(left, right):
    return lax.dot_general(
        left, right, (((0,), (0,)), ((), ())), preferred_element_type=jnp.float32
    )


def outer_cols(left, right):
    return lax.dot_general(
        left, right, (((1,), (1,)), ((), ())), preferred_element_type=jnp.float32
    )


def plain_shards(
    frames,
    frames_cotangent,
    phoneme_len,
    prompt_len,
    target_segment,
    first_gain,
    first_shift,
    inward_weight,
    query_bias,
    value_bias,
    outward_weight,
    outward_bias,
    second_gain,
    second_shift,
    expand_weight,
    expand_bias,
    reduce_weight,
    reduce_bias,
):
    attention_part = (
        lax.all_gather(first_gain, ("dp", "role"), axis=0, tiled=True),
        lax.all_gather(first_shift, ("dp", "role"), axis=0, tiled=True),
        lax.all_gather(inward_weight, ("dp", "role"), axis=0, tiled=True),
        lax.all_gather(query_bias, ("dp", "role"), axis=0, tiled=True),
        lax.all_gather(value_bias, ("dp", "role"), axis=0, tiled=True),
        lax.all_gather(outward_weight, ("dp", "role"), axis=0, tiled=True),
        lax.all_gather(outward_bias, ("dp", "role"), axis=0, tiled=True),
    )
    (
        full_gain,
        full_shift,
        full_inward,
        full_query_bias,
        full_value_bias,
        full_outward,
        full_outward_bias,
    ) = attention_part
    side = lax.axis_index("role")
    local_rows = frames.shape[1]
    scale = HD ** (-0.5)
    current = frames[0].astype(jnp.float32)
    normed = normalize(
        current, full_gain.astype(jnp.float32), full_shift.astype(jnp.float32)
    ).astype(jnp.bfloat16)
    mixed = jnp.dot(normed, full_inward, preferred_element_type=jnp.float32)
    queries = (mixed[:, :D] + full_query_bias.astype(jnp.float32)).astype(jnp.bfloat16)
    keys_own = mixed[:, D : 2 * D].astype(jnp.bfloat16)
    values_own = (mixed[:, 2 * D :] + full_value_bias.astype(jnp.float32)).astype(jnp.bfloat16)
    remote_keys, remote_values = passed_along((keys_own, values_own), "role", 1)
    keys_all = jnp.concatenate([remote_keys, keys_own], axis=0)
    values_all = jnp.concatenate([remote_values, values_own], axis=0)
    row_index = jnp.arange(local_rows)[:, None]
    col_index = jnp.arange(2 * local_rows)[None, :]
    own_col = col_index - local_rows
    prefix_length = phoneme_len[0] + prompt_len[0]
    segment = target_segment[0]
    key_segment = jnp.concatenate([jnp.full((local_rows,), -1, jnp.int32), segment])
    prompt_rows = (own_col >= 0) & (own_col <= row_index) & (own_col < prefix_length)
    target_rows = (col_index < prefix_length) | (own_col >= 0) & (own_col <= row_index) & (
        key_segment[None, :] == segment[:, None]
    )
    allowed = jnp.where(side == 0, prompt_rows, target_rows)

    def attend(index):
        start = index * HD
        head_query = lax.dynamic_slice_in_dim(queries, start, HD, 1)
        head_key = lax.dynamic_slice_in_dim(keys_all, start, HD, 1)
        head_value = lax.dynamic_slice_in_dim(values_all, start, HD, 1)
        scores = outer_cols(head_query, head_key) * scale
        masked = jnp.where(allowed, scores, MASKED)
        peak = jnp.max(masked, axis=1, keepdims=True)
        expo = jnp.exp(masked - peak)
        total = jnp.sum(expo, axis=1, keepdims=True)
        probs = (expo / total).astype(jnp.bfloat16)
        return (
            jnp.dot(probs, head_value, preferred_element_type=jnp.float32),
            (peak + jnp.log(total))[:, 0],
        )

    head_outs, log_totals = lax.map(attend, jnp.arange(H))
    attended = head_outs.transpose(1, 0, 2).reshape(local_rows, D).astype(jnp.bfloat16)
    middle = (
        current
        + jnp.dot(attended, full_outward, preferred_element_type=jnp.float32)
        + full_outward_bias.astype(jnp.float32)
    )
    feed_part = (
        lax.all_gather(second_gain, ("dp", "role"), axis=0, tiled=True),
        lax.all_gather(second_shift, ("dp", "role"), axis=0, tiled=True),
        lax.all_gather(expand_weight, ("dp", "role"), axis=0, tiled=True),
        lax.all_gather(expand_bias, ("dp", "role"), axis=0, tiled=True),
        lax.all_gather(reduce_weight, ("dp", "role"), axis=0, tiled=True),
        lax.all_gather(reduce_bias, ("dp", "role"), axis=0, tiled=True),
    )
    full_gain_two, full_shift_two, full_expand, full_expand_bias, full_reduce, full_reduce_bias = (
        feed_part
    )
    gain_two = full_gain_two.astype(jnp.float32)
    shift_two = full_shift_two.astype(jnp.float32)
    normed_two = normalize(middle, gain_two, shift_two).astype(jnp.bfloat16)
    inner = jnp.dot(
        normed_two, full_expand, preferred_element_type=jnp.float32
    ) + full_expand_bias.astype(jnp.float32)
    active = smooth_gate(inner).astype(jnp.bfloat16)
    output = (
        middle
        + jnp.dot(active, full_reduce, preferred_element_type=jnp.float32)
        + full_reduce_bias.astype(jnp.float32)
    )
    result = output.astype(jnp.bfloat16)[None]
    again_expand = feed_part[2]
    again_reduce = feed_part[4]
    again_gain = attention_part[0].astype(jnp.float32)
    again_shift = attention_part[1].astype(jnp.float32)
    again_inward = attention_part[2]
    again_outward = attention_part[5]
    upstream = frames_cotangent[0]
    upstream_float = upstream.astype(jnp.float32)
    reduce_bias_term = jnp.sum(upstream_float, axis=0)
    reduce_weight_term = inner_rows(active, upstream)
    back_active = outer_cols(upstream, again_reduce)
    gate_pull = jax.vjp(smooth_gate, inner)[1]
    back_inner = gate_pull(back_active)[0].astype(jnp.bfloat16)
    expand_bias_term = jnp.sum(back_inner.astype(jnp.float32), axis=0)
    expand_weight_term = inner_rows(normed_two, back_inner)
    back_normed_two = outer_cols(back_inner, again_expand)
    second_pull = jax.vjp(normalize, middle, gain_two, shift_two)[1]
    middle_part, second_gain_term, second_shift_term = second_pull(back_normed_two)
    back_middle = upstream_float + middle_part
    back_branch = back_middle.astype(jnp.bfloat16)
    outward_bias_term = jnp.sum(back_branch.astype(jnp.float32), axis=0)
    outward_weight_term = inner_rows(attended, back_branch)
    back_attended = outer_cols(back_branch, again_outward).astype(jnp.bfloat16)

    def attend_back(inputs):
        index, log_total = inputs
        start = index * HD
        head_query = lax.dynamic_slice_in_dim(queries, start, HD, 1)
        head_key = lax.dynamic_slice_in_dim(keys_all, start, HD, 1)
        head_value = lax.dynamic_slice_in_dim(values_all, start, HD, 1)
        head_upstream = lax.dynamic_slice_in_dim(back_attended, start, HD, 1)
        scores = outer_cols(head_query, head_key) * scale
        probs = jnp.where(allowed, jnp.exp(scores - log_total[:, None]), 0.0)
        back_probs = outer_cols(head_upstream, head_value)
        centre = jnp.sum(probs * back_probs, axis=1, keepdims=True)
        back_scores = (probs * (back_probs - centre)).astype(jnp.bfloat16)
        back_query = jnp.dot(back_scores, head_key, preferred_element_type=jnp.float32) * scale
        back_key = inner_rows(back_scores, head_query) * scale
        back_value = inner_rows(probs.astype(jnp.bfloat16), head_upstream)
        return (back_query, back_key, back_value)

    head_query_grads, head_key_grads, head_value_grads = lax.map(
        attend_back, (jnp.arange(H), log_totals)
    )
    back_queries = head_query_grads.transpose(1, 0, 2).reshape(local_rows, D)
    back_keys_all = head_key_grads.transpose(1, 0, 2).reshape(2 * local_rows, D)
    back_values_all = head_value_grads.transpose(1, 0, 2).reshape(2 * local_rows, D)
    returned_keys, returned_values = (
        passed_along(back_keys_all[:local_rows].astype(jnp.bfloat16), "role", -1).astype(
            jnp.float32
        ),
        passed_along(back_values_all[:local_rows].astype(jnp.bfloat16), "role", -1).astype(
            jnp.float32
        ),
    )
    query_low = back_queries.astype(jnp.bfloat16)
    key_low = (back_keys_all[local_rows:] + returned_keys).astype(jnp.bfloat16)
    value_low = (back_values_all[local_rows:] + returned_values).astype(jnp.bfloat16)
    back_mixed = jnp.concatenate([query_low, key_low, value_low], axis=1)
    query_bias_term = jnp.sum(query_low.astype(jnp.float32), axis=0)
    value_bias_term = jnp.sum(value_low.astype(jnp.float32), axis=0)
    inward_weight_term = inner_rows(normed, back_mixed)
    back_normed = outer_cols(back_mixed, again_inward)
    first_pull = jax.vjp(normalize, current, again_gain, again_shift)[1]
    frame_part, first_gain_term, first_shift_term = first_pull(back_normed)
    frames_gradient = (back_middle + frame_part).astype(jnp.bfloat16)[None]
    totals = (
        lax.psum_scatter(first_gain_term, ("dp", "role"), scatter_dimension=0, tiled=True),
        lax.psum_scatter(first_shift_term, ("dp", "role"), scatter_dimension=0, tiled=True),
        lax.psum_scatter(inward_weight_term, ("dp", "role"), scatter_dimension=0, tiled=True),
        lax.psum_scatter(query_bias_term, ("dp", "role"), scatter_dimension=0, tiled=True),
        lax.psum_scatter(value_bias_term, ("dp", "role"), scatter_dimension=0, tiled=True),
        lax.psum_scatter(outward_weight_term, ("dp", "role"), scatter_dimension=0, tiled=True),
        lax.psum_scatter(outward_bias_term, ("dp", "role"), scatter_dimension=0, tiled=True),
        lax.psum_scatter(second_gain_term, ("dp", "role"), scatter_dimension=0, tiled=True),
        lax.psum_scatter(second_shift_term, ("dp", "role"), scatter_dimension=0, tiled=True),
        lax.psum_scatter(expand_weight_term, ("dp", "role"), scatter_dimension=0, tiled=True),
        lax.psum_scatter(expand_bias_term, ("dp", "role"), scatter_dimension=0, tiled=True),
        lax.psum_scatter(reduce_weight_term, ("dp", "role"), scatter_dimension=0, tiled=True),
        lax.psum_scatter(reduce_bias_term, ("dp", "role"), scatter_dimension=0, tiled=True),
    )
    return (
        result,
        frames_gradient,
        totals[0],
        totals[1],
        totals[2],
        totals[3],
        totals[4],
        totals[5],
        totals[6],
        totals[7],
        totals[8],
        totals[9],
        totals[10],
        totals[11],
        totals[12],
    )


def solution(mesh):
    placed = (
        P("dp", "role", None),
        P("dp", "role", None),
        P("dp"),
        P("dp"),
        P("dp", None),
        P(("dp", "role")),
        P(("dp", "role")),
        P(("dp", "role"), None),
        P(("dp", "role")),
        P(("dp", "role")),
        P(("dp", "role"), None),
        P(("dp", "role")),
        P(("dp", "role")),
        P(("dp", "role")),
        P(("dp", "role"), None),
        P(("dp", "role")),
        P(("dp", "role"), None),
        P(("dp", "role")),
    )
    fused = mesh.shape["dp"] == 16 and mesh.shape["role"] == 2
    return jax.shard_map(
        fused_shards if fused else plain_shards,
        mesh=mesh,
        in_specs=placed,
        out_specs=(
            P("dp", "role", None),
            P("dp", "role", None),
            P(("dp", "role")),
            P(("dp", "role")),
            P(("dp", "role"), None),
            P(("dp", "role")),
            P(("dp", "role")),
            P(("dp", "role"), None),
            P(("dp", "role")),
            P(("dp", "role")),
            P(("dp", "role")),
            P(("dp", "role"), None),
            P(("dp", "role")),
            P(("dp", "role"), None),
            P(("dp", "role")),
        ),
        check_vma=False,
    )
```

```python
import functools

import jax
import jax.numpy as jnp
from jax import lax
from jax.experimental import pallas as pl
from jax.experimental.pallas import tpu as pltpu
from jax.sharding import PartitionSpec as P

D = 1024
H = 16
HD = 64
EPS = 1e-05
MASKED = -1e30
LOG2E = 1.4426950408889634
BF = jnp.bfloat16
F32 = jnp.float32
MESH = pl.DeviceIdType.MESH


def dot(left, right):
    return lax.dot_general(left, right, (((1,), (0,)), ((), ())), preferred_element_type=F32)


def dot_nt(left, right):
    return lax.dot_general(left, right, (((1,), (1,)), ((), ())), preferred_element_type=F32)


def flip(value):
    return value.astype(F32).T.astype(value.dtype)


def centre(values):
    mean_value = jnp.mean(values, axis=-1, keepdims=True)
    centered = values - mean_value
    spread = jnp.mean(centered * centered, axis=-1, keepdims=True)
    return centered * lax.rsqrt(spread + EPS), lax.rsqrt(spread + EPS)


def norm_back(unit, rate, gain, upstream):
    pulled = upstream * gain
    first = jnp.mean(pulled, axis=-1, keepdims=True)
    second = jnp.mean(pulled * unit, axis=-1, keepdims=True)
    return rate * (pulled - first - unit * second)


LEAD = 1
EARLY_CHUNK = 2
LOOK = 2
LAG_IN = 7
LAG_FF = 7
RED_SPLIT = (0, 0, 0, 0)


def scratch_list():
    dma = pltpu.SemaphoreType.DMA
    v = pltpu.VMEM
    return dict(
        small=v((4, 2, 2, 2, 16, 128), BF),
        vec=v((8, 1024), F32),
        ebias=v((4, 8, 512), F32),
        frames_all=v((2, 384, 1024), BF),
        c_all=v((2, 384, 1024), BF),
        n_all=v((2, 384, 1024), BF),
        n1t=v((1024, 768), BF),
        n2t=v((1024, 768), BF),
        win=v((6, 4, 2, 2, 64, 256), BF),
        wout=v((4, 2, 2, 2, 32, 1024), BF),
        wexp=v((4, 4, 2, 2, 64, 512), BF),
        wred=v((4, 4, 4, 32, 1024), BF),
        qkv=v((3, 4, 768, 128), BF),
        mask=v((768, 768), BF),
        lse=v((4, 6, 8, 256), F32),
        half=v((2, 384, 512), BF),
        half_t=v((2, 512, 384), BF),
        wide=v((384, 1024), BF),
        att_t=v((1024, 384), BF),
        middle=v((384, 1024), F32),
        out_acc=v((2, 384, 1024), F32),
        bn_acc=v((2, 384, 1024), F32),
        cross=v((384, 1024), F32),
        ffb=v((3, 768, 512), BF),
        act_t=v((512, 768), BF),
        ba_all=v((2, 384, 512), BF),
        dkv=v((2, 768, 128), F32),
        gvec=v((8, 1024), F32),
        gexp=v((4, 8, 512), F32),
        outx=v((4, 2, 2, 32, 1024), BF),
        rb=v((4, 2, 4, 64, 512), BF),
        ra=v((4, 64, 512), BF),
        rz=v((4, 6, 64, 512), BF),
        rx=v((4, 2, 64, 512), BF),
        ra_in=v((6, 4, 64, 256), BF),
        rz_in=v((6, 3, 64, 256), BF),
        rb_red=v((4, 2, 4, 32, 1024), BF),
        land=v((4, 7, 32, 1024), BF),
        rb_out=v((2, 4, 32, 1024), BF),
        ra_out=v((4, 32, 1024), BF),
        rz_out=v((3, 32, 1024), BF),
        sg=v((4, 2, 2, 16, 128), F32),
        rb_sg=v((2, 4, 16, 128), F32),
        ra_sg=v((4, 16, 128), F32),
        rz_sg=v((3, 16, 128), F32),
        fin=v((4, 64, 512), F32),
        fin_in=v((4, 32, 512), F32),
        fin_w=v((6, 64, 256), F32),
        fin_w_in=v((6, 32, 256), F32),
        sfin=v((16, 128), F32),
        sfin_in=v((16, 128), F32),
        own_s=dma((7,)),
        pre_s=dma((13,)),
        pre_r=dma((13,)),
        agz_s=dma((16, 3)),
        agz_r=dma((16, 3)),
        agy_s=dma((16, 3)),
        agy_r=dma((16, 3)),
        agx_s=dma((16, 2)),
        aga_s=dma((16,)),
        aga_r=dma((16,)),
        agb_s=dma((16, 2)),
        agb_r=dma((16, 2)),
        core_s=dma((9,)),
        core_r=dma((9,)),
        rsb_s=dma((16, 2)),
        rsb_r=dma((16, 2)),
        rsa_s=dma((16,)),
        rsa_r=dma((16,)),
        rsz_s=dma((16, 3)),
        rsz_r=dma((16, 3)),
        rsy_s=dma((16, 3)),
        rsy_r=dma((16, 3)),
        rsx_s=dma((16, 2)),
        rsx_r=dma((16, 2)),
        fin_s=dma((11,)),
        fin_r=dma((11,)),
    )


class Bag:
    def __init__(self, **kw):
        self.__dict__.update(kw)


N_IN = 10
N_OUT = 7


def layer_kernel(names, *refs):
    (phon_ref, prom_ref, seg_ref, frames_ref, cot_ref, small_in, win_in, wout_in, wexp_in, wred_in) = refs[:N_IN]
    (result_ref, fgrad_ref, dwin_ref, dwout_ref, dwexp_ref, dwred_ref, dsmall_ref) = refs[N_IN : N_IN + N_OUT]
    s = Bag(**dict(zip(names, refs[N_IN + N_OUT :])))

    dp = lax.axis_index("dp")
    r = lax.axis_index("role")
    o = 1 - r
    z, y, x = dp // 4, (dp // 2) % 2, dp % 2
    ya, xa = y + r * (1 - 2 * y), x + (1 - r) * (1 - 2 * x)
    yb, xb = y + (1 - r) * (1 - 2 * y), x + r * (1 - 2 * x)
    yc, xc = 1 - y, 1 - x
    core_dev = (dp, o)
    a_dev = (z * 4 + ya * 2 + xa, r)
    b_dev = (z * 4 + yb * 2 + xb, r)
    z_dev = [(((z + k) % 4) * 4 + y * 2 + x, r) for k in (1, 2, 3)]
    z_at = [(z + k) % 4 for k in (1, 2, 3)]
    z_from = [(z + 4 - k) % 4 for k in (1, 2, 3)]
    at_end = (z == 0) | (z == 3)
    in_middle = (z == 1) | (z == 2)
    far = z_from[1]
    far_end = (jnp.where(z == 2, 3, 0) * 4 + y * 2 + x, r)
    near_middle = (jnp.where(z == 0, 1, 2) * 4 + y * 2 + x, r)
    place = 2 * y + x

    def copy(src, dst, ss, rs, dev):
        return pltpu.make_async_remote_copy(
            src_ref=src, dst_ref=dst, send_sem=ss, recv_sem=rs, device_id=dev, device_id_type=MESH
        )

    barrier = pltpu.get_barrier_semaphore()
    for dev in z_dev + [a_dev, b_dev, core_dev]:
        pl.semaphore_signal(barrier, inc=1, device_id=dev, device_id_type=MESH)
    pl.semaphore_wait(barrier, 6)

    my_rows = pl.ds(pl.multiple_of(r * 32, 32), 32)
    o_rows = pl.ds(pl.multiple_of(o * 32, 32), 32)

    def part_cols(part, who):
        return pl.ds(pl.multiple_of((part // 2) * 1024 + who * 512 + (part % 2) * 256, 256), 256)

    pre = []
    pre.append(copy(small_in, s.small.at[z, y, x, r], s.pre_s.at[0], s.pre_r.at[0], core_dev))
    for i in range(6):
        pre.append(
            copy(
                win_in.at[:, part_cols(i, o)],
                s.win.at[i, z, y, x, my_rows],
                s.pre_s.at[1 + i],
                s.pre_r.at[1 + i],
                core_dev,
            )
        )
    pre.append(copy(frames_ref, s.frames_all.at[r], s.pre_s.at[7], s.pre_r.at[7], core_dev))
    for j in range(4):
        pre.append(
            copy(
                s.half.at[o, j * 32 : (j + 1) * 32],
                s.wexp.at[j, z, y, x, my_rows],
                s.pre_s.at[8 + j],
                s.pre_r.at[8 + j],
                core_dev,
            )
        )
    pre.append(copy(cot_ref, s.c_all.at[r], s.pre_s.at[12], s.pre_r.at[12], core_dev))
    for item in pre[:8]:
        item.start()
    group_32 = lax.broadcasted_iota(jnp.int32, (32, 128), 1) // 32

    def pick(parts, group):
        picked = parts[3]
        for g in range(3):
            picked = jnp.where(group == g, parts[g], picked)
        return picked

    for who in range(2):
        for block in range(4):
            source = [
                wexp_in[:, (2 * (4 * block + q) + who) * 128 : (2 * (4 * block + q) + who + 1) * 128].astype(F32)
                for q in range(4)
            ]
            for j in range(4):
                chosen = pick([source[(g + j) % 4] for g in range(4)], group_32)
                s.half[who, j * 32 : (j + 1) * 32, block * 128 : (block + 1) * 128] = chosen.astype(BF)
    for item in pre[8:]:
        item.start()
    own_frames = pltpu.make_async_copy(frames_ref, s.frames_all.at[r], s.own_s.at[0])
    own_cot = pltpu.make_async_copy(cot_ref, s.c_all.at[r], s.own_s.at[1])
    own_frames.start()
    own_cot.start()
    own_more = [pltpu.make_async_copy(wout_in, s.wout.at[z, y, x, r], s.own_s.at[2])]
    for j in range(4):
        group = (place + 4 - j) % 4
        rows = pl.ds(pl.multiple_of(group * 32, 32), 32)
        own_more.append(pltpu.make_async_copy(wred_in.at[rows], s.wred.at[j, z, group], s.own_s.at[3 + j]))
    for item in own_more:
        item.start()
    s.small[z, y, x, r] = small_in[...]
    for i in range(6):
        s.win[i, z, y, x, my_rows] = win_in[:, part_cols(i, r)]
    for j in range(4):
        s.wexp[j, z, y, x, my_rows] = s.half[r, j * 32 : (j + 1) * 32]

    def ag_item(t, piece, col, split):
        return Bag(t=t, piece=piece, col=col, split=split)

    def slot(j, b, c):
        return (2 * b + c + 4 - j) % 4

    gathers = [ag_item(0, lambda a, b, c: s.small.at[a, b, c], lambda b, c: s.small.at[:, b, c], False)]
    for i in range(6):
        gathers.append(
            ag_item(
                1 + i, lambda a, b, c, i=i: s.win.at[i, a, b, c], lambda b, c, i=i: s.win.at[i, :, b, c], False
            )
        )
    gathers.append(ag_item(7, lambda a, b, c: s.wout.at[a, b, c, r], lambda b, c: s.wout.at[:, b, c, r], False))
    for j in range(4):
        gathers.append(
            ag_item(
                8 + 2 * j, lambda a, b, c, j=j: s.wexp.at[j, a, b, c], lambda b, c, j=j: s.wexp.at[j, :, b, c], True
            )
        )
        gathers.append(
            ag_item(
                9 + 2 * j,
                lambda a, b, c, j=j: s.wred.at[j, a, slot(j, b, c)],
                lambda b, c, j=j: s.wred.at[j, :, slot(j, b, c)],
                bool(RED_SPLIT[j]),
            )
        )

    def when(cond, go):
        if isinstance(cond, bool):
            if cond:
                go()
        else:
            pl.when(cond)(go)

    def z_copies(it, yy, xx, ss, rs):
        p = it.piece(z, yy, xx)
        return [copy(p, p, ss.at[it.t, k], rs.at[it.t, k], z_dev[k]) for k in range(3)]

    def straight(it, k):
        if not it.split or k == 1:
            return True
        return z != 3 if k == 0 else z != 0

    def z_start(it, yy, xx, ss, rs):
        for k, c in enumerate(z_copies(it, yy, xx, ss, rs)):
            when(straight(it, k), c.start)

    def z_relay(it, yy, xx, rs, which):
        p = it.piece(far, yy, xx)

        @pl.when(in_middle)
        def _():
            copy(p, p, s.agx_s.at[it.t, which], rs.at[it.t, 1], far_end).wait_recv()
            copy(p, p, s.agx_s.at[it.t, which], rs.at[it.t, jnp.where(z == 2, 2, 0)], far_end).start()

    def z_wait(it, yy, xx, ss, rs):
        for k in range(3):
            p = it.piece(z_from[k], yy, xx)
            c = copy(p, p, ss.at[it.t, k], rs.at[it.t, k], z_dev[k])
            when(at_end if it.split and k == 1 else True, c.wait_recv)

    def z_sent(it, yy, xx, ss, rs, which):
        for k, c in enumerate(z_copies(it, yy, xx, ss, rs)):
            when(straight(it, k), c.wait_send)
        if it.split:
            p = it.piece(far, yy, xx)
            pl.when(in_middle)(copy(p, p, s.agx_s.at[it.t, which], rs.at[it.t, 0], far_end).wait_send)

    def a_piece(it, yy, xx):
        p = it.piece(z, yy, xx)
        return copy(p, p, s.aga_s.at[it.t], s.aga_r.at[it.t], a_dev)

    def a_copy(it, yy, xx):
        return copy(it.col(yy, xx), it.col(yy, xx), s.aga_s.at[it.t], s.aga_r.at[it.t], a_dev)

    def b_copy(it, which, yy, xx):
        return copy(it.col(yy, xx), it.col(yy, xx), s.agb_s.at[it.t, which], s.agb_r.at[it.t, which], b_dev)

    def e0(it):
        if it.split:
            a_piece(it, y, x).start()
        z_start(it, y, x, s.agz_s, s.agz_r)

    def e1(it):
        if it.split:
            z_relay(it, y, x, s.agz_r, 0)
            a_piece(it, ya, xa).wait_recv()
            z_start(it, ya, xa, s.agy_s, s.agy_r)
            return
        z_wait(it, y, x, s.agz_s, s.agz_r)
        a_copy(it, y, x).start()
        b_copy(it, 0, y, x).start()

    def e2(it):
        if it.split:
            z_relay(it, ya, xa, s.agy_r, 1)
            z_wait(it, y, x, s.agz_s, s.agz_r)
            b_copy(it, 0, y, x).start()
            z_wait(it, ya, xa, s.agy_s, s.agy_r)
            b_copy(it, 1, ya, xa).start()
            return
        a_copy(it, ya, xa).wait_recv()
        b_copy(it, 1, ya, xa).start()

    def e3(it):
        b_copy(it, 0, yb, xb).wait_recv()
        b_copy(it, 1, yc, xc).wait_recv()

    def sent(it):
        z_sent(it, y, x, s.agz_s, s.agz_r, 0)
        if it.split:
            a_piece(it, y, x).wait_send()
            z_sent(it, ya, xa, s.agy_s, s.agy_r, 1)
        else:
            a_copy(it, y, x).wait_send()
        b_copy(it, 0, y, x).wait_send()
        b_copy(it, 1, ya, xa).wait_send()

    def pre_in(index, dst):
        copy(dst, dst, s.pre_s.at[index], s.pre_r.at[index], core_dev).wait_recv()

    def ready(i):
        if i == 0:
            pre_in(0, s.small.at[z, y, x, o])
        elif i < 7:
            pre_in(i, s.win.at[i - 1, z, y, x, o_rows])
        elif i >= 8 and i % 2 == 0:
            j = (i - 8) // 2
            pre_in(8 + j, s.wexp.at[j, z, y, x, o_rows])

    done = []

    def ahead(count):
        for i in range(len(done), count + 1):
            done.append(i)
            for event, lag in ((e0, 0), (e1, LOOK), (e2, 2 * LOOK)):
                if 0 <= i - lag < len(gathers):
                    if lag == 0:
                        ready(i)
                    event(gathers[i - lag])

    def arrive(i, lag):
        ahead(i + lag)
        e3(gathers[i])

    ahead(2)

    for edge, k in ((0, 0), (3, 2)):

        @pl.when(z == edge)
        def _(k=k):
            for base in (0, 3):
                s.rz[:, base + k] = jnp.zeros((4, 64, 512), BF)
                for j in range(4):
                    if RED_SPLIT[j]:
                        s.land[j, 1 + base + k] = jnp.zeros((32, 1024), BF)

    own_frames.wait()
    own_cot.wait()
    for item in own_more:
        item.wait()
    prefix = phon_ref[0] + prom_ref[0]
    seg_row = seg_ref[...].astype(F32)
    seg_wide = jnp.broadcast_to(seg_row, (384, 384))
    seg_tall = seg_wide.T
    key_at = lax.broadcasted_iota(jnp.int32, (384, 384), 0)
    row_at = lax.broadcasted_iota(jnp.int32, (384, 384), 1)
    causal = key_at <= row_at
    seen = key_at < prefix

    def as_bias(allowed):
        return jnp.where(allowed, 0.0, MASKED).astype(BF)

    s.mask[0:384, 0:384] = as_bias(causal & seen)
    s.mask[0:384, 384:768] = as_bias(seen)
    s.mask[384:768, 384:768] = as_bias(causal & (seg_wide == seg_tall))

    arrive(0, LAG_IN)

    def tile_sum(q):
        total = jnp.zeros((16, 128), F32)
        for xx in range(2):
            for who in range(2):
                total = total + s.small[q // 2, q % 2, xx, who].astype(F32)
        return total

    for q in range(8):
        s.vec[:, q * 128 : (q + 1) * 128] = tile_sum(q)[0:8]
    group_1 = lax.broadcasted_iota(jnp.int32, (1, 128), 1) // 32
    for block in range(4):
        tiles = [s.small[block, q // 2, q % 2, r].astype(F32)[8:9] for q in range(4)]
        for j in range(4):
            s.ebias[j, 0:1, block * 128 : (block + 1) * 128] = pick([tiles[(g + j) % 4] for g in range(4)], group_1)

    def vec_row(i):
        return s.vec[i : i + 1, :]

    pre_in(7, s.frames_all.at[o])

    def norm_tile(i, carry):
        who, rows = i // 3, pl.ds(pl.multiple_of((i % 3) * 128, 128), 128)
        unit, _ = centre(s.frames_all[who, rows].astype(F32))
        normed = unit * vec_row(0) + vec_row(1)
        s.n_all[who, rows] = normed.astype(BF)
        s.n1t[:, pl.ds(pl.multiple_of(i * 128, 128), 128)] = normed.T.astype(BF)
        return carry

    lax.fori_loop(0, 6, norm_tile, 0)

    def project(part):
        section, n = part // 2, part % 2
        mixed = dot(s.n_all[...].reshape(768, 1024), s.win[part].reshape(1024, 256))
        if section != 1:
            bias_at = pl.ds(pl.multiple_of(r * 512 + n * 256, 256), 256)
            bias_row = 2 if section == 0 else 3
            mixed = mixed + s.vec[bias_row : bias_row + 1, bias_at]
        mixed = mixed.astype(BF)
        s.qkv[section, 2 * n] = mixed[:, 0:128]
        s.qkv[section, 2 * n + 1] = mixed[:, 128:256]

    for part in range(6):
        arrive(1 + part, LAG_IN)
        project(part)

    factor = HD**-0.5 * LOG2E
    low_lane = lax.broadcasted_iota(jnp.int32, (128, 128), 1) < 64

    def pair_rows(block):
        zero = jnp.zeros_like(block)
        return jnp.concatenate([jnp.where(low_lane, block, zero), jnp.where(low_lane, zero, block)], axis=0)

    def pair_mask(keys, rb):
        bias = s.mask[0:keys, rb * 128 : (rb + 1) * 128].astype(F32)
        return jnp.concatenate([bias, bias], axis=1)

    def key_count(rb):
        return (rb + 1) * 128 if rb < 3 else 384 + (rb - 2) * 128

    def attend(hp, carry):
        v_t = flip(s.qkv[2, hp])
        dims = pl.ds(pl.multiple_of(hp * 128, 128), 128)
        for rb in range(6):
            keys = key_count(rb)
            both = pair_rows(s.qkv[0, hp, rb * 128 : (rb + 1) * 128])
            scores = dot_nt(s.qkv[1, hp, 0:keys], both) * factor + pair_mask(keys, rb)
            peak = jnp.max(scores, axis=0, keepdims=True)
            expo = jnp.exp2(scores - peak)
            total = jnp.sum(expo, axis=0, keepdims=True)
            heads = dot(v_t[:, 0:keys], expo.astype(BF)) / total
            s.lse[hp, rb] = jnp.broadcast_to(peak + jnp.log2(total), (8, 256))
            out = jnp.concatenate([heads[0:64, 0:128], heads[64:128, 128:256]], axis=0)
            at = (rb % 3) * 128
            s.half_t[rb // 3, dims, at : at + 128] = out.astype(BF)
            s.half[rb // 3, at : at + 128, dims] = out.T.astype(BF)
        return carry

    for j in range(4):
        pre[8 + j].wait_send()
    lax.fori_loop(0, 2, attend, 0)
    ahead(6 + LAG_IN + 1)
    lax.fori_loop(2, 4, attend, 0)
    ahead(6 + LAG_IN + 2)

    my_half = pl.ds(pl.multiple_of(r * 512, 512), 512)
    o_half = pl.ds(pl.multiple_of(o * 512, 512), 512)

    def core_copy(index, src, dst):
        return copy(src, dst, s.core_s.at[index], s.core_r.at[index], core_dev)

    core_copy(0, s.half.at[o], s.wide.at[:, my_half]).start()
    core_copy(1, s.half_t.at[o], s.att_t.at[my_half]).start()
    s.wide[:, my_half] = s.half[r]
    s.att_t[my_half] = s.half_t[r]
    arrive(7, LAG_FF)
    out_swap = core_copy(2, s.wout.at[:, :, :, r], s.wout.at[:, :, :, r])
    out_swap.start()
    core_copy(0, s.wide.at[:, o_half], s.wide.at[:, o_half]).wait_recv()
    core_copy(1, s.att_t.at[o_half], s.att_t.at[o_half]).wait_recv()
    core_copy(2, s.wout.at[:, :, :, o], s.wout.at[:, :, :, o]).wait_recv()
    def out_tile(n, carry):
        cols = pl.ds(pl.multiple_of(n * 256, 256), 256)
        branch = dot(s.wide[...], s.wout[:, :, :, :, :, cols].reshape(1024, 256))
        s.middle[:, cols] = s.frames_all[r, :, cols].astype(F32) + branch + s.vec[4:5, cols]
        return carry

    lax.fori_loop(0, 4, out_tile, 0)

    def norm_two(i, carry):
        rows = pl.ds(pl.multiple_of(i * 128, 128), 128)
        unit, _ = centre(s.middle[rows])
        s.n_all[r, rows] = (unit * vec_row(5) + vec_row(6)).astype(BF)
        return carry

    lax.fori_loop(0, 3, norm_two, 0)
    core_copy(3, s.n_all.at[r], s.n_all.at[r]).start()
    pre_in(12, s.c_all.at[o])
    s.out_acc[...] = jnp.zeros_like(s.out_acc)
    s.bn_acc[...] = jnp.zeros_like(s.bn_acc)
    core_copy(3, s.n_all.at[o], s.n_all.at[o]).wait_recv()
    core_copy(3, s.n_all.at[r], s.n_all.at[r]).wait_send()

    def flip_two(i, carry):
        who, rows = i // 3, pl.ds(pl.multiple_of((i % 3) * 128, 128), 128)
        s.n2t[:, pl.ds(pl.multiple_of(i * 128, 128), 128)] = flip(s.n_all[who, rows])
        return carry

    lax.fori_loop(0, 6, flip_two, 0)

    def rs_exp(j):
        return Bag(
            t=j, fin=j, split=True, piece=lambda a, b, c: s.wexp.at[j, a, b, c],
            col=lambda b, c: s.wexp.at[j, :, b, c], rb=lambda w: s.rb.at[j, w], ra=s.ra.at[j],
            rz=lambda k: s.rz.at[j, k], rx=lambda w: s.rx.at[j, w],
        )

    def rs_in(i):
        slot, part = ((0, 0), (0, 1), (1, 0), (1, 1), (2, 0), (2, 1))[i]
        half = slice(256 * part, 256 * part + 256)
        return Bag(
            t=9 + i, fin=4 + i, split=False, piece=lambda a, b, c: s.win.at[i, a, b, c],
            col=lambda b, c: s.win.at[i, :, b, c], rb=lambda w: s.rb.at[slot, w, :, :, half],
            ra=s.ra_in.at[i], rz=lambda k: s.rz_in.at[i, k],
        )

    def rs_red(j):
        split = bool(RED_SPLIT[j])
        return Bag(
            t=4 + j, fin=None, split=split, piece=lambda a, b, c: s.wred.at[j, a, slot(j, b, c)],
            col=lambda b, c: s.wred.at[j, :, slot(j, b, c)], rb=lambda w: s.rb_red.at[j, w],
            ra=s.land.at[j, 0] if split else s.land.at[j, 0:4],
            rz=lambda k: s.land.at[j, k + (1 if split else 4)], rx=lambda w: s.land.at[j, 7 + w],
        )

    def rs_out():
        return Bag(
            t=8, fin=None, split=False, piece=lambda a, b, c: s.wout.at[a, b, c, r],
            col=lambda b, c: s.wout.at[:, b, c, r], rb=lambda w: s.rb_out.at[w], ra=s.ra_out,
            rz=lambda k: s.rz_out.at[k],
        )

    def rs_small():
        return Bag(
            t=15, fin=None, split=False, piece=lambda a, b, c: s.sg.at[a, b, c],
            col=lambda b, c: s.sg.at[:, b, c], rb=lambda w: s.rb_sg.at[w], ra=s.ra_sg,
            rz=lambda k: s.rz_sg.at[k],
        )

    def rb_copy(it, which, yy, xx):
        return copy(it.col(yy, xx), it.rb(which), s.rsb_s.at[it.t, which], s.rsb_r.at[it.t, which], b_dev)

    def ra_copy(it):
        src = it.piece(z, ya, xa) if it.split else it.col(ya, xa)
        return copy(src, it.ra, s.rsa_s.at[it.t], s.rsa_r.at[it.t], a_dev)

    def add_into(it, yy, xx, sources):
        target = it.col(yy, xx)
        kind = F32 if it.t == 15 else BF

        def body(i, carry):
            total = target[i].astype(F32)
            for src in sources:
                total = total + src[i].astype(F32)
            target[i] = total.astype(kind)
            return carry

        lax.fori_loop(0, 4, body, 0)

    def own_copy(it, k, yy, xx, base, ss, rs):
        return copy(it.piece(z_at[k], yy, xx), it.rz(base + k), ss.at[it.t, k], rs.at[it.t, k], z_dev[k])

    def far_copy(it, k, yy, xx, which):
        return copy(
            it.piece(z_at[k], yy, xx), it.rx(which), s.rsx_s.at[it.t, which], s.rsx_r.at[it.t, which], near_middle
        )

    def own_start(it, yy, xx, base, ss, rs, which):
        for k in range(3):
            c = own_copy(it, k, yy, xx, base, ss, rs)
            if not it.split:
                c.start()
            elif k == 1:
                pl.when(at_end)(c.start)
            else:
                edge = 3 if k == 0 else 0
                pl.when(z != edge)(c.start)
                pl.when(z == edge)(far_copy(it, k, yy, xx, which).start)

    def own_relay(it, yy, xx, base, ss, rs, which):
        @pl.when(in_middle)
        def _():
            far_copy(it, 1, yy, xx, which).wait_recv()
            held = it.piece(z_at[1], yy, xx)
            held[...] = (held[...].astype(F32) + it.rx(which)[...].astype(F32)).astype(BF)
            own_copy(it, 1, yy, xx, base, ss, rs).start()

    def own_wait(it, yy, xx, base, ss, rs):
        for k in range(3):
            c = own_copy(it, k, yy, xx, base, ss, rs)
            if not it.split or k == 1:
                c.wait_recv()
            else:
                pl.when(z != (0 if k == 0 else 3))(c.wait_recv)

    def own_sent(it, yy, xx, base, ss, rs, which):
        for k in range(3):
            c = own_copy(it, k, yy, xx, base, ss, rs)
            if not it.split or k == 1:
                c.wait_send()
            else:
                edge = 3 if k == 0 else 0
                pl.when(z != edge)(c.wait_send)
                pl.when(z == edge)(far_copy(it, k, yy, xx, which).wait_send)

    def z_args(it, second):
        if second:
            return (ya, xa, 3, s.rsy_s, s.rsy_r)
        return (y, x, 0, s.rsz_s, s.rsz_r)

    def z_total(it, second):
        yy, xx, base, ss, rs = z_args(it, second)
        own_wait(it, yy, xx, base, ss, rs)
        total = it.piece(z, yy, xx)[...].astype(F32)
        for k in range(3):
            total = total + it.rz(base + k)[...].astype(F32)
        return total

    def f0(it):
        rb_copy(it, 0, yc, xc).start()
        rb_copy(it, 1, yb, xb).start()

    def f1(it):
        rb_copy(it, 0, yc, xc).wait_recv()
        add_into(it, ya, xa, [it.rb(0)])
        if not it.split:
            ra_copy(it).start()
            return
        own_start(it, *z_args(it, True), 1)
        rb_copy(it, 1, yb, xb).wait_recv()
        add_into(it, y, x, [it.rb(1)])
        own_start(it, *z_args(it, False), 0)

    def f2(it):
        if it.split:
            own_relay(it, *z_args(it, True), 1)
            own_relay(it, *z_args(it, False), 0)
            return
        rb_copy(it, 1, yb, xb).wait_recv()
        ra_copy(it).wait_recv()
        add_into(it, y, x, [it.rb(1), it.ra])
        own_start(it, *z_args(it, False), 0)

    def f3(it):
        if it.split:
            total = z_total(it, True)
            it.piece(z, ya, xa)[...] = total.astype(BF)
            ra_copy(it).start()

    def full_total(it):
        total = z_total(it, False)
        if it.split:
            ra_copy(it).wait_recv()
            total = total + it.ra[...].astype(F32)
        return total

    def fin_refs(index):
        if index < 4:
            return s.fin.at[index], s.fin_in.at[index]
        return s.fin_w.at[index - 4], s.fin_w_in.at[index - 4]

    def fin_copy(index):
        out, back = fin_refs(index)
        return copy(out.at[o_rows], back, s.fin_s.at[index], s.fin_r.at[index], core_dev)

    def small_fin():
        return copy(s.sfin, s.sfin_in, s.fin_s.at[10], s.fin_r.at[10], core_dev)

    def put_in(i, value, who):
        dwin_ref[:, part_cols(i, who)] = value

    def put_exp(source, who):
        for block in range(4):
            at = slice(block * 128, (block + 1) * 128)
            chunk = [source(j)[:, at] for j in range(4)]
            for q in range(4):
                cols = pl.ds(pl.multiple_of((2 * (4 * block + q) + who) * 128, 128), 128)
                dwexp_ref[:, cols] = pick([chunk[(q - g) % 4] for g in range(4)], group_32)

    def f4(it):
        if 4 <= it.t < 8:
            group = (place + 8 - it.t) % 4
            dwred_ref[pl.ds(pl.multiple_of(group * 32, 32), 32)] = full_total(it)
        elif it.t == 8:
            dwout_ref[...] = full_total(it)
        elif it.t == 15:
            s.sfin[...] = full_total(it)
            small_fin().start()
        else:
            out, _ = fin_refs(it.fin)
            out[...] = full_total(it)
            fin_copy(it.fin).start()
            if it.fin >= 4:
                put_in(it.fin - 4, out[my_rows], r)

    def f5(it):
        if it.fin is not None:
            fin_copy(it.fin).wait_recv()
            if it.fin >= 4:
                put_in(it.fin - 4, fin_refs(it.fin)[1][...], o)
            elif it.fin == 3:
                put_exp(lambda j: s.fin[j, my_rows], r)
                put_exp(lambda j: s.fin_in[j], o)
        elif it.t == 15:
            small_fin().wait_recv()
            row = lax.broadcasted_iota(jnp.int32, (16, 128), 0)
            own = s.sfin[...]
            dsmall_ref[...] = jnp.where(row < 8, own + s.sfin_in[...], own)

    def all_sent(it):
        rb_copy(it, 0, yc, xc).wait_send()
        rb_copy(it, 1, yb, xb).wait_send()
        ra_copy(it).wait_send()
        own_sent(it, *z_args(it, False), 0)
        if it.split:
            own_sent(it, *z_args(it, True), 1)
        if it.fin is not None:
            fin_copy(it.fin).wait_send()
        elif it.t == 15:
            small_fin().wait_send()

    order = []
    for j in range(4):
        order += [rs_red(j), rs_exp(j)]
    order += [rs_out()] + [rs_in(i) for i in range(3)] + [rs_small()] + [rs_in(i) for i in range(3, 6)]

    def step(i):
        for event, lag in ((f0, -LEAD), (f1, 1), (f2, 2), (f3, 3), (f4, 5), (f5, 6)):
            if 0 <= i - lag < len(order):
                event(order[i - lag])

    stepped = []

    def next_step():
        step(len(stepped))
        stepped.append(True)

    def feed(j, between):
        if j == 3 and EARLY_CHUNK == 3:
            for it in order[:LEAD]:
                f0(it)
        arrive(8 + 2 * j, LAG_FF)
        arrive(9 + 2 * j, LAG_FF)
        sent(gathers[8 + 2 * j])
        sent(gathers[9 + 2 * j])
        between(0)

        def hidden(n, inside):
            cols = pl.ds(pl.multiple_of(n * 256, 256), 256)
            left = s.n_all[...].reshape(768, 1024)
            inner = dot(left, s.wexp[j, :, :, :, :, cols].reshape(1024, 256)) + s.ebias[j, 0:1, cols]
            phi = 0.5 + 0.5 * lax.erf(inner * (2.0**-0.5))
            active = inner * phi
            s.ffb[0, :, cols] = active.astype(BF)
            s.act_t[cols] = active.T.astype(BF)
            slope = phi + inner * (jnp.exp(-0.5 * inner * inner) * 0.3989422804014327)
            up = s.c_all[...].reshape(768, 1024)
            weight = s.wred[j, pl.ds(2 * n, 2)].reshape(256, 1024)
            back = (dot_nt(up, weight) * slope).astype(BF)
            s.ffb[1, :, cols] = back
            s.gexp[j, 0:1, cols] = jnp.sum(back.astype(F32), axis=0, keepdims=True)
            return inside

        lax.fori_loop(0, 2, hidden, 0)

        def wide_tile(n, inside):
            cols = pl.ds(pl.multiple_of(n * 256, 256), 256)
            part = dot(s.ffb[0], s.wred[j, :, :, :, cols].reshape(512, 256))
            s.out_acc[:, :, cols] += part.reshape(2, 384, 256)
            back = dot_nt(s.ffb[1], s.wexp[j, n].reshape(256, 512))
            s.bn_acc[:, :, cols] += back.reshape(2, 384, 256)
            return inside

        ahead(9 + 2 * j + LAG_FF + 1)
        if j == EARLY_CHUNK == 2:
            for it in order[:LEAD]:
                f0(it)
        lax.fori_loop(0, 4, wide_tile, 0)
        between(1)

        def grad_red(n, inside):
            cols = pl.ds(pl.multiple_of(n * 256, 256), 256)
            up = s.c_all[:, :, cols].reshape(768, 256)
            s.wred[j, :, :, :, cols] = dot(s.act_t[...], up).astype(BF).reshape(4, 4, 32, 256)
            return inside

        lax.fori_loop(0, 4, grad_red, 0)

        def grad_exp(n, inside):
            cols = pl.ds(pl.multiple_of(n * 256, 256), 256)
            grad = dot(s.n2t[...], s.ffb[1, :, cols]).astype(BF)
            s.wexp[j, :, :, :, :, cols] = grad.reshape(4, 2, 2, 64, 256)
            return inside

        lax.fori_loop(0, 2, grad_exp, 0)
        between(2)

    for j in range(3):
        feed(j, lambda place: None)

    def start_reduction(place_in):
        if place_in == 0:
            next_step()
        elif place_in == 1:
            core_copy(4, s.bn_acc.at[o], s.cross).start()
            next_step()
        else:
            next_step()

    feed(3, start_reduction)

    core_copy(4, s.bn_acc.at[o], s.cross).wait_recv()
    s.n_all[o] = s.out_acc[o].astype(BF)
    core_copy(5, s.n_all.at[o], s.n_all.at[o]).start()

    def middle_back(i, carry):
        rows = pl.ds(pl.multiple_of(i * 128, 128), 128)
        unit, rate = centre(s.middle[rows])
        upstream = s.bn_acc[r, rows] + s.cross[rows]
        cot = s.c_all[r, rows].astype(F32)
        back = cot + norm_back(unit, rate, vec_row(5), upstream)
        s.bn_acc[r, rows] = back
        branch = back.astype(BF)
        s.wide[rows] = branch
        gain_t, shift_t, out_t, red_t = carry
        return (
            gain_t + jnp.sum(upstream * unit, axis=0, keepdims=True),
            shift_t + jnp.sum(upstream, axis=0, keepdims=True),
            out_t + jnp.sum(branch.astype(F32), axis=0, keepdims=True),
            red_t + jnp.sum(cot, axis=0, keepdims=True),
        )

    zero_row = jnp.zeros((1, 1024), F32)
    gain_t, shift_t, out_t, red_t = lax.fori_loop(0, 3, middle_back, (zero_row,) * 4)
    s.gvec[5:6] = gain_t
    s.gvec[6:7] = shift_t
    s.gvec[4:5] = out_t
    s.gvec[7:8] = red_t

    core_copy(0, s.half.at[o], s.half.at[o]).wait_send()
    core_copy(2, s.wout.at[:, :, :, r], s.wout.at[:, :, :, r]).wait_send()

    def back_att(n, carry):
        weight = s.wout[n].reshape(256, 1024)
        cols = pl.ds(pl.multiple_of((n % 2) * 256, 256), 256)
        s.half[n // 2, :, cols] = dot_nt(s.wide[...], weight).astype(BF)
        return carry

    lax.fori_loop(0, 4, back_att, 0)
    core_copy(6, s.half.at[o], s.ba_all.at[r]).start()
    s.ba_all[r] = s.half[r]
    next_step()
    sent(gathers[7])

    def grad_out(n, carry):
        cols = pl.ds(pl.multiple_of(n * 256, 256), 256)
        grad = dot(s.att_t[...], s.wide[:, cols]).astype(BF)
        s.wout[:, :, :, :, :, cols] = grad.reshape(4, 2, 2, 2, 32, 256)
        return carry

    lax.fori_loop(0, 4, grad_out, 0)
    core_copy(7, s.wout.at[:, :, :, o], s.outx).start()
    core_copy(5, s.n_all.at[r], s.n_all.at[r]).wait_recv()

    def result_tile(i, carry):
        rows = pl.ds(pl.multiple_of(i * 128, 128), 128)
        total = s.middle[rows] + s.out_acc[r, rows] + s.n_all[r, rows].astype(F32) + vec_row(7)
        result_ref[rows] = total.astype(BF)
        return carry

    lax.fori_loop(0, 3, result_tile, 0)
    core_copy(6, s.ba_all.at[o], s.ba_all.at[o]).wait_recv()

    def attend_back(hp, carry):
        k_t = flip(s.qkv[1, hp])
        dims = pl.ds(pl.multiple_of(hp * 128, 128), 128)
        s.dkv[...] = jnp.zeros_like(s.dkv)
        for rb in range(6):
            keys = key_count(rb)
            rows = slice(rb * 128, (rb + 1) * 128)
            both = pair_rows(s.qkv[0, hp, rows])
            at = (rb % 3) * 128
            up = pair_rows(s.ba_all[rb // 3, at : at + 128, dims])
            scores = dot_nt(s.qkv[1, hp, 0:keys], both) * factor + pair_mask(keys, rb)
            probs = jnp.exp2(scores - s.lse[hp, rb, 0:1])
            back_probs = dot_nt(s.qkv[2, hp, 0:keys], up)
            weighted = probs * back_probs
            centre_row = jnp.sum(weighted, axis=0, keepdims=True)
            back_scores = (weighted - probs * centre_row).astype(BF)
            s.dkv[1, 0:keys] += dot(probs.astype(BF), up)
            s.dkv[0, 0:keys] += dot(back_scores, both)
            query = dot(k_t[:, 0:keys], back_scores)
            query = jnp.concatenate([query[0:64, 0:128], query[64:128, 128:256]], axis=0)
            s.ffb[0, rows, dims] = (query.T * HD**-0.5).astype(BF)
        s.ffb[1, :, dims] = (s.dkv[0] * HD**-0.5).astype(BF)
        s.ffb[2, :, dims] = s.dkv[1].astype(BF)
        return carry

    core_copy(7, s.outx, s.outx).wait_recv()

    def add_out(i, carry):
        for yy in range(2):
            for xx in range(2):
                total = s.wout[i, yy, xx, r].astype(F32) + s.outx[i, yy, xx].astype(F32)
                s.wout[i, yy, xx, r] = total.astype(BF)
        return carry

    lax.fori_loop(0, 4, add_out, 0)

    lax.fori_loop(0, 1, attend_back, 0)
    next_step()
    lax.fori_loop(1, 3, attend_back, 0)
    next_step()
    lax.fori_loop(3, 4, attend_back, 0)

    core_copy(5, s.n_all.at[o], s.n_all.at[o]).wait_send()

    def back_in(n, carry):
        cols = pl.ds(pl.multiple_of(n * 256, 256), 256)
        total = dot_nt(s.ffb[0, :, 0:256], s.win[0, n].reshape(256, 256))
        for part in range(1, 6):
            at = (part % 2) * 256
            total = total + dot_nt(s.ffb[part // 2, :, at : at + 256], s.win[part, n].reshape(256, 256))
        s.out_acc[:, :, cols] = total.reshape(2, 384, 256)
        return carry

    lax.fori_loop(0, 4, back_in, 0)
    core_copy(8, s.out_acc.at[o], s.cross).start()
    next_step()
    for part in range(6):
        sent(gathers[1 + part])
        at = (part % 2) * 256
        grad = dot(s.n1t[...], s.ffb[part // 2, :, at : at + 256]).astype(BF)
        s.win[part] = grad.reshape(4, 2, 2, 64, 256)
        if part == 2:
            next_step()
    next_step()
    next_step()

    core_copy(8, s.out_acc.at[o], s.cross).wait_recv()

    def frame_back(i, carry):
        rows = pl.ds(pl.multiple_of(i * 128, 128), 128)
        unit, rate = centre(s.frames_all[r, rows].astype(F32))
        upstream = s.out_acc[r, rows] + s.cross[rows]
        back = s.bn_acc[r, rows] + norm_back(unit, rate, vec_row(0), upstream)
        fgrad_ref[rows] = back.astype(BF)
        gain_t, shift_t = carry
        return (
            gain_t + jnp.sum(upstream * unit, axis=0, keepdims=True),
            shift_t + jnp.sum(upstream, axis=0, keepdims=True),
        )

    gain_t, shift_t = lax.fori_loop(0, 3, frame_back, (zero_row,) * 2)
    s.gvec[0:1] = gain_t
    s.gvec[1:2] = shift_t
    s.gvec[2:4] = jnp.zeros((2, 1024), F32)
    s.gvec[2:3, my_half] = jnp.sum(s.ffb[0].astype(F32), axis=0, keepdims=True)
    s.gvec[3:4, my_half] = jnp.sum(s.ffb[2].astype(F32), axis=0, keepdims=True)
    s.sg[...] = jnp.zeros_like(s.sg)
    for zz in range(4):
        for yy in range(2):
            for xx in range(2):
                at = (zz * 2 + yy) * 128
                s.sg[zz, yy, xx, 0:8] = s.gvec[:, at : at + 128]
                q = 2 * yy + xx
                block = slice(zz * 128, (zz + 1) * 128)
                chunk = [s.gexp[j, 0:1, block] for j in range(4)]
                s.sg[zz, yy, xx, 8:9] = pick([chunk[(q - g) % 4] for g in range(4)], group_1)

    while len(stepped) < len(order) + 6:
        next_step()

    for i, item in enumerate(pre):
        if not 8 <= i < 12:
            item.wait_send()
    sent(gathers[0])
    core_copy(1, s.half_t.at[o], s.half_t.at[o]).wait_send()
    core_copy(4, s.bn_acc.at[o], s.cross).wait_send()
    core_copy(6, s.half.at[o], s.ba_all.at[r]).wait_send()
    core_copy(7, s.wout.at[:, :, :, o], s.outx).wait_send()
    core_copy(8, s.out_acc.at[o], s.cross).wait_send()
    for it in order:
        all_sent(it)


def hand_on(*refs):
    given, tile_ref, taken = refs[0:6], refs[6], refs[7:13]
    vectors, held, sems = refs[13:22], refs[22:28], refs[28]
    inward = [pltpu.make_async_copy(given[i], held[i], sems.at[0, i]) for i in range(6)]
    outward = [pltpu.make_async_copy(held[i], taken[i], sems.at[1, i]) for i in range(6)]
    for item in inward:
        item.start()
    quarter = (lax.axis_index("dp") * 2 + lax.axis_index("role")) % 4
    tile = tile_ref[...]
    turned = pltpu.roll(tile, (4 - quarter) % 4 * 32, 1)
    for row in range(8):
        vectors[row][...] = turned[row, 0:32]
    vectors[8][...] = tile[8]
    for i in range(6):
        inward[i].wait()
        outward[i].start()
    for item in outward:
        item.wait()


def fused_shards(
    frames, frames_cotangent, phoneme_len, prompt_len, target_segment, first_gain, first_shift, inward_weight,
    query_bias, value_bias, outward_weight, outward_bias, second_gain, second_shift, expand_weight, expand_bias,
    reduce_weight, reduce_bias,
):
    number = lax.axis_index("dp") * 2 + lax.axis_index("role")
    quarter = number % 4
    rows = jnp.stack(
        [first_gain, first_shift, query_bias, value_bias, outward_bias, second_gain, second_shift, reduce_bias]
    )
    lane = jnp.arange(128) // 32
    rows = jnp.where(lane[None] == quarter, jnp.tile(rows, (1, 4)), jnp.zeros((), BF))
    small = jnp.concatenate([rows, expand_bias[None], jnp.zeros((7, 128), BF)], axis=0)

    scratch = scratch_list()
    vmem = pl.BlockSpec(memory_space=pltpu.VMEM)
    smem = pl.BlockSpec(memory_space=pltpu.SMEM)
    hbm = pl.BlockSpec(memory_space=pl.ANY)
    outs = pl.pallas_call(
        functools.partial(layer_kernel, tuple(scratch)),
        out_shape=[
            jax.ShapeDtypeStruct((384, 1024), BF),
            jax.ShapeDtypeStruct((384, 1024), BF),
            jax.ShapeDtypeStruct((32, 3072), F32),
            jax.ShapeDtypeStruct((32, 1024), F32),
            jax.ShapeDtypeStruct((32, 4096), F32),
            jax.ShapeDtypeStruct((128, 1024), F32),
            jax.ShapeDtypeStruct((16, 128), F32),
        ],
        in_specs=[smem, smem, vmem, hbm, hbm, vmem, vmem, hbm, vmem, hbm],
        out_specs=[vmem] * 7,
        scratch_shapes=list(scratch.values()),
        compiler_params=pltpu.CompilerParams(
            collective_id=0, has_side_effects=True, vmem_limit_bytes=62 * 1024 * 1024
        ),
    )(
        phoneme_len, prompt_len, target_segment, frames[0], frames_cotangent[0], small, inward_weight,
        outward_weight, expand_weight, reduce_weight,
    )
    *moved, = pl.pallas_call(
        hand_on,
        out_shape=[jax.ShapeDtypeStruct(item.shape, item.dtype) for item in outs[:6]]
        + [jax.ShapeDtypeStruct((32,), F32)] * 8
        + [jax.ShapeDtypeStruct((128,), F32)],
        in_specs=[hbm] * 6 + [vmem],
        out_specs=[hbm] * 6 + [vmem] * 9,
        scratch_shapes=[pltpu.VMEM(item.shape, item.dtype) for item in outs[:6]]
        + [pltpu.SemaphoreType.DMA((2, 6))],
    )(*outs)
    result, frames_gradient, d_in, d_out, d_exp, d_red = moved[:6]
    mine, bias_row = moved[6:14], moved[14]
    return (
        result[None], frames_gradient[None], mine[0], mine[1], d_in, mine[2], mine[3], d_out, mine[4], mine[5],
        mine[6], d_exp, bias_row, d_red, mine[7],
    )


def passed_along(block, axis, distance):
    devices = range(lax.axis_size(axis))
    route = [(i - distance, i) for i in devices if i - distance in devices]
    return lax.ppermute(block, axis, route)


def normalize(values, gain, shift):
    mean_value = jnp.mean(values, axis=-1, keepdims=True)
    centered = values - mean_value
    spread = jnp.mean(centered * centered, axis=-1, keepdims=True)
    return centered * lax.rsqrt(spread + EPS) * gain + shift


def smooth_gate(values):
    return jax.nn.gelu(values, approximate=False)


def inner_rows(left, right):
    return lax.dot_general(
        left, right, (((0,), (0,)), ((), ())), preferred_element_type=jnp.float32
    )


def outer_cols(left, right):
    return lax.dot_general(
        left, right, (((1,), (1,)), ((), ())), preferred_element_type=jnp.float32
    )


def plain_shards(
    frames,
    frames_cotangent,
    phoneme_len,
    prompt_len,
    target_segment,
    first_gain,
    first_shift,
    inward_weight,
    query_bias,
    value_bias,
    outward_weight,
    outward_bias,
    second_gain,
    second_shift,
    expand_weight,
    expand_bias,
    reduce_weight,
    reduce_bias,
):
    attention_part = (
        lax.all_gather(first_gain, ("dp", "role"), axis=0, tiled=True),
        lax.all_gather(first_shift, ("dp", "role"), axis=0, tiled=True),
        lax.all_gather(inward_weight, ("dp", "role"), axis=0, tiled=True),
        lax.all_gather(query_bias, ("dp", "role"), axis=0, tiled=True),
        lax.all_gather(value_bias, ("dp", "role"), axis=0, tiled=True),
        lax.all_gather(outward_weight, ("dp", "role"), axis=0, tiled=True),
        lax.all_gather(outward_bias, ("dp", "role"), axis=0, tiled=True),
    )
    (
        full_gain,
        full_shift,
        full_inward,
        full_query_bias,
        full_value_bias,
        full_outward,
        full_outward_bias,
    ) = attention_part
    side = lax.axis_index("role")
    local_rows = frames.shape[1]
    scale = HD ** (-0.5)
    current = frames[0].astype(jnp.float32)
    normed = normalize(
        current, full_gain.astype(jnp.float32), full_shift.astype(jnp.float32)
    ).astype(jnp.bfloat16)
    mixed = jnp.dot(normed, full_inward, preferred_element_type=jnp.float32)
    queries = (mixed[:, :D] + full_query_bias.astype(jnp.float32)).astype(jnp.bfloat16)
    keys_own = mixed[:, D : 2 * D].astype(jnp.bfloat16)
    values_own = (mixed[:, 2 * D :] + full_value_bias.astype(jnp.float32)).astype(jnp.bfloat16)
    remote_keys, remote_values = passed_along((keys_own, values_own), "role", 1)
    keys_all = jnp.concatenate([remote_keys, keys_own], axis=0)
    values_all = jnp.concatenate([remote_values, values_own], axis=0)
    row_index = jnp.arange(local_rows)[:, None]
    col_index = jnp.arange(2 * local_rows)[None, :]
    own_col = col_index - local_rows
    prefix_length = phoneme_len[0] + prompt_len[0]
    segment = target_segment[0]
    key_segment = jnp.concatenate([jnp.full((local_rows,), -1, jnp.int32), segment])
    prompt_rows = (own_col >= 0) & (own_col <= row_index) & (own_col < prefix_length)
    target_rows = (col_index < prefix_length) | (own_col >= 0) & (own_col <= row_index) & (
        key_segment[None, :] == segment[:, None]
    )
    allowed = jnp.where(side == 0, prompt_rows, target_rows)

    def attend(index):
        start = index * HD
        head_query = lax.dynamic_slice_in_dim(queries, start, HD, 1)
        head_key = lax.dynamic_slice_in_dim(keys_all, start, HD, 1)
        head_value = lax.dynamic_slice_in_dim(values_all, start, HD, 1)
        scores = outer_cols(head_query, head_key) * scale
        masked = jnp.where(allowed, scores, MASKED)
        peak = jnp.max(masked, axis=1, keepdims=True)
        expo = jnp.exp(masked - peak)
        total = jnp.sum(expo, axis=1, keepdims=True)
        probs = (expo / total).astype(jnp.bfloat16)
        return (
            jnp.dot(probs, head_value, preferred_element_type=jnp.float32),
            (peak + jnp.log(total))[:, 0],
        )

    head_outs, log_totals = lax.map(attend, jnp.arange(H))
    attended = head_outs.transpose(1, 0, 2).reshape(local_rows, D).astype(jnp.bfloat16)
    middle = (
        current
        + jnp.dot(attended, full_outward, preferred_element_type=jnp.float32)
        + full_outward_bias.astype(jnp.float32)
    )
    feed_part = (
        lax.all_gather(second_gain, ("dp", "role"), axis=0, tiled=True),
        lax.all_gather(second_shift, ("dp", "role"), axis=0, tiled=True),
        lax.all_gather(expand_weight, ("dp", "role"), axis=0, tiled=True),
        lax.all_gather(expand_bias, ("dp", "role"), axis=0, tiled=True),
        lax.all_gather(reduce_weight, ("dp", "role"), axis=0, tiled=True),
        lax.all_gather(reduce_bias, ("dp", "role"), axis=0, tiled=True),
    )
    full_gain_two, full_shift_two, full_expand, full_expand_bias, full_reduce, full_reduce_bias = (
        feed_part
    )
    gain_two = full_gain_two.astype(jnp.float32)
    shift_two = full_shift_two.astype(jnp.float32)
    normed_two = normalize(middle, gain_two, shift_two).astype(jnp.bfloat16)
    inner = jnp.dot(
        normed_two, full_expand, preferred_element_type=jnp.float32
    ) + full_expand_bias.astype(jnp.float32)
    active = smooth_gate(inner).astype(jnp.bfloat16)
    output = (
        middle
        + jnp.dot(active, full_reduce, preferred_element_type=jnp.float32)
        + full_reduce_bias.astype(jnp.float32)
    )
    result = output.astype(jnp.bfloat16)[None]
    again_expand = feed_part[2]
    again_reduce = feed_part[4]
    again_gain = attention_part[0].astype(jnp.float32)
    again_shift = attention_part[1].astype(jnp.float32)
    again_inward = attention_part[2]
    again_outward = attention_part[5]
    upstream = frames_cotangent[0]
    upstream_float = upstream.astype(jnp.float32)
    reduce_bias_term = jnp.sum(upstream_float, axis=0)
    reduce_weight_term = inner_rows(active, upstream)
    back_active = outer_cols(upstream, again_reduce)
    gate_pull = jax.vjp(smooth_gate, inner)[1]
    back_inner = gate_pull(back_active)[0].astype(jnp.bfloat16)
    expand_bias_term = jnp.sum(back_inner.astype(jnp.float32), axis=0)
    expand_weight_term = inner_rows(normed_two, back_inner)
    back_normed_two = outer_cols(back_inner, again_expand)
    second_pull = jax.vjp(normalize, middle, gain_two, shift_two)[1]
    middle_part, second_gain_term, second_shift_term = second_pull(back_normed_two)
    back_middle = upstream_float + middle_part
    back_branch = back_middle.astype(jnp.bfloat16)
    outward_bias_term = jnp.sum(back_branch.astype(jnp.float32), axis=0)
    outward_weight_term = inner_rows(attended, back_branch)
    back_attended = outer_cols(back_branch, again_outward).astype(jnp.bfloat16)

    def attend_back(inputs):
        index, log_total = inputs
        start = index * HD
        head_query = lax.dynamic_slice_in_dim(queries, start, HD, 1)
        head_key = lax.dynamic_slice_in_dim(keys_all, start, HD, 1)
        head_value = lax.dynamic_slice_in_dim(values_all, start, HD, 1)
        head_upstream = lax.dynamic_slice_in_dim(back_attended, start, HD, 1)
        scores = outer_cols(head_query, head_key) * scale
        probs = jnp.where(allowed, jnp.exp(scores - log_total[:, None]), 0.0)
        back_probs = outer_cols(head_upstream, head_value)
        centre = jnp.sum(probs * back_probs, axis=1, keepdims=True)
        back_scores = (probs * (back_probs - centre)).astype(jnp.bfloat16)
        back_query = jnp.dot(back_scores, head_key, preferred_element_type=jnp.float32) * scale
        back_key = inner_rows(back_scores, head_query) * scale
        back_value = inner_rows(probs.astype(jnp.bfloat16), head_upstream)
        return (back_query, back_key, back_value)

    head_query_grads, head_key_grads, head_value_grads = lax.map(
        attend_back, (jnp.arange(H), log_totals)
    )
    back_queries = head_query_grads.transpose(1, 0, 2).reshape(local_rows, D)
    back_keys_all = head_key_grads.transpose(1, 0, 2).reshape(2 * local_rows, D)
    back_values_all = head_value_grads.transpose(1, 0, 2).reshape(2 * local_rows, D)
    returned_keys, returned_values = (
        passed_along(back_keys_all[:local_rows].astype(jnp.bfloat16), "role", -1).astype(
            jnp.float32
        ),
        passed_along(back_values_all[:local_rows].astype(jnp.bfloat16), "role", -1).astype(
            jnp.float32
        ),
    )
    query_low = back_queries.astype(jnp.bfloat16)
    key_low = (back_keys_all[local_rows:] + returned_keys).astype(jnp.bfloat16)
    value_low = (back_values_all[local_rows:] + returned_values).astype(jnp.bfloat16)
    back_mixed = jnp.concatenate([query_low, key_low, value_low], axis=1)
    query_bias_term = jnp.sum(query_low.astype(jnp.float32), axis=0)
    value_bias_term = jnp.sum(value_low.astype(jnp.float32), axis=0)
    inward_weight_term = inner_rows(normed, back_mixed)
    back_normed = outer_cols(back_mixed, again_inward)
    first_pull = jax.vjp(normalize, current, again_gain, again_shift)[1]
    frame_part, first_gain_term, first_shift_term = first_pull(back_normed)
    frames_gradient = (back_middle + frame_part).astype(jnp.bfloat16)[None]
    totals = (
        lax.psum_scatter(first_gain_term, ("dp", "role"), scatter_dimension=0, tiled=True),
        lax.psum_scatter(first_shift_term, ("dp", "role"), scatter_dimension=0, tiled=True),
        lax.psum_scatter(inward_weight_term, ("dp", "role"), scatter_dimension=0, tiled=True),
        lax.psum_scatter(query_bias_term, ("dp", "role"), scatter_dimension=0, tiled=True),
        lax.psum_scatter(value_bias_term, ("dp", "role"), scatter_dimension=0, tiled=True),
        lax.psum_scatter(outward_weight_term, ("dp", "role"), scatter_dimension=0, tiled=True),
        lax.psum_scatter(outward_bias_term, ("dp", "role"), scatter_dimension=0, tiled=True),
        lax.psum_scatter(second_gain_term, ("dp", "role"), scatter_dimension=0, tiled=True),
        lax.psum_scatter(second_shift_term, ("dp", "role"), scatter_dimension=0, tiled=True),
        lax.psum_scatter(expand_weight_term, ("dp", "role"), scatter_dimension=0, tiled=True),
        lax.psum_scatter(expand_bias_term, ("dp", "role"), scatter_dimension=0, tiled=True),
        lax.psum_scatter(reduce_weight_term, ("dp", "role"), scatter_dimension=0, tiled=True),
        lax.psum_scatter(reduce_bias_term, ("dp", "role"), scatter_dimension=0, tiled=True),
    )
    return (
        result,
        frames_gradient,
        totals[0],
        totals[1],
        totals[2],
        totals[3],
        totals[4],
        totals[5],
        totals[6],
        totals[7],
        totals[8],
        totals[9],
        totals[10],
        totals[11],
        totals[12],
    )


def solution(mesh):
    placed = (
        P("dp", "role", None),
        P("dp", "role", None),
        P("dp"),
        P("dp"),
        P("dp", None),
        P(("dp", "role")),
        P(("dp", "role")),
        P(("dp", "role"), None),
        P(("dp", "role")),
        P(("dp", "role")),
        P(("dp", "role"), None),
        P(("dp", "role")),
        P(("dp", "role")),
        P(("dp", "role")),
        P(("dp", "role"), None),
        P(("dp", "role")),
        P(("dp", "role"), None),
        P(("dp", "role")),
    )
    fused = mesh.shape["dp"] == 16 and mesh.shape["role"] == 2
    return jax.shard_map(
        fused_shards if fused else plain_shards,
        mesh=mesh,
        in_specs=placed,
        out_specs=(
            P("dp", "role", None),
            P("dp", "role", None),
            P(("dp", "role")),
            P(("dp", "role")),
            P(("dp", "role"), None),
            P(("dp", "role")),
            P(("dp", "role")),
            P(("dp", "role"), None),
            P(("dp", "role")),
            P(("dp", "role")),
            P(("dp", "role")),
            P(("dp", "role"), None),
            P(("dp", "role")),
            P(("dp", "role"), None),
            P(("dp", "role")),
        ),
        check_vma=False,
    )
```
